256 devices in a mesh: member: 2 (over core), tile: 128 (over x, z, y).
Axes of the slice: x: 4, y: 4, z: 8, core: 2. Of those that a mesh axis runs over, the one named last changes fastest.
Arguments:
- parent_state: float32 [4, 81, 1024, 128], P('member', None, 'tile'), may hold values from -6 to 6
- nest_state: float32 [4, 81, 32768], P('member', None, 'tile'), may hold values from -6 to 6
- terrain: int32 [1024, 128], P('tile'), may hold values from 0 to 3000
- shift_x: int32 [4], replicated, may hold values from -16 to 16
- boundary_index: int32 [4, 16384], P(None, 'tile'), may hold values from 0 to 131071, as said below
- reloc_dest: int32 [4, 32768], P(None, 'tile'), may hold values from 0 to 32767, as said below
Outputs:
- parent_out: float32 [4, 81, 1024, 128], P('member', None, 'tile')
- nest_out: float32 [4, 81, 32768], P('member', None, 'tile')
- nest_mean: float32 [81, 32768], P(None, 'tile')
- nest_variance: float32 [81, 32768], P(None, 'tile')
The draws below stay inside these ranges and needn't reach their ends.
Inputs may be any that keep to these rules, and one draw needn't show every extreme that they name: `boundary_index`: for each step and nest tile t, entries t * 128 to t * 128 + 127 come in 64 runs of 2; each run lies on one parent tile (rows of 8), different runs of one tile on different parent tiles, and the cells within one run differ. `reloc_dest`: for each step a permutation of the 32768 nest columns. The columns of one tile go in runs of 4 (slots g * 4 to g * 4 + 3) each wholly to one tile, into that tile's run g; the runs of one tile go to 64 different tiles, so exactly 4 or no columns pass from one tile to another.
All inputs are finite; a program needn't handle non-finite values.
Results may differ from the reference program's by a relative error of at most 0.00047.
Values may be sent and summed in bfloat16 or wider, within the bound.
No kernel may reach another device: no remote copies, remote signals or barrier semaphores. Data moves between devices by JAX's collectives and lax.ppermute only.
A program may use at most 64 MiB of HBM per device.

```python
import jax
import jax.numpy as jnp

LEV = 81
PY_DEV = 8
PXW = 128
NC_DEV = 256
CAPB = 2
STEPS = 4
MEMBERS = 4
NPY = 1024
CELLS = 1024
NCOLS = 32768
GROUPS = 64
CAP = 4
OWNERS = 64
NB_DEV = 128
N_TILE = 128


def draw_boundary_index(key, part):
    tile_count = NPY // PY_DEV
    pieces = []
    for step_no in range(STEPS):
        step_key = jax.random.fold_in(jax.random.fold_in(key, 11), step_no)
        key_start, key_jitter = jax.random.split(step_key, 2)
        starts = jax.random.randint(key_start, (tile_count, 1, 1), 0, max(tile_count // 4, 1))
        starts = starts.at[0, 0, 0].set(tile_count - OWNERS)
        starts = starts.at[1, 0, 0].set(0)
        run_index = jnp.arange(OWNERS, dtype=jnp.int32).reshape(1, OWNERS, 1)
        owner_tile = (starts + run_index) % tile_count
        stride = CELLS // CAPB
        jitter = jax.random.randint(key_jitter, (tile_count, OWNERS, CAPB), 0, stride)
        jitter = jitter.at[0, OWNERS - 1, CAPB - 1].set(stride - 1)
        jitter = jitter.at[1, 0, 0].set(0)
        within = jnp.arange(CAPB, dtype=jnp.int32).reshape(1, 1, CAPB) * stride + jitter
        pieces.append((owner_tile * CELLS + within).reshape(-1))
    return jnp.stack(pieces, axis=0).astype(jnp.int32)


def draw_reloc_dest(key, part):
    tile_count = NPY // PY_DEV
    pieces = []
    for step_no in range(STEPS):
        step_key = jax.random.fold_in(jax.random.fold_in(key, 23), step_no)
        key_order, key_offset, key_slots = jax.random.split(step_key, 3)
        order = jax.random.permutation(key_order, tile_count).astype(jnp.int32)
        inverse = jnp.argsort(order).astype(jnp.int32)
        offsets = jax.random.permutation(key_offset, tile_count)[:GROUPS].astype(jnp.int32)
        sources = jnp.arange(tile_count, dtype=jnp.int32)
        target_tile = order[(inverse[sources][:, None] + offsets[None, :]) % tile_count]
        scores = jax.random.randint(key_slots, (tile_count, GROUPS, CAP), 0, 1 << 20) * CAP
        scores = scores + jnp.arange(CAP, dtype=jnp.int32).reshape(1, 1, CAP)
        within = jnp.argsort(scores, axis=-1, stable=True).astype(jnp.int32)
        group_base = jnp.arange(GROUPS, dtype=jnp.int32).reshape(1, GROUPS, 1) * CAP
        targets = target_tile[:, :, None] * NC_DEV + group_base + within
        pieces.append(targets.reshape(-1))
    return jnp.stack(pieces, axis=0).astype(jnp.int32)


def plant(values, key, smallest, top_value):
    place = [jax.random.randint(jax.random.fold_in(key, axis), (), 0, length) for axis, length in enumerate(values.shape)]
    main_axis = values.shape.index(max(values.shape))
    beside = place[:main_axis] + [(place[main_axis] + 1) % values.shape[main_axis]] + place[main_axis + 1:]
    return values.at[tuple(place)].set(smallest).at[tuple(beside)].set(top_value)


def block_levels(own_key, extent, cuts, smallest, high):
    level, own = 1.0, jax.random.fold_in(own_key, 6)
    for dim, shards_of in cuts:
        draws = jnp.exp(jax.random.uniform(jax.random.fold_in(own, dim), (shards_of,), jnp.float32, smallest / len(cuts), high / len(cuts)))
        level = level * jnp.repeat(draws, extent[dim] // shards_of).reshape([-1 if axis == dim else 1 for axis in range(len(extent))])
    return level


def bell_draw(own_key, extent, scale, bound, shards=(), kind=jnp.bfloat16):
    values = scale * jax.random.normal(own_key, extent, jnp.float32)
    if shards:
        values = values * block_levels(own_key, extent, shards, -0.22, 0.18)
    return jnp.clip(values, -bound, bound).astype(kind)


def setup_inputs(seed: int = 0) -> dict:
    splits = jax.random.split(jax.random.key(seed), 7)
    return {
        "parent_state": bell_draw(splits[0], (MEMBERS, LEV, NPY, PXW), 1.0, 6.0, ((0, 2), (2, 128)), jnp.float32),
        "nest_state": bell_draw(splits[1], (MEMBERS, LEV, NCOLS), 1.0, 6.0, ((0, 2), (2, 128)), jnp.float32),
        "terrain": plant(jax.random.randint(splits[2], (NPY, PXW), 0, 3001), jax.random.fold_in(splits[2], 1), 0, 3000).astype(jnp.int32),
        "shift_x": plant(jax.random.randint(splits[3], (STEPS,), -16, 17), jax.random.fold_in(splits[3], 1), -16, 16).astype(jnp.int32),
        "boundary_index": draw_boundary_index(jax.random.fold_in(splits[6], 71), 0),
        "reloc_dest": draw_reloc_dest(jax.random.fold_in(splits[6], 71), 0),
    }


HORIZ_MIX = 0.15
VERT_MIX = 0.1
DRAG_RATE = 0.1
RELAX_RATE = 0.5
IMPLICIT_MIX = 0.8


def parent_update(parent, damping):
    padded = jnp.pad(parent, ((0, 0), (0, 0), (1, 1), (0, 0)))
    north_row = padded[:, :, 2:, :]
    south_row = padded[:, :, :-2, :]
    east_cell = jnp.roll(parent, -1, axis=3)
    west_cell = jnp.roll(parent, 1, axis=3)
    upper_level = jnp.concatenate([parent[:, 1:], parent[:, -1:]], axis=1)
    lower_level = jnp.concatenate([parent[:, :1], parent[:, :-1]], axis=1)
    return (parent + HORIZ_MIX * (north_row + south_row + east_cell + west_cell - 4.0 * parent)
            + VERT_MIX * (upper_level + lower_level - 2.0 * parent) - damping * parent)


def implicit_column(column_field):
    levels = column_field.shape[1]
    pivots = []
    cprime = []
    previous = 0.0
    for level in range(levels):
        neighbours = (1 if level > 0 else 0) + (1 if level < levels - 1 else 0)
        diagonal = 1.0 + IMPLICIT_MIX * neighbours
        pivot = diagonal - IMPLICIT_MIX * previous if level > 0 else diagonal
        previous = IMPLICIT_MIX / pivot
        pivots.append(pivot)
        cprime.append(previous)
    sweep = []
    forward = None
    for level in range(levels):
        source = column_field[:, level]
        if level > 0:
            source = source + IMPLICIT_MIX * forward
        forward = source / pivots[level]
        sweep.append(forward)
    result = [None] * levels
    result[levels - 1] = sweep[levels - 1]
    for level in range(levels - 2, -1, -1):
        result[level] = sweep[level] + cprime[level] * result[level + 1]
    return jnp.stack(result, axis=1)


def reference(parent_state, nest_state, terrain, shift_x, boundary_index, reloc_dest):
    damping = DRAG_RATE * terrain.astype(jnp.float32) / 3000.0
    parent = parent_state
    nest_field = nest_state
    members, levels, ncols = nest_field.shape
    for step_no in range(STEPS):
        flat_parent = parent.astype(jnp.bfloat16).reshape(members, levels, -1)
        indices = boundary_index[step_no]
        rows_at = indices // PXW
        cols_at = jnp.mod(indices % PXW + shift_x[step_no], PXW)
        picked = jnp.take(flat_parent, rows_at * PXW + cols_at, axis=2).astype(jnp.float32)
        picked = picked.reshape(members, levels, N_TILE, NB_DEV)
        blocks = nest_field.reshape(members, levels, N_TILE, NC_DEV)
        edge_cols = blocks[..., :NB_DEV]
        edge_cols = edge_cols + RELAX_RATE * (picked - edge_cols)
        blocks = jnp.concatenate([edge_cols, blocks[..., NB_DEV:]], axis=3)
        nest_field = implicit_column(blocks.reshape(members, levels, ncols))
        nest_field = jnp.zeros_like(nest_field).at[:, :, reloc_dest[step_no]].set(nest_field)
        parent = parent_update(parent, damping)
    mean_field = jnp.sum(nest_field, axis=0) / MEMBERS
    variance = jnp.sum((nest_field - mean_field) ** 2, axis=0) / MEMBERS
    return parent, nest_field, mean_field, variance
```

```python
import functools

import jax
import jax.numpy as jnp
import numpy as np
from jax import lax
from jax.experimental import pallas as pl
from jax.experimental.pallas import tpu as pltpu
from jax.sharding import PartitionSpec as P

F32 = jnp.float32
BF16 = jnp.bfloat16
LEV = 81
STEPS = 4
NT = 128
ROWS = 8
W = 128
LPAD = 96
RING = 16
BSTR = LPAD * RING
L_DEST = 81
L_REQ = 88
HORIZ = 0.15
VERT = 0.1
DRAG = 0.1
RELAX = 0.5
IMPL = 0.8
VMEM_LIMIT = 48 * 1024 * 1024


def solve_matrix():
    n = np.full(LEV, 2.0)
    n[0] = n[-1] = 1.0
    a = np.diag(1.0 + IMPL * n)
    a -= IMPL * (np.eye(LEV, k=1) + np.eye(LEV, k=-1))
    return np.linalg.inv(a)


def padded_transpose(m):
    out = np.zeros((W, W))
    out[:LEV, :LEV] = m.T
    return out


def split3(m):
    m = np.asarray(m, np.float64)
    parts = []
    for _ in range(3):
        part = m.astype(jnp.bfloat16)
        parts.append(part)
        m = m - part.astype(np.float64)
    return parts


def constants():
    s = solve_matrix()
    power = [np.linalg.matrix_power(s, k) for k in range(STEPS + 1)]
    keep = 1.0 - RELAX
    interior = padded_transpose(power[STEPS])
    bound = padded_transpose(power[STEPS] * keep**STEPS)
    q_mix = np.stack([bound, interior]).astype(np.float32)
    stack = np.concatenate(
        [
            padded_transpose(power[STEPS - k] * RELAX * keep ** (STEPS - 1 - k))
            for k in range(STEPS)
        ]
    )
    e_mix = np.concatenate(split3(stack), axis=1)
    return q_mix, e_mix


def call(body, out_shape, in_specs=None, scratch=(), name=None, flops=0, nbytes=0):
    kwargs = {} if in_specs is None else {"in_specs": in_specs}
    return pl.pallas_call(
        body,
        out_shape=out_shape,
        scratch_shapes=list(scratch),
        compiler_params=pltpu.CompilerParams(vmem_limit_bytes=VMEM_LIMIT),
        cost_estimate=pl.CostEstimate(
            flops=flops, bytes_accessed=nbytes, transcendentals=0
        ),
        name=name,
        **kwargs,
    )


VM = pl.BlockSpec(memory_space=pltpu.VMEM)
SM = pl.BlockSpec(memory_space=pltpu.SMEM)


def send_kernel(shift_ref, nest_ref, bidx_ref, dest_ref, msg_ref, pad_ref):
    zeros = jnp.zeros((W - LEV + 1, 2 * W), F32)
    for b in range(2):
        pad_ref[b, LEV - 1 :, :] = zeros
        pad_ref[b, :LEV, :] = nest_ref[b]
        pad_ref[b, L_DEST : L_DEST + STEPS, :] = dest_ref[...].astype(F32)
        for half in range(2):
            block = pad_ref[b, :, half * W : (half + 1) * W]
            start = b * 2 * W + half * W
            msg_ref[start : start + W, :] = block.T
    lane = lax.broadcasted_iota(jnp.int32, (NT, W), 1)
    tile = lax.broadcasted_iota(jnp.int32, (NT, W), 0)
    for s in range(STEPS):
        idx = bidx_ref[s : s + 1, :]
        owner = jnp.right_shift(idx, 10)
        row = jnp.bitwise_and(jnp.right_shift(idx, 7), ROWS - 1)
        col = jnp.bitwise_and(jnp.bitwise_and(idx, W - 1) + shift_ref[s], W - 1)
        cell = (row * W + col + 1).astype(F32)
        mine = tile == owner
        picked = jnp.where(mine, jnp.broadcast_to(cell, (NT, W)), 0.0)
        even = jnp.bitwise_and(lane, 1) == 0
        first = jnp.sum(jnp.where(even, picked, 0.0), axis=1, keepdims=True) - 1.0
        second = jnp.sum(jnp.where(even, 0.0, picked), axis=1, keepdims=True) - 1.0
        rows = msg_ref[pl.ds(s, NT, stride=4), :]
        rows = jnp.where(lane == L_REQ, first, rows)
        rows = jnp.where(lane == L_REQ + 1, second, rows)
        msg_ref[pl.ds(s, NT, stride=4), :] = rows


def halo_kernel(parent_ref, terrain_ref, down_ref, up_ref):
    damping = DRAG * terrain_ref[...].astype(F32) / 3000.0
    down_ref[: 2 * LEV, :, :] = parent_ref[:, 4:, :]
    up_ref[: 2 * LEV, :, :] = parent_ref[:, :4, :]
    down_ref[2 * LEV, :, :] = damping[4:, :]
    up_ref[2 * LEV, :, :] = damping[:4, :]


def ring_step(read, write, level_stride, coef, own_only=False):
    row = lax.broadcasted_iota(jnp.int32, (ROWS, W), 0)
    last = row == ROWS - 1
    head = row == 0
    c0, c1, h1, v1 = coef
    chunk = 9

    def body(step, carry):
        for member in range(2):
            for k in range(chunk):
                level = step * chunk + k
                base = member * level_stride
                below = base + jnp.maximum(level - 1, 0)
                above = base + jnp.minimum(level + 1, LEV - 1)
                x0, x1 = read(base + level)
                d0, d1 = read(below)
                u0, u1 = read(above)
                f0 = pltpu.roll(x0, ROWS - 1, 0)
                f1 = pltpu.roll(x1, ROWS - 1, 0)
                g0 = pltpu.roll(x0, 1, 0)
                g1 = pltpu.roll(x1, 1, 0)
                near0 = jnp.where(last, f1, f0) + jnp.where(head, g1, g0)
                near0 = near0 + (pltpu.roll(x0, 1, 1) + pltpu.roll(x0, W - 1, 1))
                y0 = c0 * x0 + HORIZ * near0 + VERT * (d0 + u0)
                if own_only:
                    write(member, level, y0, None)
                    continue
                near1 = jnp.where(last, f0, f1) + jnp.where(head, g0, g1)
                near1 = near1 + (pltpu.roll(x1, 1, 1) + pltpu.roll(x1, W - 1, 1))
                y1 = c1 * x1 + h1 * near1 + v1 * (d1 + u1)
                write(member, level, y0, y1)
        return carry

    lax.fori_loop(0, LEV // chunk, body, 0)


def parent_kernel(
    tile_ref, parent_ref, next_ref, prev_ref, terrain_ref, cells_ref, ring_ref, a_ref, b_ref
):
    tile = tile_ref[0]
    damping = DRAG * terrain_ref[...].astype(F32) / 3000.0
    pads = jnp.zeros(((LPAD - LEV) * RING, W), F32)
    for ref in (a_ref, b_ref):
        for member in range(2):
            top = member * BSTR + LEV * RING
            ref[top : top + (LPAD - LEV) * RING, :] = pads
    for s in range(STEPS):
        for member in range(2):
            cells_ref[s, member * W + LPAD : (member + 1) * W, :] = jnp.zeros(
                (W - LPAD, ROWS * W), BF16
            )

    def fill(level, carry):
        for member in range(2):
            src = member * LEV + level
            base = pl.multiple_of(member * BSTR + level * RING, RING)
            a_ref[pl.ds(base, ROWS), :] = parent_ref[src]
            a_ref[pl.ds(base + 8, 4), :] = next_ref[src]
            a_ref[pl.ds(base + 12, 4), :] = prev_ref[src]
        return carry

    lax.fori_loop(0, LEV, fill, 0)
    b_ref[0:4, :] = next_ref[2 * LEV]
    b_ref[4:8, :] = prev_ref[2 * LEV]
    row = lax.broadcasted_iota(jnp.int32, (ROWS, W), 0)
    south = jnp.where(tile < NT - 1, 1.0, 0.0).astype(F32)
    north = jnp.where(tile > 0, 1.0, 0.0).astype(F32)
    valid = jnp.where(row < 4, south, north)
    stay = 1.0 - 4.0 * HORIZ - 2.0 * VERT
    coef = (stay - damping, (stay - b_ref[0:8, :]) * valid, HORIZ * valid, VERT * valid)

    def emit(s, ref):
        for member in range(2):
            for y in range(ROWS):
                rows = ref[pl.ds(member * BSTR + y, LPAD, stride=RING), :]
                cells_ref[s, member * W : member * W + LPAD, y * W : (y + 1) * W] = (
                    rows.astype(BF16)
                )

    emit(0, a_ref)
    src, dst = a_ref, b_ref
    for s in range(1, STEPS):

        def read(index, src=src):
            base = pl.multiple_of(index * RING, RING)
            return src[pl.ds(base, ROWS), :], src[pl.ds(base + ROWS, ROWS), :]

        def write(member, level, y0, y1, dst=dst):
            base = pl.multiple_of((member * LPAD + level) * RING, RING)
            dst[pl.ds(base, ROWS), :] = y0
            dst[pl.ds(base + ROWS, ROWS), :] = y1

        ring_step(read, write, LPAD, coef)
        emit(s, dst)
        src, dst = dst, src

    def drain(level, carry):
        for member in range(2):
            base = pl.multiple_of((member * LPAD + level) * RING, RING)
            ring_ref[member * LEV + level] = src[pl.ds(base, RING), :]
        return carry

    lax.fori_loop(0, LEV, drain, 0)


def last_parent_kernel(ring_ref, terrain_ref, out_ref):
    damping = DRAG * terrain_ref[...].astype(F32) / 3000.0
    stay = 1.0 - 4.0 * HORIZ - 2.0 * VERT

    def read(index):
        return ring_ref[index, 0:ROWS, :], ring_ref[index, ROWS:RING, :]

    def write(member, level, y0, y1):
        out_ref[member * LEV + level] = y0

    ring_step(read, write, LEV, (stay - damping, None, None, None), own_only=True)


def gather_kernel(got_ref, cells_ref, out_ref, scr_ref):
    lane = lax.broadcasted_iota(jnp.int32, (NT, ROWS * W), 1).astype(F32)
    for s in range(STEPS):
        rows = got_ref[pl.ds(s, NT, stride=4), :]
        hot = [
            jnp.where(lane == rows[:, L_REQ + c : L_REQ + c + 1], 1.0, 0.0).astype(BF16)
            for c in range(2)
        ]
        hot = jnp.concatenate(hot, axis=0)
        res = lax.dot_general(
            hot, cells_ref[s], (((1,), (1,)), ((), ())), preferred_element_type=F32
        )
        for b in range(2):
            for c in range(2):
                scr_ref[pl.ds(b * 8 + s * 2 + c, NT, stride=16), :] = res[
                    c * W : (c + 1) * W, b * W : (b + 1) * W
                ]
    out_ref[...] = scr_ref[...].astype(BF16)


def regroup_kernel(bperm_ref, got_ref, out_ref, scr_ref, scr2_ref):
    scr_ref[...] = got_ref[...].astype(F32)
    sub = lax.broadcasted_iota(jnp.int32, (2 * NT, W), 0)
    lane = lax.broadcasted_iota(jnp.int32, (2 * NT, W), 1)
    parity = jnp.bitwise_and(jnp.right_shift(lane, 5), 1)
    target = sub - parity * NT
    for s in range(STEPS):
        owner = jnp.right_shift(bperm_ref[s : s + 1, :], 10)
        hot = jnp.where(target == owner, 1.0, 0.0).astype(BF16)
        values = jnp.concatenate(
            [
                jnp.concatenate(
                    [
                        scr_ref[pl.ds(b * 8 + s * 2 + c, NT, stride=16), :]
                        for b in range(2)
                    ],
                    axis=1,
                )
                for c in range(2)
            ],
            axis=0,
        ).astype(BF16)
        res = lax.dot_general(
            hot, values, (((0,), (0,)), ((), ())), preferred_element_type=F32
        )
        for b in range(2):
            for j in range(4):
                scr2_ref[pl.ds(b * 512 + s * 4 + j, 32, stride=16), :] = res[
                    j * 32 : (j + 1) * 32, b * W : (b + 1) * W
                ]
    for b in range(2):
        out_ref[b * 1024 : b * 1024 + 512, :] = scr2_ref[b * 512 : (b + 1) * 512, :].astype(
            BF16
        )
        out_ref[b * 1024 + 512 : (b + 1) * 1024, :] = jnp.zeros((512, W), BF16)


def plan_kernel(tile_ref, got_ref, mix_ref, hot_ref, base_ref):
    interior = jnp.where(jnp.bitwise_and(tile_ref[0], 63) < 32, 0, 1)
    n = 4 * NT
    turned = [got_ref[pl.ds(j, NT, stride=4), :].T for j in range(4)]
    sub = lax.broadcasted_iota(jnp.int32, (n, n), 0)

    def dest(s):
        row = jnp.concatenate(
            [t[L_DEST + s : L_DEST + s + 1, :] for t in turned], axis=1
        ).astype(jnp.int32)
        return jnp.right_shift(row, 8), jnp.bitwise_and(row, 3)

    tile_to, slot_to = dest(STEPS - 1)
    for s in range(STEPS - 1, -1, -1):
        if s < STEPS - 1:
            mid_tile, mid_slot = dest(s)
            move = jnp.where(sub == mid_slot * NT + mid_tile, 1.0, 0.0).astype(BF16)
            later = jnp.concatenate(
                [
                    jnp.broadcast_to(tile_to, (8, n)),
                    jnp.broadcast_to(slot_to, (8, n)),
                ],
                axis=0,
            )
            both = jnp.dot(
                later.astype(F32).astype(BF16), move, preferred_element_type=F32
            )
            tile_to = both[0:1, :].astype(jnp.int32)
            slot_to = both[8:9, :].astype(jnp.int32)
        hot_ref[s] = jnp.where(sub == tile_to * 4 + slot_to, 1.0, 0.0).astype(BF16)
    columns = jnp.concatenate(
        [got_ref[pl.ds(j, NT, stride=4), :] for j in range(4)], axis=0
    )
    mixed = lax.dot_general(
        columns,
        mix_ref[interior],
        (((1,), (0,)), ((), ())),
        precision=lax.Precision.HIGHEST,
        preferred_element_type=F32,
    )
    parts = []
    for _ in range(3):
        part = mixed.astype(BF16)
        parts.append(part)
        mixed = mixed - part.astype(F32)
    moved = jnp.dot(
        hot_ref[0], jnp.concatenate(parts, axis=1), preferred_element_type=F32
    )
    base_ref[...] = moved[:, :W] + (moved[:, W : 2 * W] + moved[:, 2 * W :])


def owner_kernel(tile_ref, got_ref, hot_ref, base_ref, mix_ref, out_ref, scr_ref):
    bound = jnp.bitwise_and(tile_ref[0], 63) < 32

    @pl.when(bound)
    def _():
        scr_ref[...] = got_ref[...].astype(F32)
        moved = []
        for s in range(STEPS):
            edge = jnp.concatenate(
                [scr_ref[pl.ds(s * 4 + j, NT, stride=16), :] for j in range(4)], axis=0
            ).astype(BF16)
            moved.append(
                jnp.dot(hot_ref[s], edge, preferred_element_type=F32).astype(BF16)
            )
        total = jnp.dot(
            jnp.concatenate(moved, axis=1), mix_ref[...], preferred_element_type=F32
        )
        out_ref[...] = base_ref[...] + (
            total[:, :W] + (total[:, W : 2 * W] + total[:, 2 * W :])
        )

    @pl.when(jnp.logical_not(bound))
    def _():
        out_ref[...] = base_ref[...]


def nest_kernel(got_ref, out_ref, scr_ref):
    for b in range(2):
        for half in range(2):
            start = b * 2 * W + half * W
            scr_ref[b, :, half * W : (half + 1) * W] = got_ref[start : start + W, :].T
    for b in range(2):
        out_ref[b] = scr_ref[b, :LEV, :]


def stats_kernel(own_ref, other_ref, mean_ref, var_ref):
    a0, a1 = own_ref[0], own_ref[1]
    b0, b1 = other_ref[0], other_ref[1]
    mean = ((a0 + a1) + (b0 + b1)) / 4.0
    mean_ref[...] = mean
    own = (a0 - mean) * (a0 - mean) + (a1 - mean) * (a1 - mean)
    other = (b0 - mean) * (b0 - mean) + (b1 - mean) * (b1 - mean)
    var_ref[...] = (own + other) / 4.0


def exchange(x):
    return lax.all_to_all(x, "tile", split_axis=0, concat_axis=0, tiled=True)


def on_device(parent_state, nest_state, terrain, shift_x, boundary_index, reloc_dest):
    q_mix, e_mix = constants()
    q_mix, e_mix = jnp.asarray(q_mix), jnp.asarray(e_mix)
    sds = jax.ShapeDtypeStruct
    tile = lax.axis_index("tile").astype(jnp.int32).reshape(1)
    parent = parent_state.reshape(2 * LEV, ROWS, W)

    message = call(
        send_kernel,
        sds((4 * NT, W), F32),
        in_specs=[SM, VM, VM, VM],
        scratch=[pltpu.VMEM((2, W, 2 * W), F32)],
        name="send",
        nbytes=1 << 19,
    )(shift_x, nest_state, boundary_index, reloc_dest)
    first = exchange(message.reshape(NT, 4, W)).reshape(4 * NT, W)

    down, up = call(
        halo_kernel,
        (sds((2 * LEV + 1, 4, W), F32), sds((2 * LEV + 1, 4, W), F32)),
        name="halo",
        nbytes=1 << 20,
    )(parent, terrain)
    forward = [(i, i + 1) for i in range(NT - 1)]
    backward = [(i + 1, i) for i in range(NT - 1)]
    from_prev = lax.ppermute(down, "tile", forward)
    from_next = lax.ppermute(up, "tile", backward)
    cells, ring = call(
        parent_kernel,
        (sds((STEPS, 2 * W, ROWS * W), BF16), sds((2 * LEV, RING, W), F32)),
        in_specs=[SM, VM, VM, VM, VM],
        scratch=[pltpu.VMEM((2 * BSTR, W), F32)] * 2,
        name="parent",
        flops=1 << 24,
        nbytes=4 << 20,
    )(tile, parent, from_next, from_prev, terrain)

    values = call(
        gather_kernel,
        sds((16 * NT, W), BF16),
        scratch=[pltpu.VMEM((16 * NT, W), F32)],
        name="gather",
        flops=1 << 29,
        nbytes=3 << 20,
    )(first, cells)
    second = exchange(values.reshape(NT, 16, W)).reshape(16 * NT, W)

    parent_out = call(
        last_parent_kernel,
        sds((2 * LEV, ROWS, W), F32),
        name="last_parent",
        flops=1 << 22,
        nbytes=2 << 20,
    )(ring, terrain)
    hot, base = call(
        plan_kernel,
        (sds((STEPS, 4 * NT, 4 * NT), BF16), sds((4 * NT, W), F32)),
        in_specs=[SM, VM, VM],
        name="plan",
        flops=1 << 28,
        nbytes=3 << 20,
    )(tile, first, q_mix)

    bperm = boundary_index.reshape(STEPS, 32, 4).transpose(0, 2, 1).reshape(STEPS, NT)
    edges = call(
        regroup_kernel,
        sds((16 * NT, W), BF16),
        scratch=[pltpu.VMEM((16 * NT, W), F32), pltpu.VMEM((8 * NT, W), F32)],
        name="regroup",
        flops=1 << 26,
        nbytes=1 << 20,
    )(bperm, second)
    third = exchange(edges.reshape(NT, 16, W)).reshape(16 * NT, W)

    columns = call(
        owner_kernel,
        sds((4 * NT, W), F32),
        in_specs=[SM, VM, VM, VM, VM],
        scratch=[pltpu.VMEM((16 * NT, W), F32)],
        name="owner",
        flops=1 << 29,
        nbytes=3 << 20,
    )(tile, third, hot, base, e_mix)
    fourth = exchange(columns.reshape(NT, 4, W)).reshape(4 * NT, W)

    nest_out = call(
        nest_kernel,
        sds((2, LEV, 2 * W), F32),
        scratch=[pltpu.VMEM((2, W, 2 * W), F32)],
        name="nest",
        nbytes=1 << 19,
    )(fourth)
    other = lax.ppermute(nest_out, "member", [(0, 1), (1, 0)])
    mean, variance = call(
        stats_kernel,
        (sds((LEV, 2 * W), F32), sds((LEV, 2 * W), F32)),
        name="stats",
        nbytes=1 << 19,
    )(nest_out, other)
    return (parent_out.reshape(parent_state.shape), nest_out, mean, variance)


def solution(mesh):
    in_specs = (
        P("member", None, "tile", None),
        P("member", None, "tile"),
        P("tile", None),
        P(),
        P(None, "tile"),
        P(None, "tile"),
    )
    out_specs = (
        P("member", None, "tile", None),
        P("member", None, "tile"),
        P(None, "tile"),
        P(None, "tile"),
    )
    return jax.shard_map(
        on_device, mesh=mesh, in_specs=in_specs, out_specs=out_specs, check_vma=False
    )
```

```python
import functools

import jax
import jax.numpy as jnp
import numpy as np
from jax import lax
from jax.experimental import pallas as pl
from jax.experimental.pallas import tpu as pltpu
from jax.sharding import PartitionSpec as P

F32 = jnp.float32
BF16 = jnp.bfloat16
LEV = 81
STEPS = 4
NT = 128
ROWS = 8
W = 128
LPAD = 96
RING = 16
BSTR = LPAD * RING
L_DEST = 81
L_REQ = 88
HORIZ = 0.15
VERT = 0.1
DRAG = 0.1
RELAX = 0.5
IMPL = 0.8
VMEM_LIMIT = 20 * 1024 * 1024


def solve_matrix():
    n = np.full(LEV, 2.0)
    n[0] = n[-1] = 1.0
    a = np.diag(1.0 + IMPL * n)
    a -= IMPL * (np.eye(LEV, k=1) + np.eye(LEV, k=-1))
    return np.linalg.inv(a)


def padded_transpose(m):
    out = np.zeros((W, W))
    out[:LEV, :LEV] = m.T
    return out


def split3(m):
    m = np.asarray(m, np.float64)
    parts = []
    for _ in range(3):
        part = m.astype(jnp.bfloat16)
        parts.append(part)
        m = m - part.astype(np.float64)
    return parts


def constants():
    s = solve_matrix()
    power = [np.linalg.matrix_power(s, k) for k in range(STEPS + 1)]
    keep = 1.0 - RELAX
    interior = padded_transpose(power[STEPS])
    bound = padded_transpose(power[STEPS] * keep**STEPS)
    q_mix = np.stack([bound, interior]).astype(np.float32)
    stack = np.concatenate(
        [
            padded_transpose(power[STEPS - k] * RELAX * keep ** (STEPS - 1 - k))
            for k in range(STEPS)
        ]
    )
    e_mix = np.concatenate(split3(stack), axis=1)
    return q_mix, e_mix


def call(body, out_shape, in_specs=None, scratch=(), name=None, flops=0, nbytes=0):
    kwargs = {} if in_specs is None else {"in_specs": in_specs}
    return pl.pallas_call(
        body,
        out_shape=out_shape,
        scratch_shapes=list(scratch),
        compiler_params=pltpu.CompilerParams(vmem_limit_bytes=VMEM_LIMIT),
        cost_estimate=pl.CostEstimate(
            flops=flops, bytes_accessed=nbytes, transcendentals=0
        ),
        name=name,
        **kwargs,
    )


VM = pl.BlockSpec(memory_space=pltpu.VMEM)
HB = pl.BlockSpec(memory_space=pltpu.HBM)
SM = pl.BlockSpec(memory_space=pltpu.SMEM)


def start_all(pairs, sems):
    copies = [pltpu.make_async_copy(x, y, sems.at[i]) for i, (x, y) in enumerate(pairs)]
    for copy in copies:
        copy.start()
    return copies


def halo_kernel(parent_hbm, terrain_hbm, down_ref, up_ref, parent_ref, terrain_ref, sems):
    copies = start_all([(parent_hbm, parent_ref), (terrain_hbm, terrain_ref)], sems)
    for copy in copies:
        copy.wait()
    damping = DRAG * terrain_ref[...].astype(F32) / 3000.0
    down_ref[: 2 * LEV, :, :] = parent_ref[:, 4:, :]
    up_ref[: 2 * LEV, :, :] = parent_ref[:, :4, :]
    down_ref[2 * LEV, :, :] = damping[4:, :]
    up_ref[2 * LEV, :, :] = damping[:4, :]


def send_kernel(
    shift_hbm, nest_hbm, bidx_hbm, dest_hbm,
    msg_ref,
    shift_ref, nest_ref, bidx_ref, dest_ref, pad_ref, sems,
):
    copies = start_all(
        [
            (nest_hbm, nest_ref),
            (bidx_hbm, bidx_ref),
            (dest_hbm, dest_ref),
            (shift_hbm, shift_ref),
        ],
        sems,
    )
    for copy in copies:
        copy.wait()
    zeros = jnp.zeros((W - LEV + 1, 2 * W), F32)
    for b in range(2):
        pad_ref[b, LEV - 1 :, :] = zeros
        for half in range(2):
            lanes = slice(half * W, (half + 1) * W)
            pad_ref[b, :LEV, lanes] = nest_ref[:, half, b, :]
        pad_ref[b, L_DEST : L_DEST + STEPS, :] = dest_ref[...].astype(F32)
        for half in range(2):
            block = pad_ref[b, :, half * W : (half + 1) * W]
            start = b * 2 * W + half * W
            msg_ref[start : start + W, :] = block.T
    lane = lax.broadcasted_iota(jnp.int32, (NT, W), 1)
    tile = lax.broadcasted_iota(jnp.int32, (NT, W), 0)
    for s in range(STEPS):
        idx = bidx_ref[s : s + 1, :]
        owner = jnp.right_shift(idx, 10)
        row = jnp.bitwise_and(jnp.right_shift(idx, 7), ROWS - 1)
        col = jnp.bitwise_and(jnp.bitwise_and(idx, W - 1) + shift_ref[s], W - 1)
        cell = (row * W + col + 1).astype(F32)
        mine = tile == owner
        picked = jnp.where(mine, jnp.broadcast_to(cell, (NT, W)), 0.0)
        even = jnp.bitwise_and(lane, 1) == 0
        first = jnp.sum(jnp.where(even, picked, 0.0), axis=1, keepdims=True) - 1.0
        second = jnp.sum(jnp.where(even, 0.0, picked), axis=1, keepdims=True) - 1.0
        rows = msg_ref[pl.ds(s, NT, stride=4), :]
        rows = jnp.where(lane == L_REQ, first, rows)
        rows = jnp.where(lane == L_REQ + 1, second, rows)
        msg_ref[pl.ds(s, NT, stride=4), :] = rows


def ring_step(read, write, level_stride, coef, own_only=False):
    row = lax.broadcasted_iota(jnp.int32, (ROWS, W), 0)
    last = row == ROWS - 1
    head = row == 0
    c0, c1, h1, v1 = coef
    chunk = 9

    def body(step, carry):
        for member in range(2):
            for k in range(chunk):
                level = step * chunk + k
                base = member * level_stride
                below = base + jnp.maximum(level - 1, 0)
                above = base + jnp.minimum(level + 1, LEV - 1)
                x0, x1 = read(base + level)
                d0, d1 = read(below)
                u0, u1 = read(above)
                f0 = pltpu.roll(x0, ROWS - 1, 0)
                f1 = pltpu.roll(x1, ROWS - 1, 0)
                g0 = pltpu.roll(x0, 1, 0)
                g1 = pltpu.roll(x1, 1, 0)
                near0 = jnp.where(last, f1, f0) + jnp.where(head, g1, g0)
                near0 = near0 + (pltpu.roll(x0, 1, 1) + pltpu.roll(x0, W - 1, 1))
                y0 = c0 * x0 + HORIZ * near0 + VERT * (d0 + u0)
                if own_only:
                    write(member, level, y0, None)
                    continue
                near1 = jnp.where(last, f0, f1) + jnp.where(head, g0, g1)
                near1 = near1 + (pltpu.roll(x1, 1, 1) + pltpu.roll(x1, W - 1, 1))
                y1 = c1 * x1 + h1 * near1 + v1 * (d1 + u1)
                write(member, level, y0, y1)
        return carry

    lax.fori_loop(0, LEV // chunk, body, 0)


def parent_kernel(
    tile_ref, parent_hbm, next_hbm, prev_hbm, terrain_hbm,
    cells_ref, ring_ref,
    parent_ref, terrain_ref, next_ref, prev_ref, a_ref, b_ref, sems,
):
    tile = tile_ref[0]
    copies = start_all(
        [
            (parent_hbm, parent_ref),
            (terrain_hbm, terrain_ref),
            (next_hbm, next_ref),
            (prev_hbm, prev_ref),
        ],
        sems,
    )
    for copy in copies[1:]:
        copy.wait()
    damping = DRAG * terrain_ref[...].astype(F32) / 3000.0
    pads = jnp.zeros(((LPAD - LEV) * RING, W), F32)
    for ref in (a_ref, b_ref):
        for member in range(2):
            top = member * BSTR + LEV * RING
            ref[top : top + (LPAD - LEV) * RING, :] = pads
    for s in range(STEPS):
        for member in range(2):
            cells_ref[s, member * W + LPAD : (member + 1) * W, :] = jnp.zeros(
                (W - LPAD, ROWS * W), BF16
            )

    copies[0].wait()

    def fill(level, carry):
        for member in range(2):
            src = member * LEV + level
            base = pl.multiple_of(member * BSTR + level * RING, RING)
            a_ref[pl.ds(base, ROWS), :] = parent_ref[src]
            a_ref[pl.ds(base + 8, 4), :] = next_ref[src]
            a_ref[pl.ds(base + 12, 4), :] = prev_ref[src]
        return carry

    lax.fori_loop(0, LEV, fill, 0)
    b_ref[0:4, :] = next_ref[2 * LEV]
    b_ref[4:8, :] = prev_ref[2 * LEV]
    row = lax.broadcasted_iota(jnp.int32, (ROWS, W), 0)
    south = jnp.where(tile < NT - 1, 1.0, 0.0).astype(F32)
    north = jnp.where(tile > 0, 1.0, 0.0).astype(F32)
    valid = jnp.where(row < 4, south, north)
    stay = 1.0 - 4.0 * HORIZ - 2.0 * VERT
    coef = (stay - damping, (stay - b_ref[0:8, :]) * valid, HORIZ * valid, VERT * valid)

    def emit(s, ref):
        for member in range(2):
            for y in range(ROWS):
                rows = ref[pl.ds(member * BSTR + y, LPAD, stride=RING), :]
                cells_ref[s, member * W : member * W + LPAD, y * W : (y + 1) * W] = (
                    rows.astype(BF16)
                )

    emit(0, a_ref)
    src, dst = a_ref, b_ref
    for s in range(1, STEPS):

        def read(index, src=src):
            base = pl.multiple_of(index * RING, RING)
            return src[pl.ds(base, ROWS), :], src[pl.ds(base + ROWS, ROWS), :]

        def write(member, level, y0, y1, dst=dst):
            base = pl.multiple_of((member * LPAD + level) * RING, RING)
            dst[pl.ds(base, ROWS), :] = y0
            dst[pl.ds(base + ROWS, ROWS), :] = y1

        ring_step(read, write, LPAD, coef)
        emit(s, dst)
        src, dst = dst, src

    def drain(level, carry):
        for member in range(2):
            base = pl.multiple_of((member * LPAD + level) * RING, RING)
            ring_ref[member * LEV + level] = src[pl.ds(base, RING), :]
        return carry

    lax.fori_loop(0, LEV, drain, 0)


def last_parent_kernel(ring_ref, terrain_ref, out_ref):
    damping = DRAG * terrain_ref[...].astype(F32) / 3000.0
    stay = 1.0 - 4.0 * HORIZ - 2.0 * VERT

    def read(index):
        return ring_ref[index, 0:ROWS, :], ring_ref[index, ROWS:RING, :]

    def write(member, level, y0, y1):
        out_ref[member * LEV + level] = y0

    ring_step(read, write, LEV, (stay - damping, None, None, None), own_only=True)


def gather_kernel(got_ref, cells_ref, out_ref, scr_ref):
    lane = lax.broadcasted_iota(jnp.int32, (NT, ROWS * W), 1).astype(F32)
    for s in range(STEPS):
        rows = got_ref[pl.ds(s, NT, stride=4), :]
        hot = [
            jnp.where(lane == rows[:, L_REQ + c : L_REQ + c + 1], 1.0, 0.0).astype(BF16)
            for c in range(2)
        ]
        hot = jnp.concatenate(hot, axis=0)
        res = lax.dot_general(
            hot, cells_ref[s], (((1,), (1,)), ((), ())), preferred_element_type=F32
        )
        for b in range(2):
            for c in range(2):
                scr_ref[pl.ds(b * 8 + s * 2 + c, NT, stride=16), :] = res[
                    c * W : (c + 1) * W, b * W : (b + 1) * W
                ]
    out_ref[...] = scr_ref[...].astype(BF16)


def regroup_kernel(bperm_ref, got_ref, out_ref, scr_ref, scr2_ref):
    scr_ref[...] = got_ref[...].astype(F32)
    sub = lax.broadcasted_iota(jnp.int32, (2 * NT, W), 0)
    lane = lax.broadcasted_iota(jnp.int32, (2 * NT, W), 1)
    parity = jnp.bitwise_and(jnp.right_shift(lane, 5), 1)
    target = sub - parity * NT
    for s in range(STEPS):
        owner = jnp.right_shift(bperm_ref[s : s + 1, :], 10)
        hot = jnp.where(target == owner, 1.0, 0.0).astype(BF16)
        values = jnp.concatenate(
            [
                jnp.concatenate(
                    [
                        scr_ref[pl.ds(b * 8 + s * 2 + c, NT, stride=16), :]
                        for b in range(2)
                    ],
                    axis=1,
                )
                for c in range(2)
            ],
            axis=0,
        ).astype(BF16)
        res = lax.dot_general(
            hot, values, (((0,), (0,)), ((), ())), preferred_element_type=F32
        )
        for b in range(2):
            for j in range(4):
                scr2_ref[pl.ds(b * 512 + s * 4 + j, 32, stride=16), :] = res[
                    j * 32 : (j + 1) * 32, b * W : (b + 1) * W
                ]
    for b in range(2):
        out_ref[b * 1024 : b * 1024 + 512, :] = scr2_ref[b * 512 : (b + 1) * 512, :].astype(
            BF16
        )
        out_ref[b * 1024 + 512 : (b + 1) * 1024, :] = jnp.zeros((512, W), BF16)


def plan_kernel(tile_ref, got_ref, mix_ref, hot_ref, base_ref):
    interior = jnp.where(jnp.bitwise_and(tile_ref[0], 63) < 32, 0, 1)
    n = 4 * NT
    turned = [got_ref[pl.ds(j, NT, stride=4), :].T for j in range(4)]
    sub = lax.broadcasted_iota(jnp.int32, (n, n), 0)

    def dest(s):
        row = jnp.concatenate(
            [t[L_DEST + s : L_DEST + s + 1, :] for t in turned], axis=1
        ).astype(jnp.int32)
        return jnp.right_shift(row, 8), jnp.bitwise_and(row, 3)

    tile_to, slot_to = dest(STEPS - 1)
    for s in range(STEPS - 1, -1, -1):
        if s < STEPS - 1:
            mid_tile, mid_slot = dest(s)
            move = jnp.where(sub == mid_slot * NT + mid_tile, 1.0, 0.0).astype(BF16)
            later = jnp.concatenate(
                [
                    jnp.broadcast_to(tile_to, (8, n)),
                    jnp.broadcast_to(slot_to, (8, n)),
                ],
                axis=0,
            )
            both = jnp.dot(
                later.astype(F32).astype(BF16), move, preferred_element_type=F32
            )
            tile_to = both[0:1, :].astype(jnp.int32)
            slot_to = both[8:9, :].astype(jnp.int32)
        hot_ref[s] = jnp.where(sub == tile_to * 4 + slot_to, 1.0, 0.0).astype(BF16)
    columns = jnp.concatenate(
        [got_ref[pl.ds(j, NT, stride=4), :] for j in range(4)], axis=0
    )
    mixed = lax.dot_general(
        columns,
        mix_ref[interior],
        (((1,), (0,)), ((), ())),
        precision=lax.Precision.HIGHEST,
        preferred_element_type=F32,
    )
    parts = []
    for _ in range(3):
        part = mixed.astype(BF16)
        parts.append(part)
        mixed = mixed - part.astype(F32)
    moved = jnp.dot(
        hot_ref[0], jnp.concatenate(parts, axis=1), preferred_element_type=F32
    )
    base_ref[...] = moved[:, :W] + (moved[:, W : 2 * W] + moved[:, 2 * W :])


def owner_kernel(tile_ref, got_ref, hot_ref, base_ref, mix_ref, out_ref, scr_ref):
    bound = jnp.bitwise_and(tile_ref[0], 63) < 32

    @pl.when(bound)
    def _():
        scr_ref[...] = got_ref[...].astype(F32)
        moved = []
        for s in range(STEPS):
            edge = jnp.concatenate(
                [scr_ref[pl.ds(s * 4 + j, NT, stride=16), :] for j in range(4)], axis=0
            ).astype(BF16)
            moved.append(
                jnp.dot(hot_ref[s], edge, preferred_element_type=F32).astype(BF16)
            )
        total = jnp.dot(
            jnp.concatenate(moved, axis=1), mix_ref[...], preferred_element_type=F32
        )
        out_ref[...] = base_ref[...] + (
            total[:, :W] + (total[:, W : 2 * W] + total[:, 2 * W :])
        )

    @pl.when(jnp.logical_not(bound))
    def _():
        out_ref[...] = base_ref[...]


def nest_kernel(got_ref, out_ref, scr_ref):
    for b in range(2):
        for half in range(2):
            start = b * 2 * W + half * W
            scr_ref[...] = got_ref[start : start + W, :].T
            out_ref[pl.ds(half * 2 + b, LEV, stride=4), :] = scr_ref[:LEV, :]


def stats_kernel(own_ref, other_ref, mean_ref, var_ref):
    for half in range(2):
        a0, a1, b0, b1 = (
            ref[pl.ds(half * 2 + b, LEV, stride=4), :]
            for ref in (own_ref, other_ref)
            for b in range(2)
        )
        lanes = slice(half * W, (half + 1) * W)
        mean = ((a0 + a1) + (b0 + b1)) / 4.0
        mean_ref[:, lanes] = mean
        own = (a0 - mean) * (a0 - mean) + (a1 - mean) * (a1 - mean)
        other = (b0 - mean) * (b0 - mean) + (b1 - mean) * (b1 - mean)
        var_ref[:, lanes] = (own + other) / 4.0


def in_hbm(x):
    return pltpu.with_memory_space_constraint(x, pltpu.HBM)


def exchange(x):
    return lax.all_to_all(x, "tile", split_axis=0, concat_axis=0, tiled=True)


def on_device(parent_state, nest_state, terrain, shift_x, boundary_index, reloc_dest):
    q_mix, e_mix = constants()
    q_mix, e_mix = jnp.asarray(q_mix), jnp.asarray(e_mix)
    sds = jax.ShapeDtypeStruct
    tile = lax.axis_index("tile").astype(jnp.int32).reshape(1)
    parent = parent_state.reshape(2 * LEV, ROWS, W)

    nest = nest_state.reshape(2, LEV, 2, W).transpose(1, 2, 0, 3)
    parent, terrain = in_hbm(parent), in_hbm(terrain)
    down, up = call(
        halo_kernel,
        (sds((2 * LEV + 1, 4, W), F32), sds((2 * LEV + 1, 4, W), F32)),
        in_specs=[HB] * 2,
        scratch=[
            pltpu.VMEM((2 * LEV, ROWS, W), F32),
            pltpu.VMEM((ROWS, W), jnp.int32),
            pltpu.SemaphoreType.DMA((2,)),
        ],
        name="halo",
        nbytes=1 << 20,
    )(parent, terrain)
    nest, down, up = lax.optimization_barrier((nest, down, up))
    nest = in_hbm(nest)
    message = call(
        send_kernel,
        sds((4 * NT, W), F32),
        in_specs=[HB] * 4,
        scratch=[
            pltpu.SMEM((STEPS,), jnp.int32),
            pltpu.VMEM((LEV, 2, 2, W), F32),
            pltpu.VMEM((STEPS, NT), jnp.int32),
            pltpu.VMEM((STEPS, 2 * W), jnp.int32),
            pltpu.VMEM((2, W, 2 * W), F32),
            pltpu.SemaphoreType.DMA((4,)),
        ],
        name="send",
        nbytes=64 << 20,
    )(in_hbm(shift_x), nest, in_hbm(boundary_index), in_hbm(reloc_dest))
    forward = [(i, i + 1) for i in range(NT - 1)]
    backward = [(i + 1, i) for i in range(NT - 1)]
    from_prev = lax.ppermute(down, "tile", forward)
    from_next = lax.ppermute(up, "tile", backward)
    first = exchange(message.reshape(NT, 4, W)).reshape(4 * NT, W)
    cells, ring = call(
        parent_kernel,
        (sds((STEPS, 2 * W, ROWS * W), BF16), sds((2 * LEV, RING, W), F32)),
        in_specs=[SM, HB, HB, HB, HB],
        scratch=[
            pltpu.VMEM((2 * LEV, ROWS, W), F32),
            pltpu.VMEM((ROWS, W), jnp.int32),
            pltpu.VMEM((2 * LEV + 1, 4, W), F32),
            pltpu.VMEM((2 * LEV + 1, 4, W), F32),
            pltpu.VMEM((2 * BSTR, W), F32),
            pltpu.VMEM((2 * BSTR, W), F32),
            pltpu.SemaphoreType.DMA((4,)),
        ],
        name="parent",
        flops=1 << 24,
        nbytes=4 << 20,
    )(tile, parent, in_hbm(from_next), in_hbm(from_prev), terrain)

    values = call(
        gather_kernel,
        sds((16 * NT, W), BF16),
        scratch=[pltpu.VMEM((16 * NT, W), F32)],
        name="gather",
        flops=1 << 29,
        nbytes=3 << 20,
    )(first, cells)
    second = exchange(values.reshape(NT, 16, W)).reshape(16 * NT, W)

    parent_out = call(
        last_parent_kernel,
        sds((2 * LEV, ROWS, W), F32),
        name="last_parent",
        flops=1 << 22,
        nbytes=2 << 20,
    )(ring, terrain)
    hot, base = call(
        plan_kernel,
        (sds((STEPS, 4 * NT, 4 * NT), BF16), sds((4 * NT, W), F32)),
        in_specs=[SM, VM, VM],
        name="plan",
        flops=1 << 28,
        nbytes=3 << 20,
    )(tile, first, q_mix)

    second, parent_out = lax.optimization_barrier((second, parent_out))
    bperm = boundary_index.reshape(STEPS, 32, 4).transpose(0, 2, 1).reshape(STEPS, NT)
    edges = call(
        regroup_kernel,
        sds((16 * NT, W), BF16),
        scratch=[pltpu.VMEM((16 * NT, W), F32), pltpu.VMEM((8 * NT, W), F32)],
        name="regroup",
        flops=1 << 26,
        nbytes=1 << 20,
    )(bperm, second)
    third = exchange(edges.reshape(NT, 16, W)).reshape(16 * NT, W)

    columns = call(
        owner_kernel,
        sds((4 * NT, W), F32),
        in_specs=[SM, VM, VM, VM, VM],
        scratch=[pltpu.VMEM((16 * NT, W), F32)],
        name="owner",
        flops=1 << 29,
        nbytes=3 << 20,
    )(tile, third, hot, base, e_mix)
    fourth = exchange(columns.reshape(NT, 4, W)).reshape(4 * NT, W)

    nest_out = call(
        nest_kernel,
        sds((4 * LEV, W), F32),
        scratch=[pltpu.VMEM((W, W), F32)],
        name="nest",
        nbytes=1 << 19,
    )(fourth)
    other = lax.ppermute(nest_out, "member", [(0, 1), (1, 0)])
    mean, variance = call(
        stats_kernel,
        (sds((LEV, 2 * W), F32), sds((LEV, 2 * W), F32)),
        name="stats",
        nbytes=1 << 19,
    )(nest_out, other)
    nest_out = nest_out.reshape(LEV, 2, 2, W).transpose(2, 0, 1, 3)
    nest_out = nest_out.reshape(nest_state.shape)
    return (parent_out.reshape(parent_state.shape), nest_out, mean, variance)


def solution(mesh):
    in_specs = (
        P("member", None, "tile", None),
        P("member", None, "tile"),
        P("tile", None),
        P(),
        P(None, "tile"),
        P(None, "tile"),
    )
    out_specs = (
        P("member", None, "tile", None),
        P("member", None, "tile"),
        P(None, "tile"),
        P(None, "tile"),
    )
    return jax.shard_map(
        on_device, mesh=mesh, in_specs=in_specs, out_specs=out_specs, check_vma=False
    )
```

```python
import functools

import jax
import jax.numpy as jnp
import numpy as np
from jax import lax
from jax.experimental import pallas as pl
from jax.experimental.pallas import tpu as pltpu
from jax.sharding import PartitionSpec as P

F32 = jnp.float32
BF16 = jnp.bfloat16
LEV = 81
STEPS = 4
NT = 128
ROWS = 8
W = 128
LPAD = 96
RING = 16
BSTR = LPAD * RING
L_DEST = 81
L_REQ = 88
HORIZ = 0.15
VERT = 0.1
DRAG = 0.1
RELAX = 0.5
IMPL = 0.8
VMEM_LIMIT = 20 * 1024 * 1024


def solve_matrix():
    n = np.full(LEV, 2.0)
    n[0] = n[-1] = 1.0
    a = np.diag(1.0 + IMPL * n)
    a -= IMPL * (np.eye(LEV, k=1) + np.eye(LEV, k=-1))
    return np.linalg.inv(a)


def padded_transpose(m):
    out = np.zeros((W, W))
    out[:LEV, :LEV] = m.T
    return out


def split3(m):
    m = np.asarray(m, np.float64)
    parts = []
    for _ in range(3):
        part = m.astype(jnp.bfloat16)
        parts.append(part)
        m = m - part.astype(np.float64)
    return parts


def constants():
    s = solve_matrix()
    power = [np.linalg.matrix_power(s, k) for k in range(STEPS + 1)]
    keep = 1.0 - RELAX
    interior = padded_transpose(power[STEPS])
    bound = padded_transpose(power[STEPS] * keep**STEPS)
    q_mix = np.stack([bound, interior]).astype(np.float32)
    stack = np.concatenate(
        [
            padded_transpose(power[STEPS - k] * RELAX * keep ** (STEPS - 1 - k))
            for k in range(STEPS)
        ]
    )
    e_mix = np.concatenate(split3(stack), axis=1)
    return q_mix, e_mix


def call(body, out_shape, in_specs=None, scratch=(), name=None, flops=0, nbytes=0):
    kwargs = {} if in_specs is None else {"in_specs": in_specs}
    return pl.pallas_call(
        body,
        out_shape=out_shape,
        scratch_shapes=list(scratch),
        compiler_params=pltpu.CompilerParams(vmem_limit_bytes=VMEM_LIMIT),
        cost_estimate=pl.CostEstimate(
            flops=flops, bytes_accessed=nbytes, transcendentals=0
        ),
        name=name,
        **kwargs,
    )


VM = pl.BlockSpec(memory_space=pltpu.VMEM)
HB = pl.BlockSpec(memory_space=pltpu.HBM)
SM = pl.BlockSpec(memory_space=pltpu.SMEM)


def start_all(pairs, sems):
    copies = [pltpu.make_async_copy(x, y, sems.at[i]) for i, (x, y) in enumerate(pairs)]
    for copy in copies:
        copy.start()
    return copies


def halo_kernel(parent_hbm, terrain_hbm, down_ref, up_ref, parent_ref, terrain_ref, sems):
    copies = start_all([(parent_hbm, parent_ref), (terrain_hbm, terrain_ref)], sems)
    for copy in copies:
        copy.wait()
    damping = DRAG * terrain_ref[...].astype(F32) / 3000.0
    down_ref[: 2 * LEV, :, :] = parent_ref[:, 4:, :]
    up_ref[: 2 * LEV, :, :] = parent_ref[:, :4, :]
    down_ref[2 * LEV, :, :] = damping[4:, :]
    up_ref[2 * LEV, :, :] = damping[:4, :]


def send_kernel(
    shift_hbm, nest_hbm, bidx_hbm, dest_hbm,
    msg_ref,
    shift_ref, nest_ref, bidx_ref, dest_ref, pad_ref, sems,
):
    copies = start_all(
        [
            (nest_hbm, nest_ref),
            (bidx_hbm, bidx_ref),
            (dest_hbm, dest_ref),
            (shift_hbm, shift_ref),
        ],
        sems,
    )
    for copy in copies:
        copy.wait()
    zeros = jnp.zeros((W - LEV + 1, 2 * W), F32)
    for b in range(2):
        pad_ref[b, LEV - 1 :, :] = zeros
        for half in range(2):
            lanes = slice(half * W, (half + 1) * W)
            pad_ref[b, :LEV, lanes] = nest_ref[:, half, b, :]
        pad_ref[b, L_DEST : L_DEST + STEPS, :] = dest_ref[...].astype(F32)
        for half in range(2):
            block = pad_ref[b, :, half * W : (half + 1) * W]
            start = b * 2 * W + half * W
            msg_ref[start : start + W, :] = block.T
    lane = lax.broadcasted_iota(jnp.int32, (NT, W), 1)
    tile = lax.broadcasted_iota(jnp.int32, (NT, W), 0)
    for s in range(STEPS):
        idx = bidx_ref[s : s + 1, :]
        owner = jnp.right_shift(idx, 10)
        row = jnp.bitwise_and(jnp.right_shift(idx, 7), ROWS - 1)
        col = jnp.bitwise_and(jnp.bitwise_and(idx, W - 1) + shift_ref[s], W - 1)
        cell = (row * W + col + 1).astype(F32)
        mine = tile == owner
        picked = jnp.where(mine, jnp.broadcast_to(cell, (NT, W)), 0.0)
        even = jnp.bitwise_and(lane, 1) == 0
        first = jnp.sum(jnp.where(even, picked, 0.0), axis=1, keepdims=True) - 1.0
        second = jnp.sum(jnp.where(even, 0.0, picked), axis=1, keepdims=True) - 1.0
        rows = msg_ref[pl.ds(s, NT, stride=4), :]
        rows = jnp.where(lane == L_REQ, first, rows)
        rows = jnp.where(lane == L_REQ + 1, second, rows)
        msg_ref[pl.ds(s, NT, stride=4), :] = rows


def ring_step(read, write, level_stride, coef, own_only=False):
    row = lax.broadcasted_iota(jnp.int32, (ROWS, W), 0)
    last = row == ROWS - 1
    head = row == 0
    c0, c1, h1, v1 = coef
    chunk = 9

    def body(step, carry):
        for member in range(2):
            for k in range(chunk):
                level = step * chunk + k
                base = member * level_stride
                below = base + jnp.maximum(level - 1, 0)
                above = base + jnp.minimum(level + 1, LEV - 1)
                x0, x1 = read(base + level)
                d0, d1 = read(below)
                u0, u1 = read(above)
                f0 = pltpu.roll(x0, ROWS - 1, 0)
                f1 = pltpu.roll(x1, ROWS - 1, 0)
                g0 = pltpu.roll(x0, 1, 0)
                g1 = pltpu.roll(x1, 1, 0)
                near0 = jnp.where(last, f1, f0) + jnp.where(head, g1, g0)
                near0 = near0 + (pltpu.roll(x0, 1, 1) + pltpu.roll(x0, W - 1, 1))
                y0 = c0 * x0 + HORIZ * near0 + VERT * (d0 + u0)
                if own_only:
                    write(member, level, y0, None)
                    continue
                near1 = jnp.where(last, f0, f1) + jnp.where(head, g0, g1)
                near1 = near1 + (pltpu.roll(x1, 1, 1) + pltpu.roll(x1, W - 1, 1))
                y1 = c1 * x1 + h1 * near1 + v1 * (d1 + u1)
                write(member, level, y0, y1)
        return carry

    lax.fori_loop(0, LEV // chunk, body, 0)


def parent_kernel(
    tile_ref, parent_hbm, next_hbm, prev_hbm, terrain_hbm,
    cells_ref, ring_ref,
    parent_ref, terrain_ref, next_ref, prev_ref, a_ref, b_ref, sems,
):
    tile = tile_ref[0]
    copies = start_all(
        [
            (parent_hbm, parent_ref),
            (terrain_hbm, terrain_ref),
            (next_hbm, next_ref),
            (prev_hbm, prev_ref),
        ],
        sems,
    )
    for copy in copies[1:]:
        copy.wait()
    damping = DRAG * terrain_ref[...].astype(F32) / 3000.0
    pads = jnp.zeros(((LPAD - LEV) * RING, W), F32)
    for ref in (a_ref, b_ref):
        for member in range(2):
            top = member * BSTR + LEV * RING
            ref[top : top + (LPAD - LEV) * RING, :] = pads
    for s in range(STEPS):
        for member in range(2):
            cells_ref[s, member * W + LPAD : (member + 1) * W, :] = jnp.zeros(
                (W - LPAD, ROWS * W), BF16
            )

    copies[0].wait()

    def fill(level, carry):
        for member in range(2):
            src = member * LEV + level
            base = pl.multiple_of(member * BSTR + level * RING, RING)
            a_ref[pl.ds(base, ROWS), :] = parent_ref[src]
            a_ref[pl.ds(base + 8, 4), :] = next_ref[src]
            a_ref[pl.ds(base + 12, 4), :] = prev_ref[src]
        return carry

    lax.fori_loop(0, LEV, fill, 0)
    b_ref[0:4, :] = next_ref[2 * LEV]
    b_ref[4:8, :] = prev_ref[2 * LEV]
    row = lax.broadcasted_iota(jnp.int32, (ROWS, W), 0)
    south = jnp.where(tile < NT - 1, 1.0, 0.0).astype(F32)
    north = jnp.where(tile > 0, 1.0, 0.0).astype(F32)
    valid = jnp.where(row < 4, south, north)
    stay = 1.0 - 4.0 * HORIZ - 2.0 * VERT
    coef = (stay - damping, (stay - b_ref[0:8, :]) * valid, HORIZ * valid, VERT * valid)

    def emit(s, ref):
        for member in range(2):
            for y in range(ROWS):
                rows = ref[pl.ds(member * BSTR + y, LPAD, stride=RING), :]
                cells_ref[s, member * W : member * W + LPAD, y * W : (y + 1) * W] = (
                    rows.astype(BF16)
                )

    emit(0, a_ref)
    src, dst = a_ref, b_ref
    for s in range(1, STEPS):

        def read(index, src=src):
            base = pl.multiple_of(index * RING, RING)
            return src[pl.ds(base, ROWS), :], src[pl.ds(base + ROWS, ROWS), :]

        def write(member, level, y0, y1, dst=dst):
            base = pl.multiple_of((member * LPAD + level) * RING, RING)
            dst[pl.ds(base, ROWS), :] = y0
            dst[pl.ds(base + ROWS, ROWS), :] = y1

        ring_step(read, write, LPAD, coef)
        emit(s, dst)
        src, dst = dst, src

    def drain(level, carry):
        for member in range(2):
            base = pl.multiple_of((member * LPAD + level) * RING, RING)
            ring_ref[member * LEV + level] = src[pl.ds(base, RING), :]
        return carry

    lax.fori_loop(0, LEV, drain, 0)


def last_parent_kernel(ring_ref, terrain_ref, out_ref):
    damping = DRAG * terrain_ref[...].astype(F32) / 3000.0
    stay = 1.0 - 4.0 * HORIZ - 2.0 * VERT

    def read(index):
        return ring_ref[index, 0:ROWS, :], ring_ref[index, ROWS:RING, :]

    def write(member, level, y0, y1):
        out_ref[member * LEV + level] = y0

    ring_step(read, write, LEV, (stay - damping, None, None, None), own_only=True)


def gather_kernel(got_ref, cells_ref, out_ref, scr_ref):
    lane = lax.broadcasted_iota(jnp.int32, (NT, ROWS * W), 1).astype(F32)
    for s in range(STEPS):
        rows = got_ref[pl.ds(s, NT, stride=4), :]
        hot = [
            jnp.where(lane == rows[:, L_REQ + c : L_REQ + c + 1], 1.0, 0.0).astype(BF16)
            for c in range(2)
        ]
        hot = jnp.concatenate(hot, axis=0)
        res = lax.dot_general(
            hot, cells_ref[s], (((1,), (1,)), ((), ())), preferred_element_type=F32
        )
        for b in range(2):
            for c in range(2):
                scr_ref[pl.ds(b * 8 + s * 2 + c, NT, stride=16), :] = res[
                    c * W : (c + 1) * W, b * W : (b + 1) * W
                ]
    out_ref[...] = scr_ref[...].astype(BF16)


def regroup_kernel(bperm_ref, got_ref, out_ref, scr_ref, scr2_ref):
    scr_ref[...] = got_ref[...].astype(F32)
    sub = lax.broadcasted_iota(jnp.int32, (2 * NT, W), 0)
    lane = lax.broadcasted_iota(jnp.int32, (2 * NT, W), 1)
    parity = jnp.bitwise_and(jnp.right_shift(lane, 5), 1)
    target = sub - parity * NT
    for s in range(STEPS):
        owner = jnp.right_shift(bperm_ref[s : s + 1, :], 10)
        hot = jnp.where(target == owner, 1.0, 0.0).astype(BF16)
        values = jnp.concatenate(
            [
                jnp.concatenate(
                    [
                        scr_ref[pl.ds(b * 8 + s * 2 + c, NT, stride=16), :]
                        for b in range(2)
                    ],
                    axis=1,
                )
                for c in range(2)
            ],
            axis=0,
        ).astype(BF16)
        res = lax.dot_general(
            hot, values, (((0,), (0,)), ((), ())), preferred_element_type=F32
        )
        for b in range(2):
            for j in range(4):
                scr2_ref[pl.ds(b * 512 + s * 4 + j, 32, stride=16), :] = res[
                    j * 32 : (j + 1) * 32, b * W : (b + 1) * W
                ]
    for b in range(2):
        out_ref[b * 1024 : b * 1024 + 512, :] = scr2_ref[b * 512 : (b + 1) * 512, :].astype(
            BF16
        )
        out_ref[b * 1024 + 512 : (b + 1) * 1024, :] = jnp.zeros((512, W), BF16)


def plan_kernel(tile_ref, got_ref, mix_ref, hot_ref, base_ref):
    interior = jnp.where(jnp.bitwise_and(tile_ref[0], 63) < 32, 0, 1)
    n = 4 * NT
    turned = [got_ref[pl.ds(j, NT, stride=4), :].T for j in range(4)]
    sub = lax.broadcasted_iota(jnp.int32, (n, n), 0)

    def dest(s):
        row = jnp.concatenate(
            [t[L_DEST + s : L_DEST + s + 1, :] for t in turned], axis=1
        ).astype(jnp.int32)
        return jnp.right_shift(row, 8), jnp.bitwise_and(row, 3)

    tile_to, slot_to = dest(STEPS - 1)
    for s in range(STEPS - 1, -1, -1):
        if s < STEPS - 1:
            mid_tile, mid_slot = dest(s)
            move = jnp.where(sub == mid_slot * NT + mid_tile, 1.0, 0.0).astype(BF16)
            later = jnp.concatenate(
                [
                    jnp.broadcast_to(tile_to, (8, n)),
                    jnp.broadcast_to(slot_to, (8, n)),
                ],
                axis=0,
            )
            both = jnp.dot(
                later.astype(F32).astype(BF16), move, preferred_element_type=F32
            )
            tile_to = both[0:1, :].astype(jnp.int32)
            slot_to = both[8:9, :].astype(jnp.int32)
        hot_ref[s] = jnp.where(sub == tile_to * 4 + slot_to, 1.0, 0.0).astype(BF16)
    columns = jnp.concatenate(
        [got_ref[pl.ds(j, NT, stride=4), :] for j in range(4)], axis=0
    )
    mixed = lax.dot_general(
        columns,
        mix_ref[interior],
        (((1,), (0,)), ((), ())),
        precision=lax.Precision.HIGHEST,
        preferred_element_type=F32,
    )
    parts = []
    for _ in range(3):
        part = mixed.astype(BF16)
        parts.append(part)
        mixed = mixed - part.astype(F32)
    moved = jnp.dot(
        hot_ref[0], jnp.concatenate(parts, axis=1), preferred_element_type=F32
    )
    base_ref[...] = moved[:, :W] + (moved[:, W : 2 * W] + moved[:, 2 * W :])


def owner_kernel(tile_ref, got_ref, hot_ref, base_ref, mix_ref, out_ref, scr_ref):
    bound = jnp.bitwise_and(tile_ref[0], 63) < 32

    @pl.when(bound)
    def _():
        scr_ref[...] = got_ref[...].astype(F32)
        moved = []
        for s in range(STEPS):
            edge = jnp.concatenate(
                [scr_ref[pl.ds(s * 4 + j, NT, stride=16), :] for j in range(4)], axis=0
            ).astype(BF16)
            moved.append(
                jnp.dot(hot_ref[s], edge, preferred_element_type=F32).astype(BF16)
            )
        total = jnp.dot(
            jnp.concatenate(moved, axis=1), mix_ref[...], preferred_element_type=F32
        )
        out_ref[...] = base_ref[...] + (
            total[:, :W] + (total[:, W : 2 * W] + total[:, 2 * W :])
        )

    @pl.when(jnp.logical_not(bound))
    def _():
        out_ref[...] = base_ref[...]


def nest_kernel(got_ref, out_ref, scr_ref):
    for b in range(2):
        for half in range(2):
            start = b * 2 * W + half * W
            scr_ref[...] = got_ref[start : start + W, :].T
            out_ref[pl.ds(half * 2 + b, LEV, stride=4), :] = scr_ref[:LEV, :]


def stats_kernel(own_ref, other_ref, mean_ref, var_ref):
    for half in range(2):
        a0, a1, b0, b1 = (
            ref[pl.ds(half * 2 + b, LEV, stride=4), :]
            for ref in (own_ref, other_ref)
            for b in range(2)
        )
        lanes = slice(half * W, (half + 1) * W)
        mean = ((a0 + a1) + (b0 + b1)) / 4.0
        mean_ref[:, lanes] = mean
        own = (a0 - mean) * (a0 - mean) + (a1 - mean) * (a1 - mean)
        other = (b0 - mean) * (b0 - mean) + (b1 - mean) * (b1 - mean)
        var_ref[:, lanes] = (own + other) / 4.0


def in_hbm(x):
    return pltpu.with_memory_space_constraint(x, pltpu.HBM)


def exchange(x):
    return lax.all_to_all(x, "tile", split_axis=0, concat_axis=0, tiled=True)


def on_device(parent_state, nest_state, terrain, shift_x, boundary_index, reloc_dest):
    q_mix, e_mix = constants()
    q_mix, e_mix = jnp.asarray(q_mix), jnp.asarray(e_mix)
    sds = jax.ShapeDtypeStruct
    tile = lax.axis_index("tile").astype(jnp.int32).reshape(1)
    parent = parent_state.reshape(2 * LEV, ROWS, W)

    nest = nest_state.reshape(2, LEV, 2, W).transpose(1, 2, 0, 3)
    parent, terrain = in_hbm(parent), in_hbm(terrain)
    down, up = call(
        halo_kernel,
        (sds((2 * LEV + 1, 4, W), F32), sds((2 * LEV + 1, 4, W), F32)),
        in_specs=[HB] * 2,
        scratch=[
            pltpu.VMEM((2 * LEV, ROWS, W), F32),
            pltpu.VMEM((ROWS, W), jnp.int32),
            pltpu.SemaphoreType.DMA((2,)),
        ],
        name="halo",
        nbytes=1 << 20,
    )(parent, terrain)
    nest, down, up = lax.optimization_barrier((nest, down, up))
    nest = in_hbm(nest)
    message = call(
        send_kernel,
        sds((4 * NT, W), F32),
        in_specs=[HB] * 4,
        scratch=[
            pltpu.SMEM((STEPS,), jnp.int32),
            pltpu.VMEM((LEV, 2, 2, W), F32),
            pltpu.VMEM((STEPS, NT), jnp.int32),
            pltpu.VMEM((STEPS, 2 * W), jnp.int32),
            pltpu.VMEM((2, W, 2 * W), F32),
            pltpu.SemaphoreType.DMA((4,)),
        ],
        name="send",
        nbytes=64 << 20,
    )(in_hbm(shift_x), nest, in_hbm(boundary_index), in_hbm(reloc_dest))
    forward = [(i, i + 1) for i in range(NT - 1)]
    backward = [(i + 1, i) for i in range(NT - 1)]
    from_prev = lax.ppermute(down, "tile", forward)
    from_next = lax.ppermute(up, "tile", backward)
    first = exchange(message.reshape(NT, 4, W)).reshape(4 * NT, W)
    cells, ring = call(
        parent_kernel,
        (
            pltpu.VMEM((STEPS, 2 * W, ROWS * W), BF16),
            pltpu.VMEM((2 * LEV, RING, W), F32),
        ),
        in_specs=[SM, HB, HB, HB, HB],
        scratch=[
            pltpu.VMEM((2 * LEV, ROWS, W), F32),
            pltpu.VMEM((ROWS, W), jnp.int32),
            pltpu.VMEM((2 * LEV + 1, 4, W), F32),
            pltpu.VMEM((2 * LEV + 1, 4, W), F32),
            pltpu.VMEM((2 * BSTR, W), F32),
            pltpu.VMEM((2 * BSTR, W), F32),
            pltpu.SemaphoreType.DMA((4,)),
        ],
        name="parent",
        flops=1 << 40,
        nbytes=1 << 36,
    )(tile, parent, in_hbm(from_next), in_hbm(from_prev), terrain)

    values = call(
        gather_kernel,
        sds((16 * NT, W), BF16),
        scratch=[pltpu.VMEM((16 * NT, W), F32)],
        name="gather",
        flops=1 << 29,
        nbytes=3 << 20,
    )(first, cells)
    second = exchange(values.reshape(NT, 16, W)).reshape(16 * NT, W)

    parent_out = call(
        last_parent_kernel,
        sds((2 * LEV, ROWS, W), F32),
        name="last_parent",
        flops=1 << 22,
        nbytes=2 << 20,
    )(ring, terrain)
    hot, base = call(
        plan_kernel,
        (sds((STEPS, 4 * NT, 4 * NT), BF16), sds((4 * NT, W), F32)),
        in_specs=[SM, VM, VM],
        name="plan",
        flops=1 << 28,
        nbytes=3 << 20,
    )(tile, first, q_mix)

    second, parent_out = lax.optimization_barrier((second, parent_out))
    bperm = boundary_index.reshape(STEPS, 32, 4).transpose(0, 2, 1).reshape(STEPS, NT)
    edges = call(
        regroup_kernel,
        sds((16 * NT, W), BF16),
        scratch=[pltpu.VMEM((16 * NT, W), F32), pltpu.VMEM((8 * NT, W), F32)],
        name="regroup",
        flops=1 << 26,
        nbytes=1 << 20,
    )(bperm, second)
    third = exchange(edges.reshape(NT, 16, W)).reshape(16 * NT, W)

    columns = call(
        owner_kernel,
        sds((4 * NT, W), F32),
        in_specs=[SM, VM, VM, VM, VM],
        scratch=[pltpu.VMEM((16 * NT, W), F32)],
        name="owner",
        flops=1 << 29,
        nbytes=3 << 20,
    )(tile, third, hot, base, e_mix)
    fourth = exchange(columns.reshape(NT, 4, W)).reshape(4 * NT, W)

    nest_out = call(
        nest_kernel,
        sds((4 * LEV, W), F32),
        scratch=[pltpu.VMEM((W, W), F32)],
        name="nest",
        nbytes=1 << 19,
    )(fourth)
    other = lax.ppermute(nest_out, "member", [(0, 1), (1, 0)])
    mean, variance = call(
        stats_kernel,
        (sds((LEV, 2 * W), F32), sds((LEV, 2 * W), F32)),
        name="stats",
        nbytes=1 << 19,
    )(nest_out, other)
    nest_out = nest_out.reshape(LEV, 2, 2, W).transpose(2, 0, 1, 3)
    nest_out = nest_out.reshape(nest_state.shape)
    return (parent_out.reshape(parent_state.shape), nest_out, mean, variance)


def solution(mesh):
    in_specs = (
        P("member", None, "tile", None),
        P("member", None, "tile"),
        P("tile", None),
        P(),
        P(None, "tile"),
        P(None, "tile"),
    )
    out_specs = (
        P("member", None, "tile", None),
        P("member", None, "tile"),
        P(None, "tile"),
        P(None, "tile"),
    )
    return jax.shard_map(
        on_device, mesh=mesh, in_specs=in_specs, out_specs=out_specs, check_vma=False
    )
```

```python
import functools

import jax
import jax.numpy as jnp
import numpy as np
from jax import lax
from jax.experimental import pallas as pl
from jax.experimental.pallas import tpu as pltpu
from jax.sharding import PartitionSpec as P

F32 = jnp.float32
BF16 = jnp.bfloat16
LEV = 81
STEPS = 4
NT = 128
ROWS = 8
W = 128
LPAD = 96
RING = 16
BSTR = LPAD * RING
SPLIT = 40
L_TOP = 81
L_REQ = 86
L_INNER = 88
L_DEST = (48, 8)
HORIZ = 0.15
VERT = 0.1
DRAG = 0.1
RELAX = 0.5
IMPL = 0.8
VMEM_LIMIT = 20 * 1024 * 1024


def solve_matrix():
    n = np.full(LEV, 2.0)
    n[0] = n[-1] = 1.0
    a = np.diag(1.0 + IMPL * n)
    a -= IMPL * (np.eye(LEV, k=1) + np.eye(LEV, k=-1))
    return np.linalg.inv(a)


def padded_transpose(m):
    out = np.zeros((W, W))
    out[:LEV, :LEV] = m.T
    return out


def split3(m):
    m = np.asarray(m, np.float64)
    parts = []
    for _ in range(3):
        part = m.astype(jnp.bfloat16)
        parts.append(part)
        m = m - part.astype(np.float64)
    return parts


def constants():
    s = solve_matrix()
    power = [np.linalg.matrix_power(s, k) for k in range(STEPS + 1)]
    keep = 1.0 - RELAX
    inner = power[STEPS].T
    bound = power[STEPS].T * keep**STEPS
    send = np.zeros((2, W, 2, W))
    send[0, :LEV, 0, :SPLIT] = bound[:, :SPLIT]
    send[0, :LEV, 1, SPLIT:LEV] = bound[:, SPLIT:]
    send[1, :LEV, 0, L_INNER:] = inner[:, :SPLIT]
    send[1, :LEV, 1, L_INNER:] = inner[:, SPLIT : 2 * SPLIT]
    send[1, :LEV, 1, L_TOP] = inner[:, 2 * SPLIT]
    for part in range(2):
        for owner in range(2):
            for k in range(STEPS):
                send[part, LEV + k, owner, L_DEST[owner] + part * STEPS + k] = 1.0
    send = send.reshape(2 * W, 2 * W).astype(np.float32)
    mix = [
        padded_transpose(power[STEPS - k] * RELAX * keep ** (STEPS - 1 - k))
        for k in range(STEPS)
    ]
    edge = np.stack(
        [
            np.concatenate(split3(np.concatenate(mix[:2])), axis=1),
            np.concatenate(split3(np.concatenate(mix[2:])), axis=1),
        ]
    )
    return send, edge


def call(body, out_shape, in_specs=None, scratch=(), name=None, flops=0, nbytes=0):
    kwargs = {} if in_specs is None else {"in_specs": in_specs}
    return pl.pallas_call(
        body,
        out_shape=out_shape,
        scratch_shapes=list(scratch),
        compiler_params=pltpu.CompilerParams(vmem_limit_bytes=VMEM_LIMIT),
        cost_estimate=pl.CostEstimate(
            flops=flops, bytes_accessed=nbytes, transcendentals=0
        ),
        name=name,
        **kwargs,
    )


VM = pl.BlockSpec(memory_space=pltpu.VMEM)
HB = pl.BlockSpec(memory_space=pltpu.HBM)
SM = pl.BlockSpec(memory_space=pltpu.SMEM)


def start_all(pairs, sems):
    copies = [pltpu.make_async_copy(x, y, sems.at[i]) for i, (x, y) in enumerate(pairs)]
    for copy in copies:
        copy.start()
    return copies


def halo_kernel(parent_hbm, terrain_hbm, down_ref, up_ref, parent_ref, terrain_ref, sems):
    copies = start_all([(parent_hbm, parent_ref), (terrain_hbm, terrain_ref)], sems)
    for copy in copies:
        copy.wait()
    damping = DRAG * terrain_ref[...].astype(F32) / 3000.0
    down_ref[: 2 * LEV, :, :] = parent_ref[:, 4:, :]
    up_ref[: 2 * LEV, :, :] = parent_ref[:, :4, :]
    down_ref[2 * LEV, :, :] = damping[4:, :]
    up_ref[2 * LEV, :, :] = damping[:4, :]


def send_kernel(
    shift_hbm, nest_hbm, bidx_hbm, dest_hbm, mix_hbm,
    msg_ref,
    shift_ref, nest_ref, bidx_ref, dest_ref, mix_ref, pad_ref, sems,
):
    copies = start_all(
        [
            (nest_hbm, nest_ref),
            (bidx_hbm, bidx_ref),
            (dest_hbm, dest_ref),
            (shift_hbm, shift_ref),
            (mix_hbm, mix_ref),
        ],
        sems,
    )
    for copy in copies:
        copy.wait()
    zeros = jnp.zeros((W - LEV + 1, W), F32)
    for b in range(2):
        for part in range(2):
            top = part * W
            pad_ref[b, top + LEV - 1 : top + W, :] = zeros
            pad_ref[b, top : top + LEV, :] = nest_ref[:, part, b, :]
            pad_ref[b, top + LEV : top + LEV + STEPS, :] = dest_ref[
                :, part * W : (part + 1) * W
            ].astype(F32)
        res = lax.dot_general(
            pad_ref[b],
            mix_ref[...],
            (((0,), (0,)), ((), ())),
            precision=lax.Precision.HIGHEST,
            preferred_element_type=F32,
        )
        for owner in range(2):
            start = b * 2 * W + owner * W
            msg_ref[start : start + W, :] = res[:, owner * W : (owner + 1) * W]
    lane = lax.broadcasted_iota(jnp.int32, (NT, W), 1)
    tile = lax.broadcasted_iota(jnp.int32, (NT, W), 0)
    for s in range(STEPS):
        idx = bidx_ref[s : s + 1, :]
        owner = jnp.right_shift(idx, 10)
        row = jnp.bitwise_and(jnp.right_shift(idx, 7), ROWS - 1)
        col = jnp.bitwise_and(jnp.bitwise_and(idx, W - 1) + shift_ref[s], W - 1)
        cell = (row * W + col + 1).astype(F32)
        mine = tile == owner
        picked = jnp.where(mine, jnp.broadcast_to(cell, (NT, W)), 0.0)
        even = jnp.bitwise_and(lane, 1) == 0
        first = jnp.sum(jnp.where(even, picked, 0.0), axis=1, keepdims=True) - 1.0
        second = jnp.sum(jnp.where(even, 0.0, picked), axis=1, keepdims=True) - 1.0
        rows = msg_ref[pl.ds(s, NT, stride=4), :]
        rows = jnp.where(lane == L_REQ, first, rows)
        rows = jnp.where(lane == L_REQ + 1, second, rows)
        msg_ref[pl.ds(s, NT, stride=4), :] = rows


def ring_step(read, write, level_stride, coef, own_only=False):
    row = lax.broadcasted_iota(jnp.int32, (ROWS, W), 0)
    last = row == ROWS - 1
    head = row == 0
    c0, c1, h1, v1 = coef
    chunk = 9

    def body(step, carry):
        for member in range(2):
            for k in range(chunk):
                level = step * chunk + k
                base = member * level_stride
                below = base + jnp.maximum(level - 1, 0)
                above = base + jnp.minimum(level + 1, LEV - 1)
                x0, x1 = read(base + level)
                d0, d1 = read(below)
                u0, u1 = read(above)
                f0 = pltpu.roll(x0, ROWS - 1, 0)
                f1 = pltpu.roll(x1, ROWS - 1, 0)
                g0 = pltpu.roll(x0, 1, 0)
                g1 = pltpu.roll(x1, 1, 0)
                near0 = jnp.where(last, f1, f0) + jnp.where(head, g1, g0)
                near0 = near0 + (pltpu.roll(x0, 1, 1) + pltpu.roll(x0, W - 1, 1))
                y0 = c0 * x0 + HORIZ * near0 + VERT * (d0 + u0)
                if own_only:
                    write(member, level, y0, None)
                    continue
                near1 = jnp.where(last, f0, f1) + jnp.where(head, g0, g1)
                near1 = near1 + (pltpu.roll(x1, 1, 1) + pltpu.roll(x1, W - 1, 1))
                y1 = c1 * x1 + h1 * near1 + v1 * (d1 + u1)
                write(member, level, y0, y1)
        return carry

    lax.fori_loop(0, LEV // chunk, body, 0)


def parent_kernel(
    tile_ref, parent_hbm, next_hbm, prev_hbm, terrain_hbm,
    cells_ref, ring_ref,
    parent_ref, terrain_ref, next_ref, prev_ref, a_ref, b_ref, sems,
):
    tile = tile_ref[0]
    copies = start_all(
        [
            (parent_hbm, parent_ref),
            (terrain_hbm, terrain_ref),
            (next_hbm, next_ref),
            (prev_hbm, prev_ref),
        ],
        sems,
    )
    for copy in copies[1:]:
        copy.wait()
    damping = DRAG * terrain_ref[...].astype(F32) / 3000.0
    pads = jnp.zeros(((LPAD - LEV) * RING, W), F32)
    for ref in (a_ref, b_ref):
        for member in range(2):
            top = member * BSTR + LEV * RING
            ref[top : top + (LPAD - LEV) * RING, :] = pads
    for s in range(STEPS):
        for member in range(2):
            cells_ref[s, member * W + LPAD : (member + 1) * W, :] = jnp.zeros(
                (W - LPAD, ROWS * W), BF16
            )

    copies[0].wait()

    def fill(level, carry):
        for member in range(2):
            src = member * LEV + level
            base = pl.multiple_of(member * BSTR + level * RING, RING)
            a_ref[pl.ds(base, ROWS), :] = parent_ref[src]
            a_ref[pl.ds(base + 8, 4), :] = next_ref[src]
            a_ref[pl.ds(base + 12, 4), :] = prev_ref[src]
        return carry

    lax.fori_loop(0, LEV, fill, 0)
    b_ref[0:4, :] = next_ref[2 * LEV]
    b_ref[4:8, :] = prev_ref[2 * LEV]
    row = lax.broadcasted_iota(jnp.int32, (ROWS, W), 0)
    south = jnp.where(tile < NT - 1, 1.0, 0.0).astype(F32)
    north = jnp.where(tile > 0, 1.0, 0.0).astype(F32)
    valid = jnp.where(row < 4, south, north)
    stay = 1.0 - 4.0 * HORIZ - 2.0 * VERT
    coef = (stay - damping, (stay - b_ref[0:8, :]) * valid, HORIZ * valid, VERT * valid)

    def emit(s, ref):
        for member in range(2):
            for y in range(ROWS):
                rows = ref[pl.ds(member * BSTR + y, LPAD, stride=RING), :]
                cells_ref[s, member * W : member * W + LPAD, y * W : (y + 1) * W] = (
                    rows.astype(BF16)
                )

    emit(0, a_ref)
    src, dst = a_ref, b_ref
    for s in range(1, STEPS):

        def read(index, src=src):
            base = pl.multiple_of(index * RING, RING)
            return src[pl.ds(base, ROWS), :], src[pl.ds(base + ROWS, ROWS), :]

        def write(member, level, y0, y1, dst=dst):
            base = pl.multiple_of((member * LPAD + level) * RING, RING)
            dst[pl.ds(base, ROWS), :] = y0
            dst[pl.ds(base + ROWS, ROWS), :] = y1

        ring_step(read, write, LPAD, coef)
        emit(s, dst)
        src, dst = dst, src

    def drain(level, carry):
        for member in range(2):
            base = pl.multiple_of((member * LPAD + level) * RING, RING)
            ring_ref[member * LEV + level] = src[pl.ds(base, RING), :]
        return carry

    lax.fori_loop(0, LEV, drain, 0)


def last_parent_kernel(ring_ref, terrain_ref, out_ref):
    damping = DRAG * terrain_ref[...].astype(F32) / 3000.0
    stay = 1.0 - 4.0 * HORIZ - 2.0 * VERT

    def read(index):
        return ring_ref[index, 0:ROWS, :], ring_ref[index, ROWS:RING, :]

    def write(member, level, y0, y1):
        out_ref[member * LEV + level] = y0

    ring_step(read, write, LEV, (stay - damping, None, None, None), own_only=True)


def gather_kernel(got_ref, cells_ref, out_ref, scr_ref):
    lane = lax.broadcasted_iota(jnp.int32, (NT, ROWS * W), 1).astype(F32)
    for s in range(STEPS):
        rows = got_ref[pl.ds(s, NT, stride=4), :]
        hot = [
            jnp.where(lane == rows[:, L_REQ + c : L_REQ + c + 1], 1.0, 0.0).astype(BF16)
            for c in range(2)
        ]
        hot = jnp.concatenate(hot, axis=0)
        res = lax.dot_general(
            hot, cells_ref[s], (((1,), (1,)), ((), ())), preferred_element_type=F32
        )
        for b in range(2):
            for c in range(2):
                scr_ref[pl.ds(b * 8 + s * 2 + c, NT, stride=16), :] = res[
                    c * W : (c + 1) * W, b * W : (b + 1) * W
                ]
    out_ref[...] = scr_ref[...].astype(BF16)


def regroup_kernel(bperm_ref, got_ref, out_ref, scr_ref, scr2_ref):
    scr_ref[...] = got_ref[...].astype(F32)
    sub = lax.broadcasted_iota(jnp.int32, (2 * NT, W), 0)
    lane = lax.broadcasted_iota(jnp.int32, (2 * NT, W), 1)
    parity = jnp.bitwise_and(jnp.right_shift(lane, 5), 1)
    target = sub - parity * NT
    for s in range(STEPS):
        owner = jnp.right_shift(bperm_ref[s : s + 1, :], 10)
        hot = jnp.where(target == owner, 1.0, 0.0).astype(BF16)
        values = jnp.concatenate(
            [
                jnp.concatenate(
                    [
                        scr_ref[pl.ds(b * 8 + s * 2 + c, NT, stride=16), :]
                        for b in range(2)
                    ],
                    axis=1,
                )
                for c in range(2)
            ],
            axis=0,
        ).astype(BF16)
        res = lax.dot_general(
            hot, values, (((0,), (0,)), ((), ())), preferred_element_type=F32
        )
        for b in range(2):
            for j in range(4):
                start = (b * 64 + (s // 2) * 32) * 8 + (s % 2) * 4 + j
                scr2_ref[pl.ds(start, 32, stride=8), :] = res[
                    j * 32 : (j + 1) * 32, b * W : (b + 1) * W
                ]
    out_ref[...] = scr2_ref[...].astype(BF16)


def plan_kernel(tile_ref, got_ref, hot_ref, base_ref):
    late = jnp.bitwise_and(jnp.right_shift(tile_ref[0], 5), 1) == 1
    n = 4 * NT
    turned = [got_ref[pl.ds(j, NT, stride=4), :].T for j in range(4)]
    sub = lax.broadcasted_iota(jnp.int32, (n, n), 0)

    def pick(early_value, late_value):
        return jnp.where(late, late_value, early_value)

    def one_hot(row):
        return jnp.where(sub == row, 1.0, 0.0).astype(BF16)

    def dest(part, s):
        k = part * STEPS + s
        row = jnp.concatenate(
            [
                pick(
                    t[L_DEST[0] + k : L_DEST[0] + k + 1, :],
                    t[L_DEST[1] + k : L_DEST[1] + k + 1, :],
                )
                for t in turned
            ],
            axis=1,
        )
        row = (row + 0.5).astype(jnp.int32)
        return jnp.right_shift(row, 8), jnp.bitwise_and(row, 3)

    def finals(part):
        tile_to, slot_to = dest(part, STEPS - 1)
        rows = {STEPS - 1: tile_to * 4 + slot_to}
        for s in range(STEPS - 2, -1, -1):
            mid_tile, mid_slot = dest(part, s)
            move = one_hot(mid_slot * NT + mid_tile)
            later = jnp.concatenate(
                [
                    jnp.broadcast_to(tile_to, (8, n)),
                    jnp.broadcast_to(slot_to, (8, n)),
                ],
                axis=0,
            )
            both = jnp.dot(
                later.astype(F32).astype(BF16), move, preferred_element_type=F32
            )
            tile_to = both[0:1, :].astype(jnp.int32)
            slot_to = both[8:9, :].astype(jnp.int32)
            rows[s] = tile_to * 4 + slot_to
        return rows

    columns = jnp.concatenate(
        [got_ref[pl.ds(j, NT, stride=4), :] for j in range(4)], axis=0
    )
    parts = []
    for _ in range(3):
        part = columns.astype(BF16)
        parts.append(part)
        columns = columns - part.astype(F32)
    parts = jnp.concatenate(parts, axis=1)

    def moved(row):
        res = jnp.dot(one_hot(row), parts, preferred_element_type=F32)
        return res[:, :W] + (res[:, W : 2 * W] + res[:, 2 * W :])

    bound = finals(0)
    hot_ref[0] = one_hot(pick(bound[0], bound[2]))
    hot_ref[1] = one_hot(pick(bound[1], bound[3]))
    outer = moved(bound[0])
    inner = moved(finals(1)[0])
    lane = lax.broadcasted_iota(jnp.int32, (n, W), 1)
    low = pick(0, SPLIT)
    high = pick(SPLIT, LEV)
    extra = pick(W, L_TOP)
    is_inner = jnp.logical_or(lane >= L_INNER, lane == extra)
    is_outer = jnp.logical_and(lane >= low, lane < high)
    base_ref[...] = jnp.where(is_outer, outer, jnp.where(is_inner, inner, 0.0))


def owner_kernel(tile_ref, got_ref, hot_ref, base_ref, mix_ref, out_ref, scr_ref):
    late = jnp.bitwise_and(jnp.right_shift(tile_ref[0], 5), 1)
    scr_ref[...] = got_ref[...].astype(F32)
    moved = []
    for s in range(2):
        edge = jnp.concatenate(
            [scr_ref[pl.ds(s * 4 + j, NT, stride=8), :] for j in range(4)], axis=0
        ).astype(BF16)
        moved.append(jnp.dot(hot_ref[s], edge, preferred_element_type=F32).astype(BF16))
    total = jnp.dot(
        jnp.concatenate(moved, axis=1), mix_ref[late], preferred_element_type=F32
    )
    out_ref[...] = base_ref[...] + (
        total[:, :W] + (total[:, W : 2 * W] + total[:, 2 * W :])
    )


def nest_kernel(got_ref, out_ref, sum_ref, early_ref, late_ref):
    for b in range(2):
        early = got_ref[b * 2 * W : b * 2 * W + W, :]
        late = got_ref[b * 2 * W + W : (b + 1) * 2 * W, :]
        sum_ref[...] = (early + late).T
        early_ref[...] = early.T
        late_ref[...] = late.T
        out_ref[pl.ds(b, LEV, stride=4), :] = sum_ref[:LEV, :]
        inner = 2 + b
        out_ref[pl.ds(inner, SPLIT, stride=4), :] = early_ref[L_INNER:, :]
        out_ref[pl.ds(inner + 4 * SPLIT, SPLIT, stride=4), :] = late_ref[L_INNER:, :]
        top = inner + 8 * SPLIT
        out_ref[top : top + 1, :] = late_ref[L_TOP : L_TOP + 1, :]


def stats_kernel(own_ref, other_ref, mean_ref, var_ref):
    for half in range(2):
        a0, a1, b0, b1 = (
            ref[pl.ds(half * 2 + b, LEV, stride=4), :]
            for ref in (own_ref, other_ref)
            for b in range(2)
        )
        lanes = slice(half * W, (half + 1) * W)
        mean = ((a0 + a1) + (b0 + b1)) / 4.0
        mean_ref[:, lanes] = mean
        own = (a0 - mean) * (a0 - mean) + (a1 - mean) * (a1 - mean)
        other = (b0 - mean) * (b0 - mean) + (b1 - mean) * (b1 - mean)
        var_ref[:, lanes] = (own + other) / 4.0


def in_hbm(x):
    return pltpu.with_memory_space_constraint(x, pltpu.HBM)


def exchange(x):
    return lax.all_to_all(x, "tile", split_axis=0, concat_axis=0, tiled=True)


def on_device(parent_state, nest_state, terrain, shift_x, boundary_index, reloc_dest):
    q_mix, e_mix = constants()
    q_mix, e_mix = jnp.asarray(q_mix), jnp.asarray(e_mix)
    sds = jax.ShapeDtypeStruct
    tile = lax.axis_index("tile").astype(jnp.int32).reshape(1)
    parent = parent_state.reshape(2 * LEV, ROWS, W)

    nest = nest_state.reshape(2, LEV, 2, W).transpose(1, 2, 0, 3)
    parent, terrain = in_hbm(parent), in_hbm(terrain)
    down, up = call(
        halo_kernel,
        (sds((2 * LEV + 1, 4, W), F32), sds((2 * LEV + 1, 4, W), F32)),
        in_specs=[HB] * 2,
        scratch=[
            pltpu.VMEM((2 * LEV, ROWS, W), F32),
            pltpu.VMEM((ROWS, W), jnp.int32),
            pltpu.SemaphoreType.DMA((2,)),
        ],
        name="halo",
        nbytes=1 << 20,
    )(parent, terrain)
    nest, down, up = lax.optimization_barrier((nest, down, up))
    nest = in_hbm(nest)
    message = call(
        send_kernel,
        sds((4 * NT, W), F32),
        in_specs=[HB] * 5,
        scratch=[
            pltpu.SMEM((STEPS,), jnp.int32),
            pltpu.VMEM((LEV, 2, 2, W), F32),
            pltpu.VMEM((STEPS, NT), jnp.int32),
            pltpu.VMEM((STEPS, 2 * W), jnp.int32),
            pltpu.VMEM((2 * W, 2 * W), F32),
            pltpu.VMEM((2, 2 * W, W), F32),
            pltpu.SemaphoreType.DMA((5,)),
        ],
        name="send",
        nbytes=64 << 20,
    )(
        in_hbm(shift_x),
        nest,
        in_hbm(boundary_index),
        in_hbm(reloc_dest),
        in_hbm(q_mix),
    )
    forward = [(i, i + 1) for i in range(NT - 1)]
    backward = [(i + 1, i) for i in range(NT - 1)]
    from_prev = lax.ppermute(down, "tile", forward)
    from_next = lax.ppermute(up, "tile", backward)
    first = exchange(message.reshape(NT, 4, W)).reshape(4 * NT, W)
    cells, ring = call(
        parent_kernel,
        (
            pltpu.VMEM((STEPS, 2 * W, ROWS * W), BF16),
            pltpu.VMEM((2 * LEV, RING, W), F32),
        ),
        in_specs=[SM, HB, HB, HB, HB],
        scratch=[
            pltpu.VMEM((2 * LEV, ROWS, W), F32),
            pltpu.VMEM((ROWS, W), jnp.int32),
            pltpu.VMEM((2 * LEV + 1, 4, W), F32),
            pltpu.VMEM((2 * LEV + 1, 4, W), F32),
            pltpu.VMEM((2 * BSTR, W), F32),
            pltpu.VMEM((2 * BSTR, W), F32),
            pltpu.SemaphoreType.DMA((4,)),
        ],
        name="parent",
        flops=1 << 40,
        nbytes=1 << 36,
    )(tile, parent, in_hbm(from_next), in_hbm(from_prev), terrain)

    values = call(
        gather_kernel,
        sds((16 * NT, W), BF16),
        scratch=[pltpu.VMEM((16 * NT, W), F32)],
        name="gather",
        flops=1 << 29,
        nbytes=3 << 20,
    )(first, cells)
    second = exchange(values.reshape(NT, 16, W)).reshape(16 * NT, W)

    parent_out = call(
        last_parent_kernel,
        sds((2 * LEV, ROWS, W), F32),
        name="last_parent",
        flops=1 << 22,
        nbytes=2 << 20,
    )(ring, terrain)
    hot, base = call(
        plan_kernel,
        (sds((2, 4 * NT, 4 * NT), BF16), sds((4 * NT, W), F32)),
        in_specs=[SM, VM],
        name="plan",
        flops=1 << 28,
        nbytes=3 << 20,
    )(tile, first)

    second, parent_out = lax.optimization_barrier((second, parent_out))
    bperm = boundary_index.reshape(STEPS, 32, 4).transpose(0, 2, 1).reshape(STEPS, NT)
    edges = call(
        regroup_kernel,
        sds((8 * NT, W), BF16),
        scratch=[pltpu.VMEM((16 * NT, W), F32), pltpu.VMEM((8 * NT, W), F32)],
        name="regroup",
        flops=1 << 26,
        nbytes=1 << 20,
    )(bperm, second)
    third = exchange(edges.reshape(NT, 8, W)).reshape(8 * NT, W)

    columns = call(
        owner_kernel,
        sds((4 * NT, W), F32),
        in_specs=[SM, VM, VM, VM, VM],
        scratch=[pltpu.VMEM((8 * NT, W), F32)],
        name="owner",
        flops=1 << 29,
        nbytes=3 << 20,
    )(tile, third, hot, base, e_mix)
    fourth = exchange(columns.reshape(NT, 4, W)).reshape(4 * NT, W)

    nest_out = call(
        nest_kernel,
        sds((4 * LEV, W), F32),
        scratch=[pltpu.VMEM((W, W), F32)] * 3,
        name="nest",
        nbytes=1 << 19,
    )(fourth)
    other = lax.ppermute(nest_out, "member", [(0, 1), (1, 0)])
    mean, variance = call(
        stats_kernel,
        (sds((LEV, 2 * W), F32), sds((LEV, 2 * W), F32)),
        name="stats",
        nbytes=1 << 19,
    )(nest_out, other)
    nest_out = nest_out.reshape(LEV, 2, 2, W).transpose(2, 0, 1, 3)
    nest_out = nest_out.reshape(nest_state.shape)
    return (parent_out.reshape(parent_state.shape), nest_out, mean, variance)


def solution(mesh):
    in_specs = (
        P("member", None, "tile", None),
        P("member", None, "tile"),
        P("tile", None),
        P(),
        P(None, "tile"),
        P(None, "tile"),
    )
    out_specs = (
        P("member", None, "tile", None),
        P("member", None, "tile"),
        P(None, "tile"),
        P(None, "tile"),
    )
    return jax.shard_map(
        on_device, mesh=mesh, in_specs=in_specs, out_specs=out_specs, check_vma=False
    )
```

```python
import functools

import jax
import jax.numpy as jnp
import numpy as np
from jax import lax
from jax.experimental import pallas as pl
from jax.experimental.pallas import tpu as pltpu
from jax.sharding import PartitionSpec as P

F32 = jnp.float32
BF16 = jnp.bfloat16
LEV = 81
STEPS = 4
NT = 128
ROWS = 8
W = 128
LPAD = 96
RING = 16
BSTR = LPAD * RING
SENT = 6
FLAT = 2 * LEV * ROWS
HALO_ROWS = 992
DIST = ((0, 1), (2, 3), (4, None), (5, None))
SPLIT = 40
L_TOP = 81
L_REQ = 86
L_INNER = 88
L_DEST = (48, 8)
HORIZ = 0.15
VERT = 0.1
DRAG = 0.1
RELAX = 0.5
IMPL = 0.8
VMEM_LIMIT = 20 * 1024 * 1024


def solve_matrix():
    n = np.full(LEV, 2.0)
    n[0] = n[-1] = 1.0
    a = np.diag(1.0 + IMPL * n)
    a -= IMPL * (np.eye(LEV, k=1) + np.eye(LEV, k=-1))
    return np.linalg.inv(a)


def padded_transpose(m):
    out = np.zeros((W, W))
    out[:LEV, :LEV] = m.T
    return out


def split3(m):
    m = np.asarray(m, np.float64)
    parts = []
    for _ in range(3):
        part = m.astype(jnp.bfloat16)
        parts.append(part)
        m = m - part.astype(np.float64)
    return parts


def constants():
    s = solve_matrix()
    power = [np.linalg.matrix_power(s, k) for k in range(STEPS + 1)]
    keep = 1.0 - RELAX
    inner = power[STEPS].T
    bound = power[STEPS].T * keep**STEPS
    send = np.zeros((2, W, 2, W))
    send[0, :LEV, 0, :SPLIT] = bound[:, :SPLIT]
    send[0, :LEV, 1, SPLIT:LEV] = bound[:, SPLIT:]
    send[1, :LEV, 0, L_INNER:] = inner[:, :SPLIT]
    send[1, :LEV, 1, L_INNER:] = inner[:, SPLIT : 2 * SPLIT]
    send[1, :LEV, 1, L_TOP] = inner[:, 2 * SPLIT]
    for part in range(2):
        for owner in range(2):
            for k in range(STEPS):
                send[part, LEV + k, owner, L_DEST[owner] + part * STEPS + k] = 1.0
    send = send.reshape(2 * W, 2 * W).astype(np.float32)
    mix = [
        padded_transpose(power[STEPS - k] * RELAX * keep ** (STEPS - 1 - k))
        for k in range(STEPS)
    ]
    edge = np.stack(
        [
            np.concatenate(split3(np.concatenate(mix[:2])), axis=1),
            np.concatenate(split3(np.concatenate(mix[2:])), axis=1),
        ]
    )
    return send, edge


def call(
    body, out_shape, in_specs=None, out_specs=None, scratch=(), name=None, flops=0, nbytes=0
):
    kwargs = {} if in_specs is None else {"in_specs": in_specs}
    if out_specs is not None:
        kwargs["out_specs"] = out_specs
    return pl.pallas_call(
        body,
        out_shape=out_shape,
        scratch_shapes=list(scratch),
        compiler_params=pltpu.CompilerParams(vmem_limit_bytes=VMEM_LIMIT),
        cost_estimate=pl.CostEstimate(
            flops=flops, bytes_accessed=nbytes, transcendentals=0
        ),
        name=name,
        **kwargs,
    )


VM = pl.BlockSpec(memory_space=pltpu.VMEM)
HB = pl.BlockSpec(memory_space=pltpu.HBM)
SM = pl.BlockSpec(memory_space=pltpu.SMEM)


def start_all(pairs, sems):
    copies = [pltpu.make_async_copy(x, y, sems.at[i]) for i, (x, y) in enumerate(pairs)]
    for copy in copies:
        copy.start()
    return copies


def halo_kernel(
    tile_ref, parent_hbm, terrain_hbm,
    parent_ref, first_ref, second_ref,
    terrain_ref, down_ref, up_ref, damp_ref, sems,
):
    copies = start_all([(parent_hbm, parent_ref), (terrain_hbm, terrain_ref)], sems)
    for copy in copies:
        copy.wait()
    damp_ref[...] = DRAG * terrain_ref[...].astype(F32) / 3000.0
    for ref, rows in ((down_ref, (7, 6, 5, 4)), (up_ref, (0, 1, 2, 3))):
        ref[HALO_ROWS - 24 :, :] = jnp.zeros((24, W), F32)
        for row, (coarse, fine) in zip(rows, DIST):
            for count, base, value in (
                (2 * LEV, 0, parent_ref[pl.ds(row, 2 * LEV, stride=ROWS), :]),
                (1, 2 * LEV * SENT, damp_ref[row : row + 1, :]),
            ):
                ref[pl.ds(base + coarse, count, stride=SENT), :] = value
                if fine is not None:
                    rest = value - value.astype(BF16).astype(F32)
                    ref[pl.ds(base + fine, count, stride=SENT), :] = rest
    even = jnp.bitwise_and(tile_ref[0], 1) == 0
    down, up = down_ref[...], up_ref[...]
    first_ref[...] = jnp.where(even, down, up).astype(BF16)
    second_ref[...] = jnp.where(even, up, down).astype(BF16)


def send_kernel(
    shift_hbm, nest_hbm, bidx_hbm, dest_hbm, mix_hbm,
    msg_ref,
    shift_ref, nest_ref, bidx_ref, dest_ref, mix_ref, pad_ref, sems,
):
    copies = start_all(
        [
            (nest_hbm, nest_ref),
            (bidx_hbm, bidx_ref),
            (dest_hbm, dest_ref),
            (shift_hbm, shift_ref),
            (mix_hbm, mix_ref),
        ],
        sems,
    )
    for copy in copies:
        copy.wait()
    zeros = jnp.zeros((W - LEV + 1, W), F32)
    for b in range(2):
        for part in range(2):
            top = part * W
            pad_ref[b, top + LEV - 1 : top + W, :] = zeros
            pad_ref[b, top : top + LEV, :] = nest_ref[:, part, b, :]
            pad_ref[b, top + LEV : top + LEV + STEPS, :] = dest_ref[
                :, part * W : (part + 1) * W
            ].astype(F32)
        res = lax.dot_general(
            pad_ref[b],
            mix_ref[...],
            (((0,), (0,)), ((), ())),
            precision=lax.Precision.HIGHEST,
            preferred_element_type=F32,
        )
        for owner in range(2):
            start = b * 2 * W + owner * W
            msg_ref[start : start + W, :] = res[:, owner * W : (owner + 1) * W]
    lane = lax.broadcasted_iota(jnp.int32, (NT, W), 1)
    tile = lax.broadcasted_iota(jnp.int32, (NT, W), 0)
    for s in range(STEPS):
        idx = bidx_ref[s : s + 1, :]
        owner = jnp.right_shift(idx, 10)
        row = jnp.bitwise_and(jnp.right_shift(idx, 7), ROWS - 1)
        col = jnp.bitwise_and(jnp.bitwise_and(idx, W - 1) + shift_ref[s], W - 1)
        cell = (row * W + col + 1).astype(F32)
        mine = tile == owner
        picked = jnp.where(mine, jnp.broadcast_to(cell, (NT, W)), 0.0)
        even = jnp.bitwise_and(lane, 1) == 0
        first = jnp.sum(jnp.where(even, picked, 0.0), axis=1, keepdims=True) - 1.0
        second = jnp.sum(jnp.where(even, 0.0, picked), axis=1, keepdims=True) - 1.0
        rows = msg_ref[pl.ds(s, NT, stride=4), :]
        rows = jnp.where(lane == L_REQ, first, rows)
        rows = jnp.where(lane == L_REQ + 1, second, rows)
        msg_ref[pl.ds(s, NT, stride=4), :] = rows


def ring_step(read, write, level_stride, coef, own_only=False):
    row = lax.broadcasted_iota(jnp.int32, (ROWS, W), 0)
    last = row == ROWS - 1
    head = row == 0
    c0, c1, h1, v1 = coef
    chunk = 9

    def body(step, carry):
        for member in range(2):
            for k in range(chunk):
                level = step * chunk + k
                base = member * level_stride
                below = base + jnp.maximum(level - 1, 0)
                above = base + jnp.minimum(level + 1, LEV - 1)
                x0, x1 = read(base + level)
                d0, d1 = read(below)
                u0, u1 = read(above)
                f0 = pltpu.roll(x0, ROWS - 1, 0)
                f1 = pltpu.roll(x1, ROWS - 1, 0)
                g0 = pltpu.roll(x0, 1, 0)
                g1 = pltpu.roll(x1, 1, 0)
                near0 = jnp.where(last, f1, f0) + jnp.where(head, g1, g0)
                near0 = near0 + (pltpu.roll(x0, 1, 1) + pltpu.roll(x0, W - 1, 1))
                y0 = c0 * x0 + HORIZ * near0 + VERT * (d0 + u0)
                if own_only:
                    write(member, level, y0, None)
                    continue
                near1 = jnp.where(last, f0, f1) + jnp.where(head, g0, g1)
                near1 = near1 + (pltpu.roll(x1, 1, 1) + pltpu.roll(x1, W - 1, 1))
                y1 = c1 * x1 + h1 * near1 + v1 * (d1 + u1)
                write(member, level, y0, y1)
        return carry

    lax.fori_loop(0, LEV // chunk, body, 0)


def parent_kernel(
    tile_ref, parent_ref, first_ref, second_ref, terrain_hbm,
    cells_ref, ring_hbm,
    next_ref, prev_ref, halo_ref, damp_ref, a_ref, b_ref, ring_ref, terrain_ref, sems,
):
    copies = start_all([(terrain_hbm, terrain_ref)], sems)
    store = pltpu.make_async_copy(ring_ref, ring_hbm, sems.at[1])
    tile = tile_ref[0]
    even = jnp.bitwise_and(tile, 1) == 0
    first, second = first_ref[...].astype(F32), second_ref[...].astype(F32)
    next_ref[...] = jnp.where(even, first, second)
    prev_ref[...] = jnp.where(even, second, first)
    for ref, rows in ((next_ref, (0, 1, 2, 3)), (prev_ref, (7, 6, 5, 4))):
        for row, (coarse, fine) in zip(rows, DIST):
            for count, base, out in ((2 * LEV, 0, halo_ref), (1, 2 * LEV * SENT, damp_ref)):
                value = ref[pl.ds(base + coarse, count, stride=SENT), :]
                if fine is not None:
                    value = value + ref[pl.ds(base + fine, count, stride=SENT), :]
                out[pl.ds(row, count, stride=ROWS), :] = value
    copies[0].wait()
    damping = DRAG * terrain_ref[...].astype(F32) / 3000.0
    pads = jnp.zeros(((LPAD - LEV) * RING, W), F32)
    for ref in (a_ref, b_ref, ring_ref):
        for member in range(2):
            top = member * BSTR + LEV * RING
            ref[top : top + (LPAD - LEV) * RING, :] = pads
    for s in range(STEPS):
        for member in range(2):
            start = LPAD if s else LEV - 1
            cells_ref[s, member * W + start : (member + 1) * W, :] = jnp.zeros(
                (W - start, ROWS * W), BF16
            )
    row = lax.broadcasted_iota(jnp.int32, (ROWS, W), 0)
    south = jnp.where(tile < NT - 1, 1.0, 0.0).astype(F32)
    north = jnp.where(tile > 0, 1.0, 0.0).astype(F32)
    valid = jnp.where(row < 4, south, north)
    stay = 1.0 - 4.0 * HORIZ - 2.0 * VERT
    coef = (stay - damping, (stay - damp_ref[...]) * valid, HORIZ * valid, VERT * valid)

    def emit(s, ref, count, stride):
        for member in range(2):
            for y in range(ROWS):
                start = member * count * stride + y
                rows = ref[pl.ds(start, count, stride=stride), :]
                cells_ref[s, member * W : member * W + count, y * W : (y + 1) * W] = (
                    rows.astype(BF16)
                )

    def read_first(index):
        base = pl.multiple_of(index * ROWS, ROWS)
        return parent_ref[pl.ds(base, ROWS), :], halo_ref[pl.ds(base, ROWS), :]

    emit(0, parent_ref, LEV, ROWS)
    read, stride = read_first, LEV
    for s, dst in zip(range(1, STEPS), (a_ref, b_ref, ring_ref)):

        def write(member, level, y0, y1, dst=dst):
            base = pl.multiple_of((member * LPAD + level) * RING, RING)
            dst[pl.ds(base, ROWS), :] = y0
            dst[pl.ds(base + ROWS, ROWS), :] = y1

        ring_step(read, write, stride, coef)
        if s == STEPS - 1:
            store.start()
        emit(s, dst, LPAD, RING)

        def read(index, src=dst):
            base = pl.multiple_of(index * RING, RING)
            return src[pl.ds(base, ROWS), :], src[pl.ds(base + ROWS, ROWS), :]

        stride = LPAD
    store.wait()


def last_parent_kernel(ring_hbm, terrain_hbm, out_ref, ring_ref, terrain_ref, sems):
    for copy in start_all([(ring_hbm, ring_ref), (terrain_hbm, terrain_ref)], sems):
        copy.wait()
    damping = DRAG * terrain_ref[...].astype(F32) / 3000.0
    stay = 1.0 - 4.0 * HORIZ - 2.0 * VERT

    def read(index):
        base = pl.multiple_of(index * RING, RING)
        return ring_ref[pl.ds(base, ROWS), :], ring_ref[pl.ds(base + ROWS, ROWS), :]

    def write(member, level, y0, y1):
        out_ref[member * LEV + level] = y0

    ring_step(read, write, LPAD, (stay - damping, None, None, None), own_only=True)


def gather_kernel(got_ref, cells_ref, out_ref, scr_ref):
    lane = lax.broadcasted_iota(jnp.int32, (NT, ROWS * W), 1).astype(F32)
    for s in range(STEPS):
        rows = got_ref[pl.ds(s, NT, stride=4), :]
        hot = [
            jnp.where(lane == rows[:, L_REQ + c : L_REQ + c + 1], 1.0, 0.0).astype(BF16)
            for c in range(2)
        ]
        hot = jnp.concatenate(hot, axis=0)
        res = lax.dot_general(
            hot, cells_ref[s], (((1,), (1,)), ((), ())), preferred_element_type=F32
        )
        for b in range(2):
            for c in range(2):
                scr_ref[pl.ds(b * 8 + s * 2 + c, NT, stride=16), :] = res[
                    c * W : (c + 1) * W, b * W : (b + 1) * W
                ]
    out_ref[...] = scr_ref[...].astype(BF16)


def regroup_kernel(bperm_ref, got_ref, out_ref, scr_ref, scr2_ref):
    scr_ref[...] = got_ref[...].astype(F32)
    sub = lax.broadcasted_iota(jnp.int32, (2 * NT, W), 0)
    lane = lax.broadcasted_iota(jnp.int32, (2 * NT, W), 1)
    parity = jnp.bitwise_and(jnp.right_shift(lane, 5), 1)
    target = sub - parity * NT
    for s in range(STEPS):
        owner = jnp.right_shift(bperm_ref[s : s + 1, :], 10)
        hot = jnp.where(target == owner, 1.0, 0.0).astype(BF16)
        values = jnp.concatenate(
            [
                jnp.concatenate(
                    [
                        scr_ref[pl.ds(b * 8 + s * 2 + c, NT, stride=16), :]
                        for b in range(2)
                    ],
                    axis=1,
                )
                for c in range(2)
            ],
            axis=0,
        ).astype(BF16)
        res = lax.dot_general(
            hot, values, (((0,), (0,)), ((), ())), preferred_element_type=F32
        )
        for b in range(2):
            for j in range(4):
                start = (b * 64 + (s // 2) * 32) * 8 + (s % 2) * 4 + j
                scr2_ref[pl.ds(start, 32, stride=8), :] = res[
                    j * 32 : (j + 1) * 32, b * W : (b + 1) * W
                ]
    out_ref[...] = scr2_ref[...].astype(BF16)


def plan_kernel(tile_ref, got_ref, hot_ref, base_ref):
    late = jnp.bitwise_and(jnp.right_shift(tile_ref[0], 5), 1) == 1
    n = 4 * NT
    turned = [got_ref[pl.ds(j, NT, stride=4), :].T for j in range(4)]
    sub = lax.broadcasted_iota(jnp.int32, (n, n), 0)

    def pick(early_value, late_value):
        return jnp.where(late, late_value, early_value)

    def one_hot(row):
        return jnp.where(sub == row, 1.0, 0.0).astype(BF16)

    def dest(part, s):
        k = part * STEPS + s
        row = jnp.concatenate(
            [
                pick(
                    t[L_DEST[0] + k : L_DEST[0] + k + 1, :],
                    t[L_DEST[1] + k : L_DEST[1] + k + 1, :],
                )
                for t in turned
            ],
            axis=1,
        )
        row = (row + 0.5).astype(jnp.int32)
        return jnp.right_shift(row, 8), jnp.bitwise_and(row, 3)

    def finals(part):
        tile_to, slot_to = dest(part, STEPS - 1)
        rows = {STEPS - 1: tile_to * 4 + slot_to}
        for s in range(STEPS - 2, -1, -1):
            mid_tile, mid_slot = dest(part, s)
            move = one_hot(mid_slot * NT + mid_tile)
            later = jnp.concatenate(
                [
                    jnp.broadcast_to(tile_to, (8, n)),
                    jnp.broadcast_to(slot_to, (8, n)),
                ],
                axis=0,
            )
            both = jnp.dot(
                later.astype(F32).astype(BF16), move, preferred_element_type=F32
            )
            tile_to = both[0:1, :].astype(jnp.int32)
            slot_to = both[8:9, :].astype(jnp.int32)
            rows[s] = tile_to * 4 + slot_to
        return rows

    columns = jnp.concatenate(
        [got_ref[pl.ds(j, NT, stride=4), :] for j in range(4)], axis=0
    )
    parts = []
    for _ in range(3):
        part = columns.astype(BF16)
        parts.append(part)
        columns = columns - part.astype(F32)
    parts = jnp.concatenate(parts, axis=1)

    def moved(row):
        res = jnp.dot(one_hot(row), parts, preferred_element_type=F32)
        return res[:, :W] + (res[:, W : 2 * W] + res[:, 2 * W :])

    bound = finals(0)
    hot_ref[0] = one_hot(pick(bound[0], bound[2]))
    hot_ref[1] = one_hot(pick(bound[1], bound[3]))
    outer = moved(bound[0])
    inner = moved(finals(1)[0])
    lane = lax.broadcasted_iota(jnp.int32, (n, W), 1)
    low = pick(0, SPLIT)
    high = pick(SPLIT, LEV)
    extra = pick(W, L_TOP)
    is_inner = jnp.logical_or(lane >= L_INNER, lane == extra)
    is_outer = jnp.logical_and(lane >= low, lane < high)
    base_ref[...] = jnp.where(is_outer, outer, jnp.where(is_inner, inner, 0.0))


def owner_kernel(tile_ref, got_ref, hot_ref, base_ref, mix_ref, out_ref, scr_ref):
    late = jnp.bitwise_and(jnp.right_shift(tile_ref[0], 5), 1)
    scr_ref[...] = got_ref[...].astype(F32)
    moved = []
    for s in range(2):
        edge = jnp.concatenate(
            [scr_ref[pl.ds(s * 4 + j, NT, stride=8), :] for j in range(4)], axis=0
        ).astype(BF16)
        moved.append(jnp.dot(hot_ref[s], edge, preferred_element_type=F32).astype(BF16))
    total = jnp.dot(
        jnp.concatenate(moved, axis=1), mix_ref[late], preferred_element_type=F32
    )
    out_ref[...] = base_ref[...] + (
        total[:, :W] + (total[:, W : 2 * W] + total[:, 2 * W :])
    )


def nest_kernel(got_ref, out_ref, sum_ref, early_ref, late_ref):
    for b in range(2):
        early = got_ref[b * 2 * W : b * 2 * W + W, :]
        late = got_ref[b * 2 * W + W : (b + 1) * 2 * W, :]
        sum_ref[...] = (early + late).T
        early_ref[...] = early.T
        late_ref[...] = late.T
        out_ref[pl.ds(b, LEV, stride=4), :] = sum_ref[:LEV, :]
        inner = 2 + b
        out_ref[pl.ds(inner, SPLIT, stride=4), :] = early_ref[L_INNER:, :]
        out_ref[pl.ds(inner + 4 * SPLIT, SPLIT, stride=4), :] = late_ref[L_INNER:, :]
        top = inner + 8 * SPLIT
        out_ref[top : top + 1, :] = late_ref[L_TOP : L_TOP + 1, :]


def stats_kernel(own_ref, other_ref, mean_ref, var_ref):
    for half in range(2):
        a0, a1, b0, b1 = (
            ref[pl.ds(half * 2 + b, LEV, stride=4), :]
            for ref in (own_ref, other_ref)
            for b in range(2)
        )
        lanes = slice(half * W, (half + 1) * W)
        mean = ((a0 + a1) + (b0 + b1)) / 4.0
        mean_ref[:, lanes] = mean
        own = (a0 - mean) * (a0 - mean) + (a1 - mean) * (a1 - mean)
        other = (b0 - mean) * (b0 - mean) + (b1 - mean) * (b1 - mean)
        var_ref[:, lanes] = (own + other) / 4.0


def in_hbm(x):
    return pltpu.with_memory_space_constraint(x, pltpu.HBM)


def exchange(x):
    return lax.all_to_all(x, "tile", split_axis=0, concat_axis=0, tiled=True)


def on_device(parent_state, nest_state, terrain, shift_x, boundary_index, reloc_dest):
    q_mix, e_mix = constants()
    q_mix, e_mix = jnp.asarray(q_mix), jnp.asarray(e_mix)
    sds = jax.ShapeDtypeStruct
    tile = lax.axis_index("tile").astype(jnp.int32).reshape(1)
    parent = parent_state.reshape(FLAT, W)

    nest = nest_state.reshape(2, LEV, 2, W).transpose(1, 2, 0, 3)
    kept, down, up = call(
        halo_kernel,
        (
            pltpu.VMEM((FLAT, W), F32),
            sds((HALO_ROWS, W), BF16),
            sds((HALO_ROWS, W), BF16),
        ),
        in_specs=[SM, HB, HB],
        scratch=[
            pltpu.VMEM((ROWS, W), jnp.int32),
            pltpu.VMEM((HALO_ROWS, W), F32),
            pltpu.VMEM((HALO_ROWS, W), F32),
            pltpu.VMEM((ROWS, W), F32),
            pltpu.SemaphoreType.DMA((2,)),
        ],
        name="halo",
        nbytes=1 << 20,
    )(tile, in_hbm(parent), in_hbm(terrain))
    nest, down, up = lax.optimization_barrier((nest, down, up))
    nest = in_hbm(nest)
    message = call(
        send_kernel,
        sds((4 * NT, W), F32),
        in_specs=[HB] * 5,
        scratch=[
            pltpu.SMEM((STEPS,), jnp.int32),
            pltpu.VMEM((LEV, 2, 2, W), F32),
            pltpu.VMEM((STEPS, NT), jnp.int32),
            pltpu.VMEM((STEPS, 2 * W), jnp.int32),
            pltpu.VMEM((2 * W, 2 * W), F32),
            pltpu.VMEM((2, 2 * W, W), F32),
            pltpu.SemaphoreType.DMA((5,)),
        ],
        name="send",
        nbytes=64 << 20,
    )(
        in_hbm(shift_x),
        nest,
        in_hbm(boundary_index),
        in_hbm(reloc_dest),
        in_hbm(q_mix),
    )
    pairs = [(i, i + 1) for i in range(0, NT, 2)] + [(i + 1, i) for i in range(0, NT, 2)]
    gaps = [(i, i + 1) for i in range(1, NT - 1, 2)]
    gaps = gaps + [(i + 1, i) for i in range(1, NT - 1, 2)]
    from_pair = lax.ppermute(down, "tile", pairs)
    from_gap = lax.ppermute(up, "tile", gaps)
    first = exchange(message.reshape(NT, 4, W)).reshape(4 * NT, W)
    cells, ring = call(
        parent_kernel,
        (
            pltpu.VMEM((STEPS, 2 * W, ROWS * W), BF16),
            pltpu.HBM((2 * BSTR, W), F32),
        ),
        in_specs=[SM, VM, VM, VM, HB],
        out_specs=(VM, HB),
        scratch=[
            pltpu.VMEM((HALO_ROWS, W), F32),
            pltpu.VMEM((HALO_ROWS, W), F32),
            pltpu.VMEM((FLAT, W), F32),
            pltpu.VMEM((ROWS, W), F32),
            pltpu.VMEM((2 * BSTR, W), F32),
            pltpu.VMEM((2 * BSTR, W), F32),
            pltpu.VMEM((2 * BSTR, W), F32),
            pltpu.VMEM((ROWS, W), jnp.int32),
            pltpu.SemaphoreType.DMA((2,)),
        ],
        name="parent",
        flops=1 << 40,
        nbytes=1 << 36,
    )(tile, kept, from_pair, from_gap, in_hbm(terrain))

    values = call(
        gather_kernel,
        sds((16 * NT, W), BF16),
        scratch=[pltpu.VMEM((16 * NT, W), F32)],
        name="gather",
        flops=1 << 29,
        nbytes=3 << 20,
    )(first, cells)
    second = exchange(values.reshape(NT, 16, W)).reshape(16 * NT, W)

    parent_out = call(
        last_parent_kernel,
        sds((2 * LEV, ROWS, W), F32),
        in_specs=[HB, HB],
        scratch=[
            pltpu.VMEM((2 * BSTR, W), F32),
            pltpu.VMEM((ROWS, W), jnp.int32),
            pltpu.SemaphoreType.DMA((2,)),
        ],
        name="last_parent",
        flops=1 << 22,
        nbytes=2 << 20,
    )(in_hbm(ring), in_hbm(terrain))
    hot, base = call(
        plan_kernel,
        (sds((2, 4 * NT, 4 * NT), BF16), sds((4 * NT, W), F32)),
        in_specs=[SM, VM],
        name="plan",
        flops=1 << 28,
        nbytes=3 << 20,
    )(tile, first)

    second, parent_out = lax.optimization_barrier((second, parent_out))
    bperm = boundary_index.reshape(STEPS, 32, 4).transpose(0, 2, 1).reshape(STEPS, NT)
    edges = call(
        regroup_kernel,
        sds((8 * NT, W), BF16),
        scratch=[pltpu.VMEM((16 * NT, W), F32), pltpu.VMEM((8 * NT, W), F32)],
        name="regroup",
        flops=1 << 26,
        nbytes=1 << 20,
    )(bperm, second)
    third = exchange(edges.reshape(NT, 8, W)).reshape(8 * NT, W)

    columns = call(
        owner_kernel,
        sds((4 * NT, W), F32),
        in_specs=[SM, VM, VM, VM, VM],
        scratch=[pltpu.VMEM((8 * NT, W), F32)],
        name="owner",
        flops=1 << 29,
        nbytes=3 << 20,
    )(tile, third, hot, base, e_mix)
    fourth = exchange(columns.reshape(NT, 4, W)).reshape(4 * NT, W)

    nest_out = call(
        nest_kernel,
        sds((4 * LEV, W), F32),
        scratch=[pltpu.VMEM((W, W), F32)] * 3,
        name="nest",
        nbytes=1 << 19,
    )(fourth)
    other = lax.ppermute(nest_out, "member", [(0, 1), (1, 0)])
    mean, variance = call(
        stats_kernel,
        (sds((LEV, 2 * W), F32), sds((LEV, 2 * W), F32)),
        name="stats",
        nbytes=1 << 19,
    )(nest_out, other)
    nest_out = nest_out.reshape(LEV, 2, 2, W).transpose(2, 0, 1, 3)
    nest_out = nest_out.reshape(nest_state.shape)
    return (parent_out.reshape(parent_state.shape), nest_out, mean, variance)


def solution(mesh):
    in_specs = (
        P("member", None, "tile", None),
        P("member", None, "tile"),
        P("tile", None),
        P(),
        P(None, "tile"),
        P(None, "tile"),
    )
    out_specs = (
        P("member", None, "tile", None),
        P("member", None, "tile"),
        P(None, "tile"),
        P(None, "tile"),
    )
    return jax.shard_map(
        on_device, mesh=mesh, in_specs=in_specs, out_specs=out_specs, check_vma=False
    )
```

```python
import functools

import jax
import jax.numpy as jnp
import numpy as np
from jax import lax
from jax.experimental import pallas as pl
from jax.experimental.pallas import tpu as pltpu
from jax.sharding import PartitionSpec as P

F32 = jnp.float32
BF16 = jnp.bfloat16
LEV = 81
STEPS = 4
NT = 128
ROWS = 8
W = 128
LPAD = 96
RING = 16
BSTR = LPAD * RING
SENT = 6
FLAT = 2 * LEV * ROWS
HALO_ROWS = 992
DIST = ((0, 1), (2, 3), (4, None), (5, None))
SPLIT = 40
PACK = 12
CUT = W - LEV
L_TOP = 81
L_REQ = 86
L_INNER = 88
L_DEST = (48, 8)
HORIZ = 0.15
VERT = 0.1
DRAG = 0.1
RELAX = 0.5
IMPL = 0.8
VMEM_LIMIT = 20 * 1024 * 1024


def solve_matrix():
    n = np.full(LEV, 2.0)
    n[0] = n[-1] = 1.0
    a = np.diag(1.0 + IMPL * n)
    a -= IMPL * (np.eye(LEV, k=1) + np.eye(LEV, k=-1))
    return np.linalg.inv(a)


def padded_transpose(m):
    out = np.zeros((W, W))
    out[:LEV, :LEV] = m.T
    return out


def split3(m):
    m = np.asarray(m, np.float64)
    parts = []
    for _ in range(3):
        part = m.astype(jnp.bfloat16)
        parts.append(part)
        m = m - part.astype(np.float64)
    return parts


def constants():
    s = solve_matrix()
    power = [np.linalg.matrix_power(s, k) for k in range(STEPS + 1)]
    keep = 1.0 - RELAX
    inner = power[STEPS].T
    bound = power[STEPS].T * keep**STEPS
    send = np.zeros((2, W, 2, W))
    send[0, :LEV, 0, :SPLIT] = bound[:, :SPLIT]
    send[0, :LEV, 1, SPLIT:LEV] = bound[:, SPLIT:]
    send[1, :LEV, 0, L_INNER:] = inner[:, :SPLIT]
    send[1, :LEV, 1, L_INNER:] = inner[:, SPLIT : 2 * SPLIT]
    send[1, :LEV, 1, L_TOP] = inner[:, 2 * SPLIT]
    for part in range(2):
        for owner in range(2):
            for k in range(STEPS):
                send[part, LEV + k, owner, L_DEST[owner] + part * STEPS + k] = 1.0
    send = send.reshape(2 * W, 2 * W).astype(np.float32)
    mix = [
        padded_transpose(power[STEPS - k] * RELAX * keep ** (STEPS - 1 - k))
        for k in range(STEPS)
    ]
    edge = np.stack(
        [
            np.concatenate(split3(np.concatenate(mix[:2])), axis=1),
            np.concatenate(split3(np.concatenate(mix[2:])), axis=1),
        ]
    )
    return send, edge


def call(
    body, out_shape, in_specs=None, out_specs=None, scratch=(), name=None, flops=0, nbytes=0
):
    kwargs = {} if in_specs is None else {"in_specs": in_specs}
    if out_specs is not None:
        kwargs["out_specs"] = out_specs
    return pl.pallas_call(
        body,
        out_shape=out_shape,
        scratch_shapes=list(scratch),
        compiler_params=pltpu.CompilerParams(vmem_limit_bytes=VMEM_LIMIT),
        cost_estimate=pl.CostEstimate(
            flops=flops, bytes_accessed=nbytes, transcendentals=0
        ),
        name=name,
        **kwargs,
    )


VM = pl.BlockSpec(memory_space=pltpu.VMEM)
HB = pl.BlockSpec(memory_space=pltpu.HBM)
SM = pl.BlockSpec(memory_space=pltpu.SMEM)


def start_all(pairs, sems):
    copies = [pltpu.make_async_copy(x, y, sems.at[i]) for i, (x, y) in enumerate(pairs)]
    for copy in copies:
        copy.start()
    return copies


def halo_kernel(
    tile_ref, parent_hbm, terrain_hbm, nest_hbm, bidx_hbm, dest_hbm, mix_hbm,
    parent_ref, first_ref, second_ref, nest_ref, bidx_ref, dest_ref, mix_ref,
    terrain_ref, down_ref, up_ref, damp_ref, sems,
):
    copies = start_all(
        [
            (parent_hbm, parent_ref),
            (terrain_hbm, terrain_ref),
            (nest_hbm, nest_ref),
            (bidx_hbm, bidx_ref),
            (dest_hbm, dest_ref),
            (mix_hbm, mix_ref),
        ],
        sems,
    )
    for copy in copies[:2]:
        copy.wait()
    damp_ref[...] = DRAG * terrain_ref[...].astype(F32) / 3000.0
    for ref, rows in ((down_ref, (7, 6, 5, 4)), (up_ref, (0, 1, 2, 3))):
        ref[HALO_ROWS - 24 :, :] = jnp.zeros((24, W), F32)
        for row, (coarse, fine) in zip(rows, DIST):
            for count, base, value in (
                (2 * LEV, 0, parent_ref[pl.ds(row, 2 * LEV, stride=ROWS), :]),
                (1, 2 * LEV * SENT, damp_ref[row : row + 1, :]),
            ):
                ref[pl.ds(base + coarse, count, stride=SENT), :] = value
                if fine is not None:
                    rest = value - value.astype(BF16).astype(F32)
                    ref[pl.ds(base + fine, count, stride=SENT), :] = rest
    even = jnp.bitwise_and(tile_ref[0], 1) == 0
    down, up = down_ref[...], up_ref[...]
    first_ref[...] = jnp.where(even, down, up).astype(BF16)
    second_ref[...] = jnp.where(even, up, down).astype(BF16)
    for copy in copies[2:]:
        copy.wait()


def send_kernel(
    shift_hbm, nest_ref, bidx_ref, dest_ref, mix_ref,
    msg_ref,
    shift_ref, pad_ref, sems,
):
    copies = start_all([(shift_hbm, shift_ref)], sems)
    zeros = jnp.zeros((W - LEV + 1, W), F32)
    for b in range(2):
        for part in range(2):
            top = part * W
            pad_ref[b, top + LEV - 1 : top + W, :] = zeros
            pad_ref[b, top : top + LEV, :] = nest_ref[:, part, b, :]
            pad_ref[b, top + LEV : top + LEV + STEPS, :] = dest_ref[
                :, part * W : (part + 1) * W
            ].astype(F32)
        res = lax.dot_general(
            pad_ref[b],
            mix_ref[...],
            (((0,), (0,)), ((), ())),
            precision=lax.Precision.HIGHEST,
            preferred_element_type=F32,
        )
        for owner in range(2):
            start = b * 2 * W + owner * W
            msg_ref[start : start + W, :] = res[:, owner * W : (owner + 1) * W]
    copies[0].wait()
    lane = lax.broadcasted_iota(jnp.int32, (NT, W), 1)
    tile = lax.broadcasted_iota(jnp.int32, (NT, W), 0)
    for s in range(STEPS):
        idx = bidx_ref[s : s + 1, :]
        owner = jnp.right_shift(idx, 10)
        row = jnp.bitwise_and(jnp.right_shift(idx, 7), ROWS - 1)
        col = jnp.bitwise_and(jnp.bitwise_and(idx, W - 1) + shift_ref[s], W - 1)
        cell = (row * W + col + 1).astype(F32)
        mine = tile == owner
        picked = jnp.where(mine, jnp.broadcast_to(cell, (NT, W)), 0.0)
        even = jnp.bitwise_and(lane, 1) == 0
        first = jnp.sum(jnp.where(even, picked, 0.0), axis=1, keepdims=True) - 1.0
        second = jnp.sum(jnp.where(even, 0.0, picked), axis=1, keepdims=True) - 1.0
        rows = msg_ref[pl.ds(s, NT, stride=4), :]
        rows = jnp.where(lane == L_REQ, first, rows)
        rows = jnp.where(lane == L_REQ + 1, second, rows)
        msg_ref[pl.ds(s, NT, stride=4), :] = rows


def ring_step(read, write, level_stride, coef, own_only=False):
    row = lax.broadcasted_iota(jnp.int32, (ROWS, W), 0)
    last = row == ROWS - 1
    head = row == 0
    c0, c1, h1, v1 = coef
    chunk = 9

    def body(step, carry):
        for member in range(2):
            for k in range(chunk):
                level = step * chunk + k
                base = member * level_stride
                below = base + jnp.maximum(level - 1, 0)
                above = base + jnp.minimum(level + 1, LEV - 1)
                x0, x1 = read(base + level)
                d0, d1 = read(below)
                u0, u1 = read(above)
                f0 = pltpu.roll(x0, ROWS - 1, 0)
                f1 = pltpu.roll(x1, ROWS - 1, 0)
                g0 = pltpu.roll(x0, 1, 0)
                g1 = pltpu.roll(x1, 1, 0)
                near0 = jnp.where(last, f1, f0) + jnp.where(head, g1, g0)
                near0 = near0 + (pltpu.roll(x0, 1, 1) + pltpu.roll(x0, W - 1, 1))
                y0 = c0 * x0 + HORIZ * near0 + VERT * (d0 + u0)
                if own_only:
                    write(member, level, y0, None)
                    continue
                near1 = jnp.where(last, f0, f1) + jnp.where(head, g0, g1)
                near1 = near1 + (pltpu.roll(x1, 1, 1) + pltpu.roll(x1, W - 1, 1))
                y1 = c1 * x1 + h1 * near1 + v1 * (d1 + u1)
                write(member, level, y0, y1)
        return carry

    lax.fori_loop(0, LEV // chunk, body, 0)


def parent_kernel(
    tile_ref, parent_ref, first_ref, second_ref, terrain_hbm,
    cells_ref, ring_hbm,
    next_ref, prev_ref, halo_ref, damp_ref, a_ref, b_ref, ring_ref, terrain_ref, sems,
):
    copies = start_all([(terrain_hbm, terrain_ref)], sems)
    store = pltpu.make_async_copy(ring_ref, ring_hbm, sems.at[1])
    tile = tile_ref[0]
    even = jnp.bitwise_and(tile, 1) == 0
    first, second = first_ref[...].astype(F32), second_ref[...].astype(F32)
    next_ref[...] = jnp.where(even, first, second)
    prev_ref[...] = jnp.where(even, second, first)
    for ref, rows in ((next_ref, (0, 1, 2, 3)), (prev_ref, (7, 6, 5, 4))):
        for row, (coarse, fine) in zip(rows, DIST):
            for count, base, out in ((2 * LEV, 0, halo_ref), (1, 2 * LEV * SENT, damp_ref)):
                value = ref[pl.ds(base + coarse, count, stride=SENT), :]
                if fine is not None:
                    value = value + ref[pl.ds(base + fine, count, stride=SENT), :]
                out[pl.ds(row, count, stride=ROWS), :] = value
    copies[0].wait()
    damping = DRAG * terrain_ref[...].astype(F32) / 3000.0
    pads = jnp.zeros(((LPAD - LEV) * RING, W), F32)
    for ref in (a_ref, b_ref, ring_ref):
        for member in range(2):
            top = member * BSTR + LEV * RING
            ref[top : top + (LPAD - LEV) * RING, :] = pads
    for s in range(STEPS):
        for member in range(2):
            start = LPAD if s else LEV - 1
            cells_ref[s, member * W + start : (member + 1) * W, :] = jnp.zeros(
                (W - start, ROWS * W), BF16
            )
    row = lax.broadcasted_iota(jnp.int32, (ROWS, W), 0)
    south = jnp.where(tile < NT - 1, 1.0, 0.0).astype(F32)
    north = jnp.where(tile > 0, 1.0, 0.0).astype(F32)
    valid = jnp.where(row < 4, south, north)
    stay = 1.0 - 4.0 * HORIZ - 2.0 * VERT
    coef = (stay - damping, (stay - damp_ref[...]) * valid, HORIZ * valid, VERT * valid)

    def emit(s, ref, count, stride):
        for member in range(2):
            for y in range(ROWS):
                start = member * count * stride + y
                rows = ref[pl.ds(start, count, stride=stride), :]
                cells_ref[s, member * W : member * W + count, y * W : (y + 1) * W] = (
                    rows.astype(BF16)
                )

    def read_first(index):
        base = pl.multiple_of(index * ROWS, ROWS)
        return parent_ref[pl.ds(base, ROWS), :], halo_ref[pl.ds(base, ROWS), :]

    emit(0, parent_ref, LEV, ROWS)
    read, stride = read_first, LEV
    for s, dst in zip(range(1, STEPS), (a_ref, b_ref, ring_ref)):

        def write(member, level, y0, y1, dst=dst):
            base = pl.multiple_of((member * LPAD + level) * RING, RING)
            dst[pl.ds(base, ROWS), :] = y0
            dst[pl.ds(base + ROWS, ROWS), :] = y1

        ring_step(read, write, stride, coef)
        if s == STEPS - 1:
            store.start()
        emit(s, dst, LPAD, RING)

        def read(index, src=dst):
            base = pl.multiple_of(index * RING, RING)
            return src[pl.ds(base, ROWS), :], src[pl.ds(base + ROWS, ROWS), :]

        stride = LPAD
    store.wait()


def last_parent_kernel(ring_hbm, terrain_hbm, out_ref, ring_ref, terrain_ref, sems):
    for copy in start_all([(ring_hbm, ring_ref), (terrain_hbm, terrain_ref)], sems):
        copy.wait()
    damping = DRAG * terrain_ref[...].astype(F32) / 3000.0
    stay = 1.0 - 4.0 * HORIZ - 2.0 * VERT

    def read(index):
        base = pl.multiple_of(index * RING, RING)
        return ring_ref[pl.ds(base, ROWS), :], ring_ref[pl.ds(base + ROWS, ROWS), :]

    def write(member, level, y0, y1):
        out_ref[member * LEV + level] = y0

    ring_step(read, write, LPAD, (stay - damping, None, None, None), own_only=True)


def gather_kernel(got_ref, cells_ref, out_ref, scr_ref):
    cell = lax.broadcasted_iota(jnp.int32, (NT, ROWS * W), 1).astype(F32)
    lane = lax.broadcasted_iota(jnp.int32, (NT, W), 1)
    rows = {}
    for s in range(STEPS):
        asked = got_ref[pl.ds(s, NT, stride=4), :]
        hot = [
            jnp.where(cell == asked[:, L_REQ + c : L_REQ + c + 1], 1.0, 0.0).astype(BF16)
            for c in range(2)
        ]
        hot = jnp.concatenate(hot, axis=0)
        res = lax.dot_general(
            hot, cells_ref[s], (((1,), (1,)), ((), ())), preferred_element_type=F32
        )
        for b in range(2):
            for c in range(2):
                rows[b * 8 + s * 2 + c] = res[c * W : (c + 1) * W, b * W : (b + 1) * W]
    for r in range(PACK):
        row = rows[r]
        if r < 8:
            extra = rows[PACK + r // 2]
            if r % 2 == 0:
                row = row + pltpu.roll(jnp.where(lane < CUT, extra, 0.0), LEV, 1)
            else:
                row = row + pltpu.roll(jnp.where(lane < CUT, 0.0, extra), LEV - CUT, 1)
        scr_ref[pl.ds(r, NT, stride=PACK), :] = row
    out_ref[...] = scr_ref[...].astype(BF16)


def regroup_kernel(bperm_ref, got_ref, out_ref, scr_ref, scr2_ref):
    scr_ref[...] = got_ref[...].astype(F32)
    low = lax.broadcasted_iota(jnp.int32, (NT, W), 1) < CUT

    def row(r):
        if r < PACK:
            return scr_ref[pl.ds(r, NT, stride=PACK), :]
        first = pltpu.roll(row(2 * (r - PACK)), W - LEV, 1)
        second = pltpu.roll(row(2 * (r - PACK) + 1), W - LEV + CUT, 1)
        return jnp.where(low, first, second)

    sub = lax.broadcasted_iota(jnp.int32, (2 * NT, W), 0)
    lane = lax.broadcasted_iota(jnp.int32, (2 * NT, W), 1)
    parity = jnp.bitwise_and(jnp.right_shift(lane, 5), 1)
    target = sub - parity * NT
    for s in range(STEPS):
        owner = jnp.right_shift(bperm_ref[s : s + 1, :], 10)
        hot = jnp.where(target == owner, 1.0, 0.0).astype(BF16)
        values = jnp.concatenate(
            [
                jnp.concatenate(
                    [row(b * 8 + s * 2 + c) for b in range(2)],
                    axis=1,
                )
                for c in range(2)
            ],
            axis=0,
        ).astype(BF16)
        res = lax.dot_general(
            hot, values, (((0,), (0,)), ((), ())), preferred_element_type=F32
        )
        for b in range(2):
            for j in range(4):
                start = (b * 64 + (s // 2) * 32) * 8 + (s % 2) * 4 + j
                scr2_ref[pl.ds(start, 32, stride=8), :] = res[
                    j * 32 : (j + 1) * 32, b * W : (b + 1) * W
                ]
    out_ref[...] = scr2_ref[...].astype(BF16)


def plan_kernel(tile_ref, got_ref, hot_ref, base_ref):
    late = jnp.bitwise_and(jnp.right_shift(tile_ref[0], 5), 1) == 1
    n = 4 * NT
    turned = [got_ref[pl.ds(j, NT, stride=4), :].T for j in range(4)]
    sub = lax.broadcasted_iota(jnp.int32, (n, n), 0)

    def pick(early_value, late_value):
        return jnp.where(late, late_value, early_value)

    def one_hot(row):
        return jnp.where(sub == row, 1.0, 0.0).astype(BF16)

    def dest(part, s):
        k = part * STEPS + s
        row = jnp.concatenate(
            [
                pick(
                    t[L_DEST[0] + k : L_DEST[0] + k + 1, :],
                    t[L_DEST[1] + k : L_DEST[1] + k + 1, :],
                )
                for t in turned
            ],
            axis=1,
        )
        row = (row + 0.5).astype(jnp.int32)
        return jnp.right_shift(row, 8), jnp.bitwise_and(row, 3)

    def finals(part):
        tile_to, slot_to = dest(part, STEPS - 1)
        rows = {STEPS - 1: tile_to * 4 + slot_to}
        for s in range(STEPS - 2, -1, -1):
            mid_tile, mid_slot = dest(part, s)
            move = one_hot(mid_slot * NT + mid_tile)
            later = jnp.concatenate(
                [
                    jnp.broadcast_to(tile_to, (8, n)),
                    jnp.broadcast_to(slot_to, (8, n)),
                ],
                axis=0,
            )
            both = jnp.dot(
                later.astype(F32).astype(BF16), move, preferred_element_type=F32
            )
            tile_to = both[0:1, :].astype(jnp.int32)
            slot_to = both[8:9, :].astype(jnp.int32)
            rows[s] = tile_to * 4 + slot_to
        return rows

    columns = jnp.concatenate(
        [got_ref[pl.ds(j, NT, stride=4), :] for j in range(4)], axis=0
    )
    parts = []
    for _ in range(3):
        part = columns.astype(BF16)
        parts.append(part)
        columns = columns - part.astype(F32)
    parts = jnp.concatenate(parts, axis=1)

    def moved(row):
        res = jnp.dot(one_hot(row), parts, preferred_element_type=F32)
        return res[:, :W] + (res[:, W : 2 * W] + res[:, 2 * W :])

    bound = finals(0)
    hot_ref[0] = one_hot(pick(bound[0], bound[2]))
    hot_ref[1] = one_hot(pick(bound[1], bound[3]))
    outer = moved(bound[0])
    inner = moved(finals(1)[0])
    lane = lax.broadcasted_iota(jnp.int32, (n, W), 1)
    low = pick(0, SPLIT)
    high = pick(SPLIT, LEV)
    extra = pick(W, L_TOP)
    is_inner = jnp.logical_or(lane >= L_INNER, lane == extra)
    is_outer = jnp.logical_and(lane >= low, lane < high)
    base_ref[...] = jnp.where(is_outer, outer, jnp.where(is_inner, inner, 0.0))


def owner_kernel(tile_ref, got_ref, hot_ref, base_ref, mix_ref, out_ref, scr_ref):
    late = jnp.bitwise_and(jnp.right_shift(tile_ref[0], 5), 1)
    scr_ref[...] = got_ref[...].astype(F32)
    moved = []
    for s in range(2):
        edge = jnp.concatenate(
            [scr_ref[pl.ds(s * 4 + j, NT, stride=8), :] for j in range(4)], axis=0
        ).astype(BF16)
        moved.append(jnp.dot(hot_ref[s], edge, preferred_element_type=F32).astype(BF16))
    total = jnp.dot(
        jnp.concatenate(moved, axis=1), mix_ref[late], preferred_element_type=F32
    )
    out_ref[...] = base_ref[...] + (
        total[:, :W] + (total[:, W : 2 * W] + total[:, 2 * W :])
    )


def nest_kernel(got_ref, out_ref, sum_ref, early_ref, late_ref):
    for b in range(2):
        early = got_ref[b * 2 * W : b * 2 * W + W, :]
        late = got_ref[b * 2 * W + W : (b + 1) * 2 * W, :]
        sum_ref[...] = (early + late).T
        early_ref[...] = early.T
        late_ref[...] = late.T
        out_ref[pl.ds(b, LEV, stride=4), :] = sum_ref[:LEV, :]
        inner = 2 + b
        out_ref[pl.ds(inner, SPLIT, stride=4), :] = early_ref[L_INNER:, :]
        out_ref[pl.ds(inner + 4 * SPLIT, SPLIT, stride=4), :] = late_ref[L_INNER:, :]
        top = inner + 8 * SPLIT
        out_ref[top : top + 1, :] = late_ref[L_TOP : L_TOP + 1, :]


def stats_kernel(own_ref, other_ref, mean_ref, var_ref):
    for half in range(2):
        a0, a1, b0, b1 = (
            ref[pl.ds(half * 2 + b, LEV, stride=4), :]
            for ref in (own_ref, other_ref)
            for b in range(2)
        )
        lanes = slice(half * W, (half + 1) * W)
        mean = ((a0 + a1) + (b0 + b1)) / 4.0
        mean_ref[:, lanes] = mean
        own = (a0 - mean) * (a0 - mean) + (a1 - mean) * (a1 - mean)
        other = (b0 - mean) * (b0 - mean) + (b1 - mean) * (b1 - mean)
        var_ref[:, lanes] = (own + other) / 4.0


def in_hbm(x):
    return pltpu.with_memory_space_constraint(x, pltpu.HBM)


def exchange(x):
    return lax.all_to_all(x, "tile", split_axis=0, concat_axis=0, tiled=True)


def on_device(parent_state, nest_state, terrain, shift_x, boundary_index, reloc_dest):
    q_mix, e_mix = constants()
    q_mix, e_mix = jnp.asarray(q_mix), jnp.asarray(e_mix)
    sds = jax.ShapeDtypeStruct
    tile = lax.axis_index("tile").astype(jnp.int32).reshape(1)
    parent = parent_state.reshape(FLAT, W)

    nest = nest_state.reshape(2, LEV, 2, W).transpose(1, 2, 0, 3)
    kept, down, up, nest, bidx, dest, q_mix = call(
        halo_kernel,
        (
            pltpu.VMEM((FLAT, W), F32),
            sds((HALO_ROWS, W), BF16),
            sds((HALO_ROWS, W), BF16),
            pltpu.VMEM((LEV, 2, 2, W), F32),
            pltpu.VMEM((STEPS, NT), jnp.int32),
            pltpu.VMEM((STEPS, 2 * W), jnp.int32),
            pltpu.VMEM((2 * W, 2 * W), F32),
        ),
        in_specs=[SM, HB, HB, HB, HB, HB, HB],
        scratch=[
            pltpu.VMEM((ROWS, W), jnp.int32),
            pltpu.VMEM((HALO_ROWS, W), F32),
            pltpu.VMEM((HALO_ROWS, W), F32),
            pltpu.VMEM((ROWS, W), F32),
            pltpu.SemaphoreType.DMA((6,)),
        ],
        name="halo",
        nbytes=1 << 20,
    )(
        tile,
        in_hbm(parent),
        in_hbm(terrain),
        in_hbm(nest),
        in_hbm(boundary_index),
        in_hbm(reloc_dest),
        in_hbm(q_mix),
    )
    message = call(
        send_kernel,
        sds((4 * NT, W), F32),
        in_specs=[HB, VM, VM, VM, VM],
        scratch=[
            pltpu.SMEM((STEPS,), jnp.int32),
            pltpu.VMEM((2, 2 * W, W), F32),
            pltpu.SemaphoreType.DMA((1,)),
        ],
        name="send",
        nbytes=64 << 20,
    )(in_hbm(shift_x), nest, bidx, dest, q_mix)
    pairs = [(i, i + 1) for i in range(0, NT, 2)] + [(i + 1, i) for i in range(0, NT, 2)]
    gaps = [(i, i + 1) for i in range(1, NT - 1, 2)]
    gaps = gaps + [(i + 1, i) for i in range(1, NT - 1, 2)]
    from_pair = lax.ppermute(down, "tile", pairs)
    from_gap = lax.ppermute(up, "tile", gaps)
    first = exchange(message.reshape(NT, 4, W)).reshape(4 * NT, W)
    cells, ring = call(
        parent_kernel,
        (
            pltpu.VMEM((STEPS, 2 * W, ROWS * W), BF16),
            pltpu.HBM((2 * BSTR, W), F32),
        ),
        in_specs=[SM, VM, VM, VM, HB],
        out_specs=(VM, HB),
        scratch=[
            pltpu.VMEM((HALO_ROWS, W), F32),
            pltpu.VMEM((HALO_ROWS, W), F32),
            pltpu.VMEM((FLAT, W), F32),
            pltpu.VMEM((ROWS, W), F32),
            pltpu.VMEM((2 * BSTR, W), F32),
            pltpu.VMEM((2 * BSTR, W), F32),
            pltpu.VMEM((2 * BSTR, W), F32),
            pltpu.VMEM((ROWS, W), jnp.int32),
            pltpu.SemaphoreType.DMA((2,)),
        ],
        name="parent",
        flops=1 << 40,
        nbytes=1 << 36,
    )(tile, kept, from_pair, from_gap, in_hbm(terrain))

    values = call(
        gather_kernel,
        sds((PACK * NT, W), BF16),
        scratch=[pltpu.VMEM((PACK * NT, W), F32)],
        name="gather",
        flops=1 << 29,
        nbytes=3 << 20,
    )(first, cells)
    second = exchange(values.reshape(PACK // 4 * NT, 4, W)).reshape(PACK * NT, W)

    parent_out = call(
        last_parent_kernel,
        sds((2 * LEV, ROWS, W), F32),
        in_specs=[HB, HB],
        scratch=[
            pltpu.VMEM((2 * BSTR, W), F32),
            pltpu.VMEM((ROWS, W), jnp.int32),
            pltpu.SemaphoreType.DMA((2,)),
        ],
        name="last_parent",
        flops=1 << 22,
        nbytes=2 << 20,
    )(in_hbm(ring), in_hbm(terrain))
    hot, base = call(
        plan_kernel,
        (sds((2, 4 * NT, 4 * NT), BF16), sds((4 * NT, W), F32)),
        in_specs=[SM, VM],
        name="plan",
        flops=1 << 28,
        nbytes=3 << 20,
    )(tile, first)

    second, parent_out = lax.optimization_barrier((second, parent_out))
    bperm = boundary_index.reshape(STEPS, 32, 4).transpose(0, 2, 1).reshape(STEPS, NT)
    edges = call(
        regroup_kernel,
        sds((8 * NT, W), BF16),
        scratch=[pltpu.VMEM((PACK * NT, W), F32), pltpu.VMEM((8 * NT, W), F32)],
        name="regroup",
        flops=1 << 26,
        nbytes=1 << 20,
    )(bperm, second)
    third = exchange(edges.reshape(NT, 8, W)).reshape(8 * NT, W)

    columns = call(
        owner_kernel,
        sds((4 * NT, W), F32),
        in_specs=[SM, VM, VM, VM, VM],
        scratch=[pltpu.VMEM((8 * NT, W), F32)],
        name="owner",
        flops=1 << 29,
        nbytes=3 << 20,
    )(tile, third, hot, base, e_mix)
    fourth = exchange(columns.reshape(NT, 4, W)).reshape(4 * NT, W)

    nest_out = call(
        nest_kernel,
        sds((4 * LEV, W), F32),
        scratch=[pltpu.VMEM((W, W), F32)] * 3,
        name="nest",
        nbytes=1 << 19,
    )(fourth)
    other = lax.ppermute(nest_out, "member", [(0, 1), (1, 0)])
    mean, variance = call(
        stats_kernel,
        (sds((LEV, 2 * W), F32), sds((LEV, 2 * W), F32)),
        name="stats",
        nbytes=1 << 19,
    )(nest_out, other)
    nest_out = nest_out.reshape(LEV, 2, 2, W).transpose(2, 0, 1, 3)
    nest_out = nest_out.reshape(nest_state.shape)
    return (parent_out.reshape(parent_state.shape), nest_out, mean, variance)


def solution(mesh):
    in_specs = (
        P("member", None, "tile", None),
        P("member", None, "tile"),
        P("tile", None),
        P(),
        P(None, "tile"),
        P(None, "tile"),
    )
    out_specs = (
        P("member", None, "tile", None),
        P("member", None, "tile"),
        P(None, "tile"),
        P(None, "tile"),
    )
    return jax.shard_map(
        on_device, mesh=mesh, in_specs=in_specs, out_specs=out_specs, check_vma=False
    )
```

```python
import functools

import jax
import jax.numpy as jnp
import numpy as np
from jax import lax
from jax.experimental import pallas as pl
from jax.experimental.pallas import tpu as pltpu
from jax.sharding import PartitionSpec as P

F32 = jnp.float32
BF16 = jnp.bfloat16
LEV = 81
STEPS = 4
NT = 128
ROWS = 8
W = 128
LPAD = 96
RING = 16
BSTR = LPAD * RING
SENT = 6
FLAT = 2 * LEV * ROWS
HALO_ROWS = 992
DIST = ((0, 1), (2, 3), (4, None), (5, None))
SPLIT = 40
PACK = 12
CUT = W - LEV
L_TOP = 81
L_REQ = 86
L_INNER = 88
L_DEST = (48, 8)
HORIZ = 0.15
VERT = 0.1
DRAG = 0.1
RELAX = 0.5
IMPL = 0.8
VMEM_LIMIT = 20 * 1024 * 1024


def solve_matrix():
    n = np.full(LEV, 2.0)
    n[0] = n[-1] = 1.0
    a = np.diag(1.0 + IMPL * n)
    a -= IMPL * (np.eye(LEV, k=1) + np.eye(LEV, k=-1))
    return np.linalg.inv(a)


def padded_transpose(m):
    out = np.zeros((W, W))
    out[:LEV, :LEV] = m.T
    return out


def split3(m):
    m = np.asarray(m, np.float64)
    parts = []
    for _ in range(3):
        part = m.astype(jnp.bfloat16)
        parts.append(part)
        m = m - part.astype(np.float64)
    return parts


def constants():
    s = solve_matrix()
    power = [np.linalg.matrix_power(s, k) for k in range(STEPS + 1)]
    keep = 1.0 - RELAX
    inner = power[STEPS].T
    bound = power[STEPS].T * keep**STEPS
    send = np.zeros((2, W, 2, W))
    send[0, :LEV, 0, :SPLIT] = bound[:, :SPLIT]
    send[0, :LEV, 1, SPLIT:LEV] = bound[:, SPLIT:]
    send[1, :LEV, 0, L_INNER:] = inner[:, :SPLIT]
    send[1, :LEV, 1, L_INNER:] = inner[:, SPLIT : 2 * SPLIT]
    send[1, :LEV, 1, L_TOP] = inner[:, 2 * SPLIT]
    for part in range(2):
        for owner in range(2):
            for k in range(STEPS):
                send[part, LEV + k, owner, L_DEST[owner] + part * STEPS + k] = 1.0
    send = send.reshape(2 * W, 2 * W).astype(np.float32)
    mix = [
        padded_transpose(power[STEPS - k] * RELAX * keep ** (STEPS - 1 - k))
        for k in range(STEPS)
    ]
    edge = np.stack(
        [
            np.concatenate(split3(np.concatenate(mix[:2])), axis=1),
            np.concatenate(split3(np.concatenate(mix[2:])), axis=1),
        ]
    )
    return send, edge


def call(
    body, out_shape, in_specs=None, out_specs=None, scratch=(), name=None, flops=0, nbytes=0
):
    kwargs = {} if in_specs is None else {"in_specs": in_specs}
    if out_specs is not None:
        kwargs["out_specs"] = out_specs
    return pl.pallas_call(
        body,
        out_shape=out_shape,
        scratch_shapes=list(scratch),
        compiler_params=pltpu.CompilerParams(vmem_limit_bytes=VMEM_LIMIT),
        cost_estimate=pl.CostEstimate(
            flops=flops, bytes_accessed=nbytes, transcendentals=0
        ),
        name=name,
        **kwargs,
    )


VM = pl.BlockSpec(memory_space=pltpu.VMEM)
HB = pl.BlockSpec(memory_space=pltpu.HBM)
SM = pl.BlockSpec(memory_space=pltpu.SMEM)


def start_all(pairs, sems):
    copies = [pltpu.make_async_copy(x, y, sems.at[i]) for i, (x, y) in enumerate(pairs)]
    for copy in copies:
        copy.start()
    return copies


def halo_kernel(
    tile_ref, parent_hbm, terrain_hbm, nest_hbm, bidx_hbm, dest_hbm, mix_hbm,
    parent_ref, first_ref, second_ref, nest_ref, bidx_ref, dest_ref, mix_ref,
    terrain_ref, down_ref, up_ref, damp_ref, sems,
):
    copies = start_all(
        [
            (parent_hbm, parent_ref),
            (terrain_hbm, terrain_ref),
            (nest_hbm, nest_ref),
            (bidx_hbm, bidx_ref),
            (dest_hbm, dest_ref),
            (mix_hbm, mix_ref),
        ],
        sems,
    )
    for copy in copies[:2]:
        copy.wait()
    damp_ref[...] = DRAG * terrain_ref[...].astype(F32) / 3000.0
    for ref, rows in ((down_ref, (7, 6, 5, 4)), (up_ref, (0, 1, 2, 3))):
        ref[HALO_ROWS - 24 :, :] = jnp.zeros((24, W), F32)
        for row, (coarse, fine) in zip(rows, DIST):
            for count, base, value in (
                (2 * LEV, 0, parent_ref[pl.ds(row, 2 * LEV, stride=ROWS), :]),
                (1, 2 * LEV * SENT, damp_ref[row : row + 1, :]),
            ):
                ref[pl.ds(base + coarse, count, stride=SENT), :] = value
                if fine is not None:
                    rest = value - value.astype(BF16).astype(F32)
                    ref[pl.ds(base + fine, count, stride=SENT), :] = rest
    even = jnp.bitwise_and(tile_ref[0], 1) == 0
    down, up = down_ref[...], up_ref[...]
    first_ref[...] = jnp.where(even, down, up).astype(BF16)
    second_ref[...] = jnp.where(even, up, down).astype(BF16)
    for copy in copies[2:]:
        copy.wait()


def send_kernel(
    shift_hbm, nest_ref, bidx_ref, dest_ref, mix_ref,
    msg_ref,
    shift_ref, pad_ref, sems,
):
    copies = start_all([(shift_hbm, shift_ref)], sems)
    zeros = jnp.zeros((W - LEV + 1, W), F32)
    for b in range(2):
        for part in range(2):
            top = part * W
            pad_ref[b, top + LEV - 1 : top + W, :] = zeros
            pad_ref[b, top : top + LEV, :] = nest_ref[:, part, b, :]
            pad_ref[b, top + LEV : top + LEV + STEPS, :] = dest_ref[
                :, part * W : (part + 1) * W
            ].astype(F32)
        res = lax.dot_general(
            pad_ref[b],
            mix_ref[...],
            (((0,), (0,)), ((), ())),
            precision=lax.Precision.HIGHEST,
            preferred_element_type=F32,
        )
        for owner in range(2):
            start = b * 2 * W + owner * W
            msg_ref[start : start + W, :] = res[:, owner * W : (owner + 1) * W]
    copies[0].wait()
    lane = lax.broadcasted_iota(jnp.int32, (NT, W), 1)
    tile = lax.broadcasted_iota(jnp.int32, (NT, W), 0)
    for s in range(STEPS):
        idx = bidx_ref[s : s + 1, :]
        owner = jnp.right_shift(idx, 10)
        row = jnp.bitwise_and(jnp.right_shift(idx, 7), ROWS - 1)
        col = jnp.bitwise_and(jnp.bitwise_and(idx, W - 1) + shift_ref[s], W - 1)
        cell = (row * W + col + 1).astype(F32)
        mine = tile == owner
        picked = jnp.where(mine, jnp.broadcast_to(cell, (NT, W)), 0.0)
        even = jnp.bitwise_and(lane, 1) == 0
        first = jnp.sum(jnp.where(even, picked, 0.0), axis=1, keepdims=True) - 1.0
        second = jnp.sum(jnp.where(even, 0.0, picked), axis=1, keepdims=True) - 1.0
        rows = msg_ref[pl.ds(s, NT, stride=4), :]
        rows = jnp.where(lane == L_REQ, first, rows)
        rows = jnp.where(lane == L_REQ + 1, second, rows)
        msg_ref[pl.ds(s, NT, stride=4), :] = rows


def ring_step(read, write, level_stride, coef, own_only=False):
    row = lax.broadcasted_iota(jnp.int32, (ROWS, W), 0)
    last = row == ROWS - 1
    head = row == 0
    c0, c1, h1, v1 = coef
    chunk = 9

    def body(step, carry):
        for member in range(2):
            for k in range(chunk):
                level = step * chunk + k
                base = member * level_stride
                below = base + jnp.maximum(level - 1, 0)
                above = base + jnp.minimum(level + 1, LEV - 1)
                x0, x1 = read(base + level)
                d0, d1 = read(below)
                u0, u1 = read(above)
                f0 = pltpu.roll(x0, ROWS - 1, 0)
                f1 = pltpu.roll(x1, ROWS - 1, 0)
                g0 = pltpu.roll(x0, 1, 0)
                g1 = pltpu.roll(x1, 1, 0)
                near0 = jnp.where(last, f1, f0) + jnp.where(head, g1, g0)
                near0 = near0 + (pltpu.roll(x0, 1, 1) + pltpu.roll(x0, W - 1, 1))
                y0 = c0 * x0 + HORIZ * near0 + VERT * (d0 + u0)
                if own_only:
                    write(member, level, y0, None)
                    continue
                near1 = jnp.where(last, f0, f1) + jnp.where(head, g0, g1)
                near1 = near1 + (pltpu.roll(x1, 1, 1) + pltpu.roll(x1, W - 1, 1))
                y1 = c1 * x1 + h1 * near1 + v1 * (d1 + u1)
                write(member, level, y0, y1)
        return carry

    lax.fori_loop(0, LEV // chunk, body, 0)


def parent_kernel(
    tile_ref, parent_ref, second_ref, first_ref, terrain_hbm,
    cells_ref, ring_hbm,
    next_ref, prev_ref, halo_ref, damp_ref, a_ref, b_ref, ring_ref, terrain_ref, sems,
):
    copies = start_all([(terrain_hbm, terrain_ref)], sems)
    store = pltpu.make_async_copy(ring_ref, ring_hbm, sems.at[1])
    tile = tile_ref[0]
    even = jnp.bitwise_and(tile, 1) == 0
    first, second = first_ref[...].astype(F32), second_ref[...].astype(F32)
    next_ref[...] = jnp.where(even, first, second)
    prev_ref[...] = jnp.where(even, second, first)
    for ref, rows in ((next_ref, (0, 1, 2, 3)), (prev_ref, (7, 6, 5, 4))):
        for row, (coarse, fine) in zip(rows, DIST):
            for count, base, out in ((2 * LEV, 0, halo_ref), (1, 2 * LEV * SENT, damp_ref)):
                value = ref[pl.ds(base + coarse, count, stride=SENT), :]
                if fine is not None:
                    value = value + ref[pl.ds(base + fine, count, stride=SENT), :]
                out[pl.ds(row, count, stride=ROWS), :] = value
    copies[0].wait()
    damping = DRAG * terrain_ref[...].astype(F32) / 3000.0
    pads = jnp.zeros(((LPAD - LEV) * RING, W), F32)
    for ref in (a_ref, b_ref, ring_ref):
        for member in range(2):
            top = member * BSTR + LEV * RING
            ref[top : top + (LPAD - LEV) * RING, :] = pads
    for s in range(STEPS):
        for member in range(2):
            start = LPAD if s else LEV - 1
            cells_ref[s, member * W + start : (member + 1) * W, :] = jnp.zeros(
                (W - start, ROWS * W), BF16
            )
    row = lax.broadcasted_iota(jnp.int32, (ROWS, W), 0)
    south = jnp.where(tile < NT - 1, 1.0, 0.0).astype(F32)
    north = jnp.where(tile > 0, 1.0, 0.0).astype(F32)
    valid = jnp.where(row < 4, south, north)
    stay = 1.0 - 4.0 * HORIZ - 2.0 * VERT
    coef = (stay - damping, (stay - damp_ref[...]) * valid, HORIZ * valid, VERT * valid)

    def emit(s, ref, count, stride):
        for member in range(2):
            for y in range(ROWS):
                start = member * count * stride + y
                rows = ref[pl.ds(start, count, stride=stride), :]
                cells_ref[s, member * W : member * W + count, y * W : (y + 1) * W] = (
                    rows.astype(BF16)
                )

    def read_first(index):
        base = pl.multiple_of(index * ROWS, ROWS)
        return parent_ref[pl.ds(base, ROWS), :], halo_ref[pl.ds(base, ROWS), :]

    emit(0, parent_ref, LEV, ROWS)
    read, stride = read_first, LEV
    for s, dst in zip(range(1, STEPS), (a_ref, b_ref, ring_ref)):

        def write(member, level, y0, y1, dst=dst):
            base = pl.multiple_of((member * LPAD + level) * RING, RING)
            dst[pl.ds(base, ROWS), :] = y0
            dst[pl.ds(base + ROWS, ROWS), :] = y1

        ring_step(read, write, stride, coef)
        if s == STEPS - 1:
            store.start()
        emit(s, dst, LPAD, RING)

        def read(index, src=dst):
            base = pl.multiple_of(index * RING, RING)
            return src[pl.ds(base, ROWS), :], src[pl.ds(base + ROWS, ROWS), :]

        stride = LPAD
    store.wait()


def last_parent_kernel(ring_hbm, terrain_hbm, out_ref, ring_ref, terrain_ref, sems):
    for copy in start_all([(ring_hbm, ring_ref), (terrain_hbm, terrain_ref)], sems):
        copy.wait()
    damping = DRAG * terrain_ref[...].astype(F32) / 3000.0
    stay = 1.0 - 4.0 * HORIZ - 2.0 * VERT

    def read(index):
        base = pl.multiple_of(index * RING, RING)
        return ring_ref[pl.ds(base, ROWS), :], ring_ref[pl.ds(base + ROWS, ROWS), :]

    def write(member, level, y0, y1):
        out_ref[member * LEV + level] = y0

    ring_step(read, write, LPAD, (stay - damping, None, None, None), own_only=True)


def gather_kernel(got_ref, cells_ref, out_ref, scr_ref):
    cell = lax.broadcasted_iota(jnp.int32, (NT, ROWS * W), 1).astype(F32)
    lane = lax.broadcasted_iota(jnp.int32, (NT, W), 1)
    rows = {}
    for s in range(STEPS):
        asked = got_ref[pl.ds(s, NT, stride=4), :]
        hot = [
            jnp.where(cell == asked[:, L_REQ + c : L_REQ + c + 1], 1.0, 0.0).astype(BF16)
            for c in range(2)
        ]
        hot = jnp.concatenate(hot, axis=0)
        res = lax.dot_general(
            hot, cells_ref[s], (((1,), (1,)), ((), ())), preferred_element_type=F32
        )
        for b in range(2):
            for c in range(2):
                rows[b * 8 + s * 2 + c] = res[c * W : (c + 1) * W, b * W : (b + 1) * W]
    for r in range(PACK):
        row = rows[r]
        if r < 8:
            extra = rows[PACK + r // 2]
            if r % 2 == 0:
                row = row + pltpu.roll(jnp.where(lane < CUT, extra, 0.0), LEV, 1)
            else:
                row = row + pltpu.roll(jnp.where(lane < CUT, 0.0, extra), LEV - CUT, 1)
        scr_ref[pl.ds(r, NT, stride=PACK), :] = row
    out_ref[...] = scr_ref[...].astype(BF16)


def regroup_kernel(bperm_ref, got_ref, out_ref, scr_ref, scr2_ref):
    scr_ref[...] = got_ref[...].astype(F32)
    low = lax.broadcasted_iota(jnp.int32, (NT, W), 1) < CUT

    def row(r):
        if r < PACK:
            return scr_ref[pl.ds(r, NT, stride=PACK), :]
        first = pltpu.roll(row(2 * (r - PACK)), W - LEV, 1)
        second = pltpu.roll(row(2 * (r - PACK) + 1), W - LEV + CUT, 1)
        return jnp.where(low, first, second)

    sub = lax.broadcasted_iota(jnp.int32, (2 * NT, W), 0)
    lane = lax.broadcasted_iota(jnp.int32, (2 * NT, W), 1)
    parity = jnp.bitwise_and(jnp.right_shift(lane, 5), 1)
    target = sub - parity * NT
    for s in range(STEPS):
        owner = jnp.right_shift(bperm_ref[s : s + 1, :], 10)
        hot = jnp.where(target == owner, 1.0, 0.0).astype(BF16)
        values = jnp.concatenate(
            [
                jnp.concatenate(
                    [row(b * 8 + s * 2 + c) for b in range(2)],
                    axis=1,
                )
                for c in range(2)
            ],
            axis=0,
        ).astype(BF16)
        res = lax.dot_general(
            hot, values, (((0,), (0,)), ((), ())), preferred_element_type=F32
        )
        for b in range(2):
            for j in range(4):
                start = (b * 64 + (s // 2) * 32) * 8 + (s % 2) * 4 + j
                scr2_ref[pl.ds(start, 32, stride=8), :] = res[
                    j * 32 : (j + 1) * 32, b * W : (b + 1) * W
                ]
    out_ref[...] = scr2_ref[...].astype(BF16)


def plan_kernel(tile_ref, got_ref, hot_ref, base_ref):
    late = jnp.bitwise_and(jnp.right_shift(tile_ref[0], 5), 1) == 1
    n = 4 * NT
    turned = [got_ref[pl.ds(j, NT, stride=4), :].T for j in range(4)]
    sub = lax.broadcasted_iota(jnp.int32, (n, n), 0)

    def pick(early_value, late_value):
        return jnp.where(late, late_value, early_value)

    def one_hot(row):
        return jnp.where(sub == row, 1.0, 0.0).astype(BF16)

    def dest(part, s):
        k = part * STEPS + s
        row = jnp.concatenate(
            [
                pick(
                    t[L_DEST[0] + k : L_DEST[0] + k + 1, :],
                    t[L_DEST[1] + k : L_DEST[1] + k + 1, :],
                )
                for t in turned
            ],
            axis=1,
        )
        row = (row + 0.5).astype(jnp.int32)
        return jnp.right_shift(row, 8), jnp.bitwise_and(row, 3)

    def finals(part):
        tile_to, slot_to = dest(part, STEPS - 1)
        rows = {STEPS - 1: tile_to * 4 + slot_to}
        for s in range(STEPS - 2, -1, -1):
            mid_tile, mid_slot = dest(part, s)
            move = one_hot(mid_slot * NT + mid_tile)
            later = jnp.concatenate(
                [
                    jnp.broadcast_to(tile_to, (8, n)),
                    jnp.broadcast_to(slot_to, (8, n)),
                ],
                axis=0,
            )
            both = jnp.dot(
                later.astype(F32).astype(BF16), move, preferred_element_type=F32
            )
            tile_to = both[0:1, :].astype(jnp.int32)
            slot_to = both[8:9, :].astype(jnp.int32)
            rows[s] = tile_to * 4 + slot_to
        return rows

    columns = jnp.concatenate(
        [got_ref[pl.ds(j, NT, stride=4), :] for j in range(4)], axis=0
    )
    parts = []
    for _ in range(3):
        part = columns.astype(BF16)
        parts.append(part)
        columns = columns - part.astype(F32)
    parts = jnp.concatenate(parts, axis=1)

    def moved(row):
        res = jnp.dot(one_hot(row), parts, preferred_element_type=F32)
        return res[:, :W] + (res[:, W : 2 * W] + res[:, 2 * W :])

    bound = finals(0)
    hot_ref[0] = one_hot(pick(bound[0], bound[2]))
    hot_ref[1] = one_hot(pick(bound[1], bound[3]))
    outer = moved(bound[0])
    inner = moved(finals(1)[0])
    lane = lax.broadcasted_iota(jnp.int32, (n, W), 1)
    low = pick(0, SPLIT)
    high = pick(SPLIT, LEV)
    extra = pick(W, L_TOP)
    is_inner = jnp.logical_or(lane >= L_INNER, lane == extra)
    is_outer = jnp.logical_and(lane >= low, lane < high)
    base_ref[...] = jnp.where(is_outer, outer, jnp.where(is_inner, inner, 0.0))


def owner_kernel(tile_ref, got_ref, hot_ref, base_ref, mix_ref, out_ref, scr_ref):
    late = jnp.bitwise_and(jnp.right_shift(tile_ref[0], 5), 1)
    scr_ref[...] = got_ref[...].astype(F32)
    moved = []
    for s in range(2):
        edge = jnp.concatenate(
            [scr_ref[pl.ds(s * 4 + j, NT, stride=8), :] for j in range(4)], axis=0
        ).astype(BF16)
        moved.append(jnp.dot(hot_ref[s], edge, preferred_element_type=F32).astype(BF16))
    total = jnp.dot(
        jnp.concatenate(moved, axis=1), mix_ref[late], preferred_element_type=F32
    )
    out_ref[...] = base_ref[...] + (
        total[:, :W] + (total[:, W : 2 * W] + total[:, 2 * W :])
    )


def nest_kernel(got_ref, out_ref, sum_ref, early_ref, late_ref):
    for b in range(2):
        early = got_ref[b * 2 * W : b * 2 * W + W, :]
        late = got_ref[b * 2 * W + W : (b + 1) * 2 * W, :]
        sum_ref[...] = (early + late).T
        early_ref[...] = early.T
        late_ref[...] = late.T
        out_ref[pl.ds(b, LEV, stride=4), :] = sum_ref[:LEV, :]
        inner = 2 + b
        out_ref[pl.ds(inner, SPLIT, stride=4), :] = early_ref[L_INNER:, :]
        out_ref[pl.ds(inner + 4 * SPLIT, SPLIT, stride=4), :] = late_ref[L_INNER:, :]
        top = inner + 8 * SPLIT
        out_ref[top : top + 1, :] = late_ref[L_TOP : L_TOP + 1, :]


def stats_kernel(own_ref, other_ref, mean_ref, var_ref):
    for half in range(2):
        a0, a1, b0, b1 = (
            ref[pl.ds(half * 2 + b, LEV, stride=4), :]
            for ref in (own_ref, other_ref)
            for b in range(2)
        )
        lanes = slice(half * W, (half + 1) * W)
        mean = ((a0 + a1) + (b0 + b1)) / 4.0
        mean_ref[:, lanes] = mean
        own = (a0 - mean) * (a0 - mean) + (a1 - mean) * (a1 - mean)
        other = (b0 - mean) * (b0 - mean) + (b1 - mean) * (b1 - mean)
        var_ref[:, lanes] = (own + other) / 4.0


def in_hbm(x):
    return pltpu.with_memory_space_constraint(x, pltpu.HBM)


def exchange(x):
    return lax.all_to_all(x, "tile", split_axis=0, concat_axis=0, tiled=True)


def on_device(parent_state, nest_state, terrain, shift_x, boundary_index, reloc_dest):
    q_mix, e_mix = constants()
    q_mix, e_mix = jnp.asarray(q_mix), jnp.asarray(e_mix)
    sds = jax.ShapeDtypeStruct
    tile = lax.axis_index("tile").astype(jnp.int32).reshape(1)
    parent = parent_state.reshape(FLAT, W)

    nest = nest_state.reshape(2, LEV, 2, W).transpose(1, 2, 0, 3)
    kept, down, up, nest, bidx, dest, q_mix = call(
        halo_kernel,
        (
            pltpu.VMEM((FLAT, W), F32),
            sds((HALO_ROWS, W), BF16),
            sds((HALO_ROWS, W), BF16),
            pltpu.VMEM((LEV, 2, 2, W), F32),
            pltpu.VMEM((STEPS, NT), jnp.int32),
            pltpu.VMEM((STEPS, 2 * W), jnp.int32),
            pltpu.VMEM((2 * W, 2 * W), F32),
        ),
        in_specs=[SM, HB, HB, HB, HB, HB, HB],
        scratch=[
            pltpu.VMEM((ROWS, W), jnp.int32),
            pltpu.VMEM((HALO_ROWS, W), F32),
            pltpu.VMEM((HALO_ROWS, W), F32),
            pltpu.VMEM((ROWS, W), F32),
            pltpu.SemaphoreType.DMA((6,)),
        ],
        name="halo",
        nbytes=1 << 20,
    )(
        tile,
        in_hbm(parent),
        in_hbm(terrain),
        in_hbm(nest),
        in_hbm(boundary_index),
        in_hbm(reloc_dest),
        in_hbm(q_mix),
    )
    message = call(
        send_kernel,
        sds((4 * NT, W), F32),
        in_specs=[HB, VM, VM, VM, VM],
        scratch=[
            pltpu.SMEM((STEPS,), jnp.int32),
            pltpu.VMEM((2, 2 * W, W), F32),
            pltpu.SemaphoreType.DMA((1,)),
        ],
        name="send",
        nbytes=64 << 20,
    )(in_hbm(shift_x), nest, bidx, dest, q_mix)
    pairs = [(i, i + 1) for i in range(0, NT, 2)] + [(i + 1, i) for i in range(0, NT, 2)]
    gaps = [(i, i + 1) for i in range(1, NT - 1, 2)]
    gaps = gaps + [(i + 1, i) for i in range(1, NT - 1, 2)]
    from_gap = lax.ppermute(up, "tile", gaps)
    from_pair = lax.ppermute(down, "tile", pairs)
    first = exchange(message.reshape(NT, 4, W)).reshape(4 * NT, W)
    cells, ring = call(
        parent_kernel,
        (
            pltpu.VMEM((STEPS, 2 * W, ROWS * W), BF16),
            pltpu.HBM((2 * BSTR, W), F32),
        ),
        in_specs=[SM, VM, VM, VM, HB],
        out_specs=(VM, HB),
        scratch=[
            pltpu.VMEM((HALO_ROWS, W), F32),
            pltpu.VMEM((HALO_ROWS, W), F32),
            pltpu.VMEM((FLAT, W), F32),
            pltpu.VMEM((ROWS, W), F32),
            pltpu.VMEM((2 * BSTR, W), F32),
            pltpu.VMEM((2 * BSTR, W), F32),
            pltpu.VMEM((2 * BSTR, W), F32),
            pltpu.VMEM((ROWS, W), jnp.int32),
            pltpu.SemaphoreType.DMA((2,)),
        ],
        name="parent",
        flops=1 << 33,
        nbytes=1 << 27,
    )(tile, kept, from_gap, from_pair, in_hbm(terrain))

    values = call(
        gather_kernel,
        sds((PACK * NT, W), BF16),
        scratch=[pltpu.VMEM((PACK * NT, W), F32)],
        name="gather",
        flops=1 << 29,
        nbytes=3 << 20,
    )(first, cells)
    second = exchange(values.reshape(PACK // 4 * NT, 4, W)).reshape(PACK * NT, W)

    hot, base = call(
        plan_kernel,
        (sds((2, 4 * NT, 4 * NT), BF16), sds((4 * NT, W), F32)),
        in_specs=[SM, VM],
        name="plan",
        flops=1 << 28,
        nbytes=3 << 20,
    )(tile, first)

    second, hot, base = lax.optimization_barrier((second, hot, base))
    bperm = boundary_index.reshape(STEPS, 32, 4).transpose(0, 2, 1).reshape(STEPS, NT)
    edges = call(
        regroup_kernel,
        sds((8 * NT, W), BF16),
        scratch=[pltpu.VMEM((PACK * NT, W), F32), pltpu.VMEM((8 * NT, W), F32)],
        name="regroup",
        flops=1 << 26,
        nbytes=1 << 20,
    )(bperm, second)
    third = exchange(edges.reshape(NT, 8, W)).reshape(8 * NT, W)

    parent_out = call(
        last_parent_kernel,
        sds((2 * LEV, ROWS, W), F32),
        in_specs=[HB, HB],
        scratch=[
            pltpu.VMEM((2 * BSTR, W), F32),
            pltpu.VMEM((ROWS, W), jnp.int32),
            pltpu.SemaphoreType.DMA((2,)),
        ],
        name="last_parent",
        flops=1 << 22,
        nbytes=2 << 20,
    )(in_hbm(ring), in_hbm(terrain))
    third, parent_out = lax.optimization_barrier((third, parent_out))
    columns = call(
        owner_kernel,
        sds((4 * NT, W), F32),
        in_specs=[SM, VM, VM, VM, VM],
        scratch=[pltpu.VMEM((8 * NT, W), F32)],
        name="owner",
        flops=1 << 29,
        nbytes=3 << 20,
    )(tile, third, hot, base, e_mix)
    fourth = exchange(columns.reshape(NT, 4, W)).reshape(4 * NT, W)

    nest_out = call(
        nest_kernel,
        sds((4 * LEV, W), F32),
        scratch=[pltpu.VMEM((W, W), F32)] * 3,
        name="nest",
        nbytes=1 << 19,
    )(fourth)
    other = lax.ppermute(nest_out, "member", [(0, 1), (1, 0)])
    mean, variance = call(
        stats_kernel,
        (sds((LEV, 2 * W), F32), sds((LEV, 2 * W), F32)),
        name="stats",
        nbytes=1 << 19,
    )(nest_out, other)
    nest_out = nest_out.reshape(LEV, 2, 2, W).transpose(2, 0, 1, 3)
    nest_out = nest_out.reshape(nest_state.shape)
    return (parent_out.reshape(parent_state.shape), nest_out, mean, variance)


def solution(mesh):
    in_specs = (
        P("member", None, "tile", None),
        P("member", None, "tile"),
        P("tile", None),
        P(),
        P(None, "tile"),
        P(None, "tile"),
    )
    out_specs = (
        P("member", None, "tile", None),
        P("member", None, "tile"),
        P(None, "tile"),
        P(None, "tile"),
    )
    return jax.shard_map(
        on_device, mesh=mesh, in_specs=in_specs, out_specs=out_specs, check_vma=False
    )
```

```python
import functools

import jax
import jax.numpy as jnp
import numpy as np
from jax import lax
from jax.experimental import pallas as pl
from jax.experimental.pallas import tpu as pltpu
from jax.sharding import PartitionSpec as P

F32 = jnp.float32
BF16 = jnp.bfloat16
LEV = 81
STEPS = 4
NT = 128
ROWS = 8
W = 128
LPAD = 96
RING = 16
BSTR = LPAD * RING
SENT = 6
FLAT = 2 * LEV * ROWS
HALO_ROWS = 992
DIST = ((0, 1), (2, 3), (4, None), (5, None))
SPLIT = 40
PACK = 12
CUT = W - LEV
L_TOP = 81
L_REQ = 86
L_INNER = 88
L_DEST = (48, 8)
HORIZ = 0.15
VERT = 0.1
DRAG = 0.1
RELAX = 0.5
IMPL = 0.8
VMEM_LIMIT = 20 * 1024 * 1024


def solve_matrix():
    n = np.full(LEV, 2.0)
    n[0] = n[-1] = 1.0
    a = np.diag(1.0 + IMPL * n)
    a -= IMPL * (np.eye(LEV, k=1) + np.eye(LEV, k=-1))
    return np.linalg.inv(a)


def padded_transpose(m):
    out = np.zeros((W, W))
    out[:LEV, :LEV] = m.T
    return out


def split3(m):
    m = np.asarray(m, np.float64)
    parts = []
    for _ in range(3):
        part = m.astype(jnp.bfloat16)
        parts.append(part)
        m = m - part.astype(np.float64)
    return parts


def constants():
    s = solve_matrix()
    power = [np.linalg.matrix_power(s, k) for k in range(STEPS + 1)]
    keep = 1.0 - RELAX
    inner = power[STEPS].T
    bound = power[STEPS].T * keep**STEPS
    send = np.zeros((2, W, 2, W))
    send[0, :LEV, 0, :SPLIT] = bound[:, :SPLIT]
    send[0, :LEV, 1, SPLIT:LEV] = bound[:, SPLIT:]
    send[1, :LEV, 0, L_INNER:] = inner[:, :SPLIT]
    send[1, :LEV, 1, L_INNER:] = inner[:, SPLIT : 2 * SPLIT]
    send[1, :LEV, 1, L_TOP] = inner[:, 2 * SPLIT]
    for part in range(2):
        for owner in range(2):
            for k in range(STEPS):
                send[part, LEV + k, owner, L_DEST[owner] + part * STEPS + k] = 1.0
    send = send.reshape(2 * W, 2 * W).astype(np.float32)
    mix = [
        padded_transpose(power[STEPS - k] * RELAX * keep ** (STEPS - 1 - k))
        for k in range(STEPS)
    ]
    edge = np.stack(
        [
            np.concatenate(split3(np.concatenate(mix[:2])), axis=1),
            np.concatenate(split3(np.concatenate(mix[2:])), axis=1),
        ]
    )
    return send, edge


def call(
    body, out_shape, in_specs=None, out_specs=None, scratch=(), name=None, flops=0, nbytes=0
):
    kwargs = {} if in_specs is None else {"in_specs": in_specs}
    if out_specs is not None:
        kwargs["out_specs"] = out_specs
    return pl.pallas_call(
        body,
        out_shape=out_shape,
        scratch_shapes=list(scratch),
        compiler_params=pltpu.CompilerParams(vmem_limit_bytes=VMEM_LIMIT),
        cost_estimate=pl.CostEstimate(
            flops=flops, bytes_accessed=nbytes, transcendentals=0
        ),
        name=name,
        **kwargs,
    )


VM = pl.BlockSpec(memory_space=pltpu.VMEM)
HB = pl.BlockSpec(memory_space=pltpu.HBM)
SM = pl.BlockSpec(memory_space=pltpu.SMEM)


def start_all(pairs, sems):
    copies = [pltpu.make_async_copy(x, y, sems.at[i]) for i, (x, y) in enumerate(pairs)]
    for copy in copies:
        copy.start()
    return copies


def halo_kernel(
    tile_ref, parent_hbm, terrain_hbm, nest_hbm, bidx_hbm, dest_hbm, mix_hbm,
    parent_ref, first_ref, second_ref, nest_ref, bidx_ref, dest_ref, mix_ref,
    terrain_ref, down_ref, up_ref, damp_ref, sems,
):
    copies = start_all(
        [
            (parent_hbm, parent_ref),
            (terrain_hbm, terrain_ref),
            (nest_hbm, nest_ref),
            (bidx_hbm, bidx_ref),
            (dest_hbm, dest_ref),
            (mix_hbm, mix_ref),
        ],
        sems,
    )
    for copy in copies[:2]:
        copy.wait()
    damp_ref[...] = DRAG * terrain_ref[...].astype(F32) / 3000.0
    for ref, rows in ((down_ref, (7, 6, 5, 4)), (up_ref, (0, 1, 2, 3))):
        ref[HALO_ROWS - 24 :, :] = jnp.zeros((24, W), F32)
        for row, (coarse, fine) in zip(rows, DIST):
            for count, base, value in (
                (2 * LEV, 0, parent_ref[pl.ds(row, 2 * LEV, stride=ROWS), :]),
                (1, 2 * LEV * SENT, damp_ref[row : row + 1, :]),
            ):
                ref[pl.ds(base + coarse, count, stride=SENT), :] = value
                if fine is not None:
                    rest = value - value.astype(BF16).astype(F32)
                    ref[pl.ds(base + fine, count, stride=SENT), :] = rest
    even = jnp.bitwise_and(tile_ref[0], 1) == 0
    down, up = down_ref[...], up_ref[...]
    first_ref[...] = jnp.where(even, down, up).astype(BF16)
    second_ref[...] = jnp.where(even, up, down).astype(BF16)
    for copy in copies[2:]:
        copy.wait()


def send_kernel(
    shift_hbm, nest_ref, bidx_ref, dest_ref, mix_ref,
    msg_ref,
    shift_ref, pad_ref, sems,
):
    copies = start_all([(shift_hbm, shift_ref)], sems)
    zeros = jnp.zeros((W - LEV + 1, W), F32)
    for b in range(2):
        for part in range(2):
            top = part * W
            pad_ref[b, top + LEV - 1 : top + W, :] = zeros
            pad_ref[b, top : top + LEV, :] = nest_ref[:, part, b, :]
            pad_ref[b, top + LEV : top + LEV + STEPS, :] = dest_ref[
                :, part * W : (part + 1) * W
            ].astype(F32)
        res = lax.dot_general(
            pad_ref[b],
            mix_ref[...],
            (((0,), (0,)), ((), ())),
            precision=lax.Precision.HIGHEST,
            preferred_element_type=F32,
        )
        for owner in range(2):
            start = b * 2 * W + owner * W
            msg_ref[start : start + W, :] = res[:, owner * W : (owner + 1) * W]
    copies[0].wait()
    lane = lax.broadcasted_iota(jnp.int32, (NT, W), 1)
    tile = lax.broadcasted_iota(jnp.int32, (NT, W), 0)
    for s in range(STEPS):
        idx = bidx_ref[s : s + 1, :]
        owner = jnp.right_shift(idx, 10)
        row = jnp.bitwise_and(jnp.right_shift(idx, 7), ROWS - 1)
        col = jnp.bitwise_and(jnp.bitwise_and(idx, W - 1) + shift_ref[s], W - 1)
        cell = (row * W + col + 1).astype(F32)
        mine = tile == owner
        picked = jnp.where(mine, jnp.broadcast_to(cell, (NT, W)), 0.0)
        even = jnp.bitwise_and(lane, 1) == 0
        first = jnp.sum(jnp.where(even, picked, 0.0), axis=1, keepdims=True) - 1.0
        second = jnp.sum(jnp.where(even, 0.0, picked), axis=1, keepdims=True) - 1.0
        rows = msg_ref[pl.ds(s, NT, stride=4), :]
        rows = jnp.where(lane == L_REQ, first, rows)
        rows = jnp.where(lane == L_REQ + 1, second, rows)
        msg_ref[pl.ds(s, NT, stride=4), :] = rows


def ring_step(read, write, level_stride, coef, own_only=False):
    row = lax.broadcasted_iota(jnp.int32, (ROWS, W), 0)
    last = row == ROWS - 1
    head = row == 0
    c0, c1, h1, v1 = coef
    chunk = 9

    def body(step, carry):
        start = step * chunk
        ends = jnp.maximum(start - 1, 0), jnp.minimum(start + chunk, LEV - 1)
        for member in range(2):
            base = member * level_stride
            column = [read(base + start + k) for k in range(chunk)]
            column = [read(base + ends[0])] + column + [read(base + ends[1])]
            for k in range(chunk):
                (d0, d1), (x0, x1), (u0, u1) = column[k : k + 3]
                f0 = pltpu.roll(x0, ROWS - 1, 0)
                f1 = pltpu.roll(x1, ROWS - 1, 0)
                g0 = pltpu.roll(x0, 1, 0)
                g1 = pltpu.roll(x1, 1, 0)
                near0 = jnp.where(last, f1, f0) + jnp.where(head, g1, g0)
                near0 = near0 + (pltpu.roll(x0, 1, 1) + pltpu.roll(x0, W - 1, 1))
                y0 = c0 * x0 + HORIZ * near0 + VERT * (d0 + u0)
                if own_only:
                    write(member, start + k, y0, None)
                    continue
                near1 = jnp.where(last, f0, f1) + jnp.where(head, g0, g1)
                near1 = near1 + (pltpu.roll(x1, 1, 1) + pltpu.roll(x1, W - 1, 1))
                y1 = c1 * x1 + h1 * near1 + v1 * (d1 + u1)
                write(member, start + k, y0, y1)
        return carry

    lax.fori_loop(0, LEV // chunk, body, 0)


def parent_kernel(
    tile_ref, parent_ref, second_ref, first_ref, terrain_hbm,
    cells_ref, ring_hbm,
    next_ref, prev_ref, halo_ref, damp_ref, a_ref, b_ref, ring_ref, terrain_ref, sems,
):
    copies = start_all([(terrain_hbm, terrain_ref)], sems)
    store = pltpu.make_async_copy(ring_ref, ring_hbm, sems.at[1])
    tile = tile_ref[0]
    even = jnp.bitwise_and(tile, 1) == 0
    first, second = first_ref[...].astype(F32), second_ref[...].astype(F32)
    next_ref[...] = jnp.where(even, first, second)
    prev_ref[...] = jnp.where(even, second, first)
    for ref, rows in ((next_ref, (0, 1, 2, 3)), (prev_ref, (7, 6, 5, 4))):
        for row, (coarse, fine) in zip(rows, DIST):
            for count, base, out in ((2 * LEV, 0, halo_ref), (1, 2 * LEV * SENT, damp_ref)):
                value = ref[pl.ds(base + coarse, count, stride=SENT), :]
                if fine is not None:
                    value = value + ref[pl.ds(base + fine, count, stride=SENT), :]
                out[pl.ds(row, count, stride=ROWS), :] = value
    copies[0].wait()
    damping = DRAG * terrain_ref[...].astype(F32) / 3000.0
    pads = jnp.zeros(((LPAD - LEV) * RING, W), F32)
    for ref in (a_ref, b_ref, ring_ref):
        for member in range(2):
            top = member * BSTR + LEV * RING
            ref[top : top + (LPAD - LEV) * RING, :] = pads
    for s in range(STEPS):
        for member in range(2):
            start = LPAD if s else LEV - 1
            cells_ref[s, member * W + start : (member + 1) * W, :] = jnp.zeros(
                (W - start, ROWS * W), BF16
            )
    row = lax.broadcasted_iota(jnp.int32, (ROWS, W), 0)
    south = jnp.where(tile < NT - 1, 1.0, 0.0).astype(F32)
    north = jnp.where(tile > 0, 1.0, 0.0).astype(F32)
    valid = jnp.where(row < 4, south, north)
    stay = 1.0 - 4.0 * HORIZ - 2.0 * VERT
    coef = (stay - damping, (stay - damp_ref[...]) * valid, HORIZ * valid, VERT * valid)

    def emit(s, ref, count, stride):
        for member in range(2):
            for y in range(ROWS):
                start = member * count * stride + y
                rows = ref[pl.ds(start, count, stride=stride), :]
                cells_ref[s, member * W : member * W + count, y * W : (y + 1) * W] = (
                    rows.astype(BF16)
                )

    def read_first(index):
        base = pl.multiple_of(index * ROWS, ROWS)
        return parent_ref[pl.ds(base, ROWS), :], halo_ref[pl.ds(base, ROWS), :]

    emit(0, parent_ref, LEV, ROWS)
    read, stride = read_first, LEV
    for s, dst in zip(range(1, STEPS), (a_ref, b_ref, ring_ref)):

        def write(member, level, y0, y1, dst=dst):
            base = pl.multiple_of((member * LPAD + level) * RING, RING)
            dst[pl.ds(base, ROWS), :] = y0
            dst[pl.ds(base + ROWS, ROWS), :] = y1

        ring_step(read, write, stride, coef)
        if s == STEPS - 1:
            store.start()
        emit(s, dst, LPAD, RING)

        def read(index, src=dst):
            base = pl.multiple_of(index * RING, RING)
            return src[pl.ds(base, ROWS), :], src[pl.ds(base + ROWS, ROWS), :]

        stride = LPAD
    store.wait()


def last_parent_kernel(ring_hbm, terrain_hbm, out_ref, ring_ref, terrain_ref, sems):
    for copy in start_all([(ring_hbm, ring_ref), (terrain_hbm, terrain_ref)], sems):
        copy.wait()
    damping = DRAG * terrain_ref[...].astype(F32) / 3000.0
    stay = 1.0 - 4.0 * HORIZ - 2.0 * VERT

    def read(index):
        base = pl.multiple_of(index * RING, RING)
        return ring_ref[pl.ds(base, ROWS), :], ring_ref[pl.ds(base + ROWS, ROWS), :]

    def write(member, level, y0, y1):
        out_ref[member * LEV + level] = y0

    ring_step(read, write, LPAD, (stay - damping, None, None, None), own_only=True)


def gather_kernel(got_ref, cells_ref, out_ref, scr_ref):
    cell = lax.broadcasted_iota(jnp.int32, (NT, ROWS * W), 1).astype(F32)
    lane = lax.broadcasted_iota(jnp.int32, (NT, W), 1)
    rows = {}
    for s in range(STEPS):
        asked = got_ref[pl.ds(s, NT, stride=4), :]
        hot = [
            jnp.where(cell == asked[:, L_REQ + c : L_REQ + c + 1], 1.0, 0.0).astype(BF16)
            for c in range(2)
        ]
        hot = jnp.concatenate(hot, axis=0)
        res = lax.dot_general(
            hot, cells_ref[s], (((1,), (1,)), ((), ())), preferred_element_type=F32
        )
        for b in range(2):
            for c in range(2):
                rows[b * 8 + s * 2 + c] = res[c * W : (c + 1) * W, b * W : (b + 1) * W]
    for r in range(PACK):
        row = rows[r]
        if r < 8:
            extra = rows[PACK + r // 2]
            if r % 2 == 0:
                row = row + pltpu.roll(jnp.where(lane < CUT, extra, 0.0), LEV, 1)
            else:
                row = row + pltpu.roll(jnp.where(lane < CUT, 0.0, extra), LEV - CUT, 1)
        scr_ref[pl.ds(r, NT, stride=PACK), :] = row
    out_ref[...] = scr_ref[...].astype(BF16)


def regroup_kernel(bperm_ref, got_ref, out_ref, scr_ref, scr2_ref):
    scr_ref[...] = got_ref[...].astype(F32)
    low = lax.broadcasted_iota(jnp.int32, (NT, W), 1) < CUT

    def row(r):
        if r < PACK:
            return scr_ref[pl.ds(r, NT, stride=PACK), :]
        first = pltpu.roll(row(2 * (r - PACK)), W - LEV, 1)
        second = pltpu.roll(row(2 * (r - PACK) + 1), W - LEV + CUT, 1)
        return jnp.where(low, first, second)

    sub = lax.broadcasted_iota(jnp.int32, (2 * NT, W), 0)
    lane = lax.broadcasted_iota(jnp.int32, (2 * NT, W), 1)
    parity = jnp.bitwise_and(jnp.right_shift(lane, 5), 1)
    target = sub - parity * NT
    for s in range(STEPS):
        owner = jnp.right_shift(bperm_ref[s : s + 1, :], 10)
        hot = jnp.where(target == owner, 1.0, 0.0).astype(BF16)
        values = jnp.concatenate(
            [
                jnp.concatenate(
                    [row(b * 8 + s * 2 + c) for b in range(2)],
                    axis=1,
                )
                for c in range(2)
            ],
            axis=0,
        ).astype(BF16)
        res = lax.dot_general(
            hot, values, (((0,), (0,)), ((), ())), preferred_element_type=F32
        )
        for b in range(2):
            for j in range(4):
                start = (b * 64 + (s // 2) * 32) * 8 + (s % 2) * 4 + j
                scr2_ref[pl.ds(start, 32, stride=8), :] = res[
                    j * 32 : (j + 1) * 32, b * W : (b + 1) * W
                ]
    out_ref[...] = scr2_ref[...].astype(BF16)


def plan_kernel(tile_ref, got_ref, hot_ref, base_ref):
    late = jnp.bitwise_and(jnp.right_shift(tile_ref[0], 5), 1) == 1
    n = 4 * NT
    turned = [got_ref[pl.ds(j, NT, stride=4), :].T for j in range(4)]
    sub = lax.broadcasted_iota(jnp.int32, (n, n), 0)

    def pick(early_value, late_value):
        return jnp.where(late, late_value, early_value)

    def one_hot(row):
        return jnp.where(sub == row, 1.0, 0.0).astype(BF16)

    def dest(part, s):
        k = part * STEPS + s
        row = jnp.concatenate(
            [
                pick(
                    t[L_DEST[0] + k : L_DEST[0] + k + 1, :],
                    t[L_DEST[1] + k : L_DEST[1] + k + 1, :],
                )
                for t in turned
            ],
            axis=1,
        )
        row = (row + 0.5).astype(jnp.int32)
        return jnp.right_shift(row, 8), jnp.bitwise_and(row, 3)

    def finals(part):
        tile_to, slot_to = dest(part, STEPS - 1)
        rows = {STEPS - 1: tile_to * 4 + slot_to}
        for s in range(STEPS - 2, -1, -1):
            mid_tile, mid_slot = dest(part, s)
            move = one_hot(mid_slot * NT + mid_tile)
            later = jnp.concatenate(
                [
                    jnp.broadcast_to(tile_to, (8, n)),
                    jnp.broadcast_to(slot_to, (8, n)),
                ],
                axis=0,
            )
            both = jnp.dot(
                later.astype(F32).astype(BF16), move, preferred_element_type=F32
            )
            tile_to = both[0:1, :].astype(jnp.int32)
            slot_to = both[8:9, :].astype(jnp.int32)
            rows[s] = tile_to * 4 + slot_to
        return rows

    columns = jnp.concatenate(
        [got_ref[pl.ds(j, NT, stride=4), :] for j in range(4)], axis=0
    )
    parts = []
    for _ in range(3):
        part = columns.astype(BF16)
        parts.append(part)
        columns = columns - part.astype(F32)
    parts = jnp.concatenate(parts, axis=1)

    def moved(row):
        res = jnp.dot(one_hot(row), parts, preferred_element_type=F32)
        return res[:, :W] + (res[:, W : 2 * W] + res[:, 2 * W :])

    bound = finals(0)
    hot_ref[0] = one_hot(pick(bound[0], bound[2]))
    hot_ref[1] = one_hot(pick(bound[1], bound[3]))
    outer = moved(bound[0])
    inner = moved(finals(1)[0])
    lane = lax.broadcasted_iota(jnp.int32, (n, W), 1)
    low = pick(0, SPLIT)
    high = pick(SPLIT, LEV)
    extra = pick(W, L_TOP)
    is_inner = jnp.logical_or(lane >= L_INNER, lane == extra)
    is_outer = jnp.logical_and(lane >= low, lane < high)
    base_ref[...] = jnp.where(is_outer, outer, jnp.where(is_inner, inner, 0.0))


def owner_kernel(tile_ref, got_ref, hot_ref, base_ref, mix_ref, out_ref, scr_ref):
    late = jnp.bitwise_and(jnp.right_shift(tile_ref[0], 5), 1)
    scr_ref[...] = got_ref[...].astype(F32)
    moved = []
    for s in range(2):
        edge = jnp.concatenate(
            [scr_ref[pl.ds(s * 4 + j, NT, stride=8), :] for j in range(4)], axis=0
        ).astype(BF16)
        moved.append(jnp.dot(hot_ref[s], edge, preferred_element_type=F32).astype(BF16))
    total = jnp.dot(
        jnp.concatenate(moved, axis=1), mix_ref[late], preferred_element_type=F32
    )
    out_ref[...] = base_ref[...] + (
        total[:, :W] + (total[:, W : 2 * W] + total[:, 2 * W :])
    )


def nest_kernel(got_ref, out_ref, sum_ref, early_ref, late_ref):
    for b in range(2):
        early = got_ref[b * 2 * W : b * 2 * W + W, :]
        late = got_ref[b * 2 * W + W : (b + 1) * 2 * W, :]
        sum_ref[...] = (early + late).T
        early_ref[...] = early.T
        late_ref[...] = late.T
        out_ref[pl.ds(b, LEV, stride=4), :] = sum_ref[:LEV, :]
        inner = 2 + b
        out_ref[pl.ds(inner, SPLIT, stride=4), :] = early_ref[L_INNER:, :]
        out_ref[pl.ds(inner + 4 * SPLIT, SPLIT, stride=4), :] = late_ref[L_INNER:, :]
        top = inner + 8 * SPLIT
        out_ref[top : top + 1, :] = late_ref[L_TOP : L_TOP + 1, :]


def stats_kernel(own_ref, other_ref, mean_ref, var_ref):
    for half in range(2):
        a0, a1, b0, b1 = (
            ref[pl.ds(half * 2 + b, LEV, stride=4), :]
            for ref in (own_ref, other_ref)
            for b in range(2)
        )
        lanes = slice(half * W, (half + 1) * W)
        mean = ((a0 + a1) + (b0 + b1)) / 4.0
        mean_ref[:, lanes] = mean
        own = (a0 - mean) * (a0 - mean) + (a1 - mean) * (a1 - mean)
        other = (b0 - mean) * (b0 - mean) + (b1 - mean) * (b1 - mean)
        var_ref[:, lanes] = (own + other) / 4.0


def in_hbm(x):
    return pltpu.with_memory_space_constraint(x, pltpu.HBM)


def exchange(x):
    return lax.all_to_all(x, "tile", split_axis=0, concat_axis=0, tiled=True)


def on_device(parent_state, nest_state, terrain, shift_x, boundary_index, reloc_dest):
    q_mix, e_mix = constants()
    q_mix, e_mix = jnp.asarray(q_mix), jnp.asarray(e_mix)
    sds = jax.ShapeDtypeStruct
    tile = lax.axis_index("tile").astype(jnp.int32).reshape(1)
    parent = parent_state.reshape(FLAT, W)

    nest = nest_state.reshape(2, LEV, 2, W).transpose(1, 2, 0, 3)
    kept, down, up, nest, bidx, dest, q_mix = call(
        halo_kernel,
        (
            pltpu.VMEM((FLAT, W), F32),
            sds((HALO_ROWS, W), BF16),
            sds((HALO_ROWS, W), BF16),
            pltpu.VMEM((LEV, 2, 2, W), F32),
            pltpu.VMEM((STEPS, NT), jnp.int32),
            pltpu.VMEM((STEPS, 2 * W), jnp.int32),
            pltpu.VMEM((2 * W, 2 * W), F32),
        ),
        in_specs=[SM, HB, HB, HB, HB, HB, HB],
        scratch=[
            pltpu.VMEM((ROWS, W), jnp.int32),
            pltpu.VMEM((HALO_ROWS, W), F32),
            pltpu.VMEM((HALO_ROWS, W), F32),
            pltpu.VMEM((ROWS, W), F32),
            pltpu.SemaphoreType.DMA((6,)),
        ],
        name="halo",
        nbytes=1 << 20,
    )(
        tile,
        in_hbm(parent),
        in_hbm(terrain),
        in_hbm(nest),
        in_hbm(boundary_index),
        in_hbm(reloc_dest),
        in_hbm(q_mix),
    )
    message = call(
        send_kernel,
        sds((4 * NT, W), F32),
        in_specs=[HB, VM, VM, VM, VM],
        scratch=[
            pltpu.SMEM((STEPS,), jnp.int32),
            pltpu.VMEM((2, 2 * W, W), F32),
            pltpu.SemaphoreType.DMA((1,)),
        ],
        name="send",
        nbytes=64 << 20,
    )(in_hbm(shift_x), nest, bidx, dest, q_mix)
    pairs = [(i, i + 1) for i in range(0, NT, 2)] + [(i + 1, i) for i in range(0, NT, 2)]
    gaps = [(i, i + 1) for i in range(1, NT - 1, 2)]
    gaps = gaps + [(i + 1, i) for i in range(1, NT - 1, 2)]
    from_gap = lax.ppermute(up, "tile", gaps)
    from_pair = lax.ppermute(down, "tile", pairs)
    first = exchange(message.reshape(NT, 4, W)).reshape(4 * NT, W)
    cells, ring = call(
        parent_kernel,
        (
            pltpu.VMEM((STEPS, 2 * W, ROWS * W), BF16),
            pltpu.HBM((2 * BSTR, W), F32),
        ),
        in_specs=[SM, VM, VM, VM, HB],
        out_specs=(VM, HB),
        scratch=[
            pltpu.VMEM((HALO_ROWS, W), F32),
            pltpu.VMEM((HALO_ROWS, W), F32),
            pltpu.VMEM((FLAT, W), F32),
            pltpu.VMEM((ROWS, W), F32),
            pltpu.VMEM((2 * BSTR, W), F32),
            pltpu.VMEM((2 * BSTR, W), F32),
            pltpu.VMEM((2 * BSTR, W), F32),
            pltpu.VMEM((ROWS, W), jnp.int32),
            pltpu.SemaphoreType.DMA((2,)),
        ],
        name="parent",
        flops=1 << 24,
        nbytes=4 << 20,
    )(tile, kept, from_gap, from_pair, in_hbm(terrain))

    values = call(
        gather_kernel,
        sds((PACK * NT, W), BF16),
        scratch=[pltpu.VMEM((PACK * NT, W), F32)],
        name="gather",
        flops=1 << 29,
        nbytes=3 << 20,
    )(first, cells)
    second = exchange(values.reshape(PACK // 4 * NT, 4, W)).reshape(PACK * NT, W)

    hot, base = call(
        plan_kernel,
        (sds((2, 4 * NT, 4 * NT), BF16), sds((4 * NT, W), F32)),
        in_specs=[SM, VM],
        name="plan",
        flops=1 << 28,
        nbytes=3 << 20,
    )(tile, first)

    second, hot, base = lax.optimization_barrier((second, hot, base))
    bperm = boundary_index.reshape(STEPS, 32, 4).transpose(0, 2, 1).reshape(STEPS, NT)
    edges = call(
        regroup_kernel,
        sds((8 * NT, W), BF16),
        scratch=[pltpu.VMEM((PACK * NT, W), F32), pltpu.VMEM((8 * NT, W), F32)],
        name="regroup",
        flops=1 << 26,
        nbytes=1 << 20,
    )(bperm, second)
    third = exchange(edges.reshape(NT, 8, W)).reshape(8 * NT, W)

    parent_out = call(
        last_parent_kernel,
        sds((2 * LEV, ROWS, W), F32),
        in_specs=[HB, HB],
        scratch=[
            pltpu.VMEM((2 * BSTR, W), F32),
            pltpu.VMEM((ROWS, W), jnp.int32),
            pltpu.SemaphoreType.DMA((2,)),
        ],
        name="last_parent",
        flops=1 << 22,
        nbytes=2 << 20,
    )(in_hbm(ring), in_hbm(terrain))
    third, parent_out = lax.optimization_barrier((third, parent_out))
    columns = call(
        owner_kernel,
        sds((4 * NT, W), F32),
        in_specs=[SM, VM, VM, VM, VM],
        scratch=[pltpu.VMEM((8 * NT, W), F32)],
        name="owner",
        flops=1 << 29,
        nbytes=3 << 20,
    )(tile, third, hot, base, e_mix)
    fourth = exchange(columns.reshape(NT, 4, W)).reshape(4 * NT, W)

    nest_out = call(
        nest_kernel,
        sds((4 * LEV, W), F32),
        scratch=[pltpu.VMEM((W, W), F32)] * 3,
        name="nest",
        nbytes=1 << 19,
    )(fourth)
    other = lax.ppermute(nest_out, "member", [(0, 1), (1, 0)])
    mean, variance = call(
        stats_kernel,
        (sds((LEV, 2 * W), F32), sds((LEV, 2 * W), F32)),
        name="stats",
        nbytes=1 << 19,
    )(nest_out, other)
    nest_out = nest_out.reshape(LEV, 2, 2, W).transpose(2, 0, 1, 3)
    nest_out = nest_out.reshape(nest_state.shape)
    return (parent_out.reshape(parent_state.shape), nest_out, mean, variance)


def solution(mesh):
    in_specs = (
        P("member", None, "tile", None),
        P("member", None, "tile"),
        P("tile", None),
        P(),
        P(None, "tile"),
        P(None, "tile"),
    )
    out_specs = (
        P("member", None, "tile", None),
        P("member", None, "tile"),
        P(None, "tile"),
        P(None, "tile"),
    )
    return jax.shard_map(
        on_device, mesh=mesh, in_specs=in_specs, out_specs=out_specs, check_vma=False
    )
```

```python
import functools

import jax
import jax.numpy as jnp
import numpy as np
from jax import lax
from jax.experimental import pallas as pl
from jax.experimental.pallas import tpu as pltpu
from jax.sharding import PartitionSpec as P

F32 = jnp.float32
BF16 = jnp.bfloat16
LEV = 81
STEPS = 4
NT = 128
ROWS = 8
W = 128
LPAD = 96
RING = 16
BSTR = LPAD * RING
SENT = 5
FLAT = 2 * LEV * ROWS
HALO_ROWS = 816
DIST = ((0, 1), (2, None), (3, None), (4, None))
SPLIT = 40
PACK = 12
EPACK = 6
CUT = W - LEV
L_TOP = 81
L_REQ = 86
L_INNER = 88
L_DEST = (48, 8)
HORIZ = 0.15
VERT = 0.1
DRAG = 0.1
RELAX = 0.5
IMPL = 0.8
VMEM_LIMIT = 20 * 1024 * 1024


def solve_matrix():
    n = np.full(LEV, 2.0)
    n[0] = n[-1] = 1.0
    a = np.diag(1.0 + IMPL * n)
    a -= IMPL * (np.eye(LEV, k=1) + np.eye(LEV, k=-1))
    return np.linalg.inv(a)


def padded_transpose(m):
    out = np.zeros((W, W))
    out[:LEV, :LEV] = m.T
    return out


def split3(m):
    m = np.asarray(m, np.float64)
    parts = []
    for _ in range(3):
        part = m.astype(jnp.bfloat16)
        parts.append(part)
        m = m - part.astype(np.float64)
    return parts


def constants():
    s = solve_matrix()
    power = [np.linalg.matrix_power(s, k) for k in range(STEPS + 1)]
    keep = 1.0 - RELAX
    inner = power[STEPS].T
    bound = power[STEPS].T * keep**STEPS
    send = np.zeros((2, W, 2, W))
    send[0, :LEV, 0, :SPLIT] = bound[:, :SPLIT]
    send[0, :LEV, 1, SPLIT:LEV] = bound[:, SPLIT:]
    send[1, :LEV, 0, L_INNER:] = inner[:, :SPLIT]
    send[1, :LEV, 1, L_INNER:] = inner[:, SPLIT : 2 * SPLIT]
    send[1, :LEV, 1, L_TOP] = inner[:, 2 * SPLIT]
    for part in range(2):
        for owner in range(2):
            for k in range(STEPS):
                send[part, LEV + k, owner, L_DEST[owner] + part * STEPS + k] = 1.0
    send = send.reshape(2 * W, 2 * W).astype(np.float32)
    mix = [
        padded_transpose(power[STEPS - k] * RELAX * keep ** (STEPS - 1 - k))
        for k in range(STEPS)
    ]
    edge = np.stack(
        [
            np.concatenate(split3(np.concatenate(mix[:2])), axis=1),
            np.concatenate(split3(np.concatenate(mix[2:])), axis=1),
        ]
    )
    return send, edge


def call(
    body, out_shape, in_specs=None, out_specs=None, scratch=(), name=None, flops=0, nbytes=0
):
    kwargs = {} if in_specs is None else {"in_specs": in_specs}
    if out_specs is not None:
        kwargs["out_specs"] = out_specs
    return pl.pallas_call(
        body,
        out_shape=out_shape,
        scratch_shapes=list(scratch),
        compiler_params=pltpu.CompilerParams(vmem_limit_bytes=VMEM_LIMIT),
        cost_estimate=pl.CostEstimate(
            flops=flops, bytes_accessed=nbytes, transcendentals=0
        ),
        name=name,
        **kwargs,
    )


VM = pl.BlockSpec(memory_space=pltpu.VMEM)
HB = pl.BlockSpec(memory_space=pltpu.HBM)
SM = pl.BlockSpec(memory_space=pltpu.SMEM)


def start_all(pairs, sems):
    copies = [pltpu.make_async_copy(x, y, sems.at[i]) for i, (x, y) in enumerate(pairs)]
    for copy in copies:
        copy.start()
    return copies


def halo_kernel(
    tile_ref, parent_hbm, terrain_hbm, nest_hbm, bidx_hbm, dest_hbm, mix_hbm,
    parent_ref, first_ref, second_ref, nest_ref, bidx_ref, dest_ref, mix_ref,
    terrain_ref, down_ref, up_ref, damp_ref, sems,
):
    copies = start_all(
        [
            (parent_hbm, parent_ref),
            (terrain_hbm, terrain_ref),
            (nest_hbm, nest_ref),
            (bidx_hbm, bidx_ref),
            (dest_hbm, dest_ref),
            (mix_hbm, mix_ref),
        ],
        sems,
    )
    for copy in copies[:2]:
        copy.wait()
    damp_ref[...] = DRAG * terrain_ref[...].astype(F32) / 3000.0
    for ref, rows in ((down_ref, (7, 6, 5, 4)), (up_ref, (0, 1, 2, 3))):
        ref[HALO_ROWS - 24 :, :] = jnp.zeros((24, W), F32)
        for row, (coarse, fine) in zip(rows, DIST):
            for count, base, value in (
                (2 * LEV, 0, parent_ref[pl.ds(row, 2 * LEV, stride=ROWS), :]),
                (1, 2 * LEV * SENT, damp_ref[row : row + 1, :]),
            ):
                ref[pl.ds(base + coarse, count, stride=SENT), :] = value
                if fine is not None:
                    rest = value - value.astype(BF16).astype(F32)
                    ref[pl.ds(base + fine, count, stride=SENT), :] = rest
    even = jnp.bitwise_and(tile_ref[0], 1) == 0
    down, up = down_ref[...], up_ref[...]
    first_ref[...] = jnp.where(even, down, up).astype(BF16)
    second_ref[...] = jnp.where(even, up, down).astype(BF16)
    for copy in copies[2:]:
        copy.wait()


def send_kernel(
    shift_hbm, nest_ref, bidx_ref, dest_ref, mix_ref,
    msg_ref,
    shift_ref, pad_ref, sems,
):
    copies = start_all([(shift_hbm, shift_ref)], sems)
    zeros = jnp.zeros((W - LEV + 1, W), F32)
    for b in range(2):
        for part in range(2):
            top = part * W
            pad_ref[b, top + LEV - 1 : top + W, :] = zeros
            pad_ref[b, top : top + LEV, :] = nest_ref[:, part, b, :]
            pad_ref[b, top + LEV : top + LEV + STEPS, :] = dest_ref[
                :, part * W : (part + 1) * W
            ].astype(F32)
        res = lax.dot_general(
            pad_ref[b],
            mix_ref[...],
            (((0,), (0,)), ((), ())),
            precision=lax.Precision.HIGHEST,
            preferred_element_type=F32,
        )
        for owner in range(2):
            start = b * 2 * W + owner * W
            msg_ref[start : start + W, :] = res[:, owner * W : (owner + 1) * W]
    copies[0].wait()
    lane = lax.broadcasted_iota(jnp.int32, (NT, W), 1)
    tile = lax.broadcasted_iota(jnp.int32, (NT, W), 0)
    asked = jnp.logical_or(lane == L_REQ, lane == L_REQ + 1)
    wanted = tile == L_REQ + jnp.bitwise_and(lane, 1)
    for s in range(STEPS):
        idx = bidx_ref[s : s + 1, :]
        owner = jnp.right_shift(idx, 10)
        row = jnp.bitwise_and(jnp.right_shift(idx, 7), ROWS - 1)
        col = jnp.bitwise_and(jnp.bitwise_and(idx, W - 1) + shift_ref[s], W - 1)
        mine = jnp.where(tile == owner, 1.0, 0.0).astype(BF16)
        found = []
        for value in (row + 1, col):
            value = jnp.broadcast_to(value.astype(F32), (NT, W))
            value = jnp.where(wanted, value, 0.0).astype(BF16)
            found.append(
                lax.dot_general(
                    mine, value, (((1,), (1,)), ((), ())), preferred_element_type=F32
                )
            )
        cell = (found[0] - 1.0) * W + found[1]
        rows = msg_ref[pl.ds(s, NT, stride=4), :]
        msg_ref[pl.ds(s, NT, stride=4), :] = jnp.where(asked, cell, rows)


def ring_step(read, write, level_stride, coef, own_only=False):
    row = lax.broadcasted_iota(jnp.int32, (ROWS, W), 0)
    last = row == ROWS - 1
    head = row == 0
    c0, c1, h1, v1 = coef
    chunk = 9

    def body(step, carry):
        start = step * chunk
        ends = jnp.maximum(start - 1, 0), jnp.minimum(start + chunk, LEV - 1)
        for member in range(2):
            base = member * level_stride
            column = [read(base + start + k) for k in range(chunk)]
            column = [read(base + ends[0])] + column + [read(base + ends[1])]
            for k in range(chunk):
                (d0, d1), (x0, x1), (u0, u1) = column[k : k + 3]
                f0 = pltpu.roll(x0, ROWS - 1, 0)
                f1 = pltpu.roll(x1, ROWS - 1, 0)
                g0 = pltpu.roll(x0, 1, 0)
                g1 = pltpu.roll(x1, 1, 0)
                near0 = jnp.where(last, f1, f0) + jnp.where(head, g1, g0)
                near0 = near0 + (pltpu.roll(x0, 1, 1) + pltpu.roll(x0, W - 1, 1))
                y0 = c0 * x0 + HORIZ * near0 + VERT * (d0 + u0)
                if own_only:
                    write(member, start + k, y0, None)
                    continue
                near1 = jnp.where(last, f0, f1) + jnp.where(head, g0, g1)
                near1 = near1 + (pltpu.roll(x1, 1, 1) + pltpu.roll(x1, W - 1, 1))
                y1 = c1 * x1 + h1 * near1 + v1 * (d1 + u1)
                write(member, start + k, y0, y1)
        return carry

    lax.fori_loop(0, LEV // chunk, body, 0)


def parent_kernel(
    tile_ref, parent_ref, second_ref, first_ref, terrain_hbm,
    cells_ref, ring_hbm,
    next_ref, prev_ref, halo_ref, damp_ref, a_ref, b_ref, ring_ref, terrain_ref, sems,
):
    copies = start_all([(terrain_hbm, terrain_ref)], sems)
    store = pltpu.make_async_copy(ring_ref, ring_hbm, sems.at[1])
    tile = tile_ref[0]
    even = jnp.bitwise_and(tile, 1) == 0
    first, second = first_ref[...].astype(F32), second_ref[...].astype(F32)
    next_ref[...] = jnp.where(even, first, second)
    prev_ref[...] = jnp.where(even, second, first)
    for ref, rows in ((next_ref, (0, 1, 2, 3)), (prev_ref, (7, 6, 5, 4))):
        for row, (coarse, fine) in zip(rows, DIST):
            for count, base, out in ((2 * LEV, 0, halo_ref), (1, 2 * LEV * SENT, damp_ref)):
                value = ref[pl.ds(base + coarse, count, stride=SENT), :]
                if fine is not None:
                    value = value + ref[pl.ds(base + fine, count, stride=SENT), :]
                out[pl.ds(row, count, stride=ROWS), :] = value
    copies[0].wait()
    damping = DRAG * terrain_ref[...].astype(F32) / 3000.0
    pads = jnp.zeros(((LPAD - LEV) * RING, W), F32)
    for ref in (a_ref, b_ref, ring_ref):
        for member in range(2):
            top = member * BSTR + LEV * RING
            ref[top : top + (LPAD - LEV) * RING, :] = pads
    for s in range(STEPS):
        for member in range(2):
            start = LPAD if s else LEV - 1
            cells_ref[s, member * W + start : (member + 1) * W, :] = jnp.zeros(
                (W - start, ROWS * W), BF16
            )
    row = lax.broadcasted_iota(jnp.int32, (ROWS, W), 0)
    south = jnp.where(tile < NT - 1, 1.0, 0.0).astype(F32)
    north = jnp.where(tile > 0, 1.0, 0.0).astype(F32)
    valid = jnp.where(row < 4, south, north)
    stay = 1.0 - 4.0 * HORIZ - 2.0 * VERT
    coef = (stay - damping, (stay - damp_ref[...]) * valid, HORIZ * valid, VERT * valid)

    def emit(s, ref, count, stride):
        for member in range(2):
            for y in range(ROWS):
                start = member * count * stride + y
                rows = ref[pl.ds(start, count, stride=stride), :]
                cells_ref[s, member * W : member * W + count, y * W : (y + 1) * W] = (
                    rows.astype(BF16)
                )

    def read_first(index):
        base = pl.multiple_of(index * ROWS, ROWS)
        return parent_ref[pl.ds(base, ROWS), :], halo_ref[pl.ds(base, ROWS), :]

    emit(0, parent_ref, LEV, ROWS)
    read, stride = read_first, LEV
    for s, dst in zip(range(1, STEPS), (a_ref, b_ref, ring_ref)):

        def write(member, level, y0, y1, dst=dst):
            base = pl.multiple_of((member * LPAD + level) * RING, RING)
            dst[pl.ds(base, ROWS), :] = y0
            dst[pl.ds(base + ROWS, ROWS), :] = y1

        ring_step(read, write, stride, coef)
        if s == STEPS - 1:
            store.start()
        emit(s, dst, LPAD, RING)

        def read(index, src=dst):
            base = pl.multiple_of(index * RING, RING)
            return src[pl.ds(base, ROWS), :], src[pl.ds(base + ROWS, ROWS), :]

        stride = LPAD
    store.wait()


def last_parent_kernel(ring_hbm, terrain_hbm, out_ref, ring_ref, terrain_ref, sems):
    for copy in start_all([(ring_hbm, ring_ref), (terrain_hbm, terrain_ref)], sems):
        copy.wait()
    damping = DRAG * terrain_ref[...].astype(F32) / 3000.0
    stay = 1.0 - 4.0 * HORIZ - 2.0 * VERT

    def read(index):
        base = pl.multiple_of(index * RING, RING)
        return ring_ref[pl.ds(base, ROWS), :], ring_ref[pl.ds(base + ROWS, ROWS), :]

    def write(member, level, y0, y1):
        out_ref[member * LEV + level] = y0

    ring_step(read, write, LPAD, (stay - damping, None, None, None), own_only=True)


def gather_kernel(got_ref, cells_ref, out_ref, scr_ref):
    cell = lax.broadcasted_iota(jnp.int32, (NT, ROWS * W), 1).astype(F32)
    lane = lax.broadcasted_iota(jnp.int32, (NT, W), 1)
    rows = {}
    for s in range(STEPS):
        asked = got_ref[pl.ds(s, NT, stride=4), :]
        hot = [
            jnp.where(cell == asked[:, L_REQ + c : L_REQ + c + 1], 1.0, 0.0).astype(BF16)
            for c in range(2)
        ]
        hot = jnp.concatenate(hot, axis=0)
        res = lax.dot_general(
            hot, cells_ref[s], (((1,), (1,)), ((), ())), preferred_element_type=F32
        )
        for b in range(2):
            for c in range(2):
                rows[b * 8 + s * 2 + c] = res[c * W : (c + 1) * W, b * W : (b + 1) * W]
    for r in range(PACK):
        row = rows[r]
        if r < 8:
            extra = rows[PACK + r // 2]
            if r % 2 == 0:
                row = row + pltpu.roll(jnp.where(lane < CUT, extra, 0.0), LEV, 1)
            else:
                row = row + pltpu.roll(jnp.where(lane < CUT, 0.0, extra), LEV - CUT, 1)
        scr_ref[pl.ds(r, NT, stride=PACK), :] = row
    out_ref[...] = scr_ref[...].astype(BF16)


def regroup_kernel(bperm_ref, got_ref, out_ref, scr_ref, scr2_ref):
    scr_ref[...] = got_ref[...].astype(F32)
    low = lax.broadcasted_iota(jnp.int32, (NT, W), 1) < CUT

    def row(r):
        if r < PACK:
            return scr_ref[pl.ds(r, NT, stride=PACK), :]
        first = pltpu.roll(row(2 * (r - PACK)), W - LEV, 1)
        second = pltpu.roll(row(2 * (r - PACK) + 1), W - LEV + CUT, 1)
        return jnp.where(low, first, second)

    sub = lax.broadcasted_iota(jnp.int32, (2 * NT, W), 0)
    lane = lax.broadcasted_iota(jnp.int32, (2 * NT, W), 1)
    parity = jnp.bitwise_and(jnp.right_shift(lane, 5), 1)
    target = sub - parity * NT
    found = {}
    for s in range(STEPS):
        owner = jnp.right_shift(bperm_ref[s : s + 1, :], 10)
        hot = jnp.where(target == owner, 1.0, 0.0).astype(BF16)
        values = jnp.concatenate(
            [
                jnp.concatenate(
                    [row(b * 8 + s * 2 + c) for b in range(2)],
                    axis=1,
                )
                for c in range(2)
            ],
            axis=0,
        ).astype(BF16)
        res = lax.dot_general(
            hot, values, (((0,), (0,)), ((), ())), preferred_element_type=F32
        )
        for b in range(2):
            for j in range(4):
                found[b, s // 2, (s % 2) * 4 + j] = res[
                    j * 32 : (j + 1) * 32, b * W : (b + 1) * W
                ]
    lane = lax.broadcasted_iota(jnp.int32, (32, W), 1)
    for b in range(2):
        for half in range(2):
            for r in range(EPACK):
                value = found[b, half, r]
                if r < 4:
                    extra = found[b, half, EPACK + r // 2]
                    turn = LEV if r % 2 == 0 else LEV - CUT
                    value = jnp.where(lane < LEV, value, pltpu.roll(extra, turn, 1))
                start = (b * 64 + half * 32) * EPACK + r
                scr2_ref[pl.ds(start, 32, stride=EPACK), :] = value
    out_ref[...] = scr2_ref[...].astype(BF16)


def plan_kernel(tile_ref, got_ref, hot_ref, base_ref):
    late = jnp.bitwise_and(jnp.right_shift(tile_ref[0], 5), 1) == 1
    n = 4 * NT
    turned = [got_ref[pl.ds(j, NT, stride=4), :].T for j in range(4)]
    sub = lax.broadcasted_iota(jnp.int32, (n, n), 0)

    def pick(early_value, late_value):
        return jnp.where(late, late_value, early_value)

    def one_hot(row):
        return jnp.where(sub == row, 1.0, 0.0).astype(BF16)

    def dest(part, s):
        k = part * STEPS + s
        row = jnp.concatenate(
            [
                pick(
                    t[L_DEST[0] + k : L_DEST[0] + k + 1, :],
                    t[L_DEST[1] + k : L_DEST[1] + k + 1, :],
                )
                for t in turned
            ],
            axis=1,
        )
        row = (row + 0.5).astype(jnp.int32)
        return jnp.right_shift(row, 8), jnp.bitwise_and(row, 3)

    def finals(part):
        tile_to, slot_to = dest(part, STEPS - 1)
        rows = {STEPS - 1: tile_to * 4 + slot_to}
        for s in range(STEPS - 2, -1, -1):
            mid_tile, mid_slot = dest(part, s)
            move = one_hot(mid_slot * NT + mid_tile)
            later = jnp.concatenate(
                [
                    jnp.broadcast_to(tile_to, (8, n)),
                    jnp.broadcast_to(slot_to, (8, n)),
                ],
                axis=0,
            )
            both = jnp.dot(
                later.astype(F32).astype(BF16), move, preferred_element_type=F32
            )
            tile_to = both[0:1, :].astype(jnp.int32)
            slot_to = both[8:9, :].astype(jnp.int32)
            rows[s] = tile_to * 4 + slot_to
        return rows

    columns = jnp.concatenate(
        [got_ref[pl.ds(j, NT, stride=4), :] for j in range(4)], axis=0
    )
    parts = []
    for _ in range(3):
        part = columns.astype(BF16)
        parts.append(part)
        columns = columns - part.astype(F32)
    parts = jnp.concatenate(parts, axis=1)

    def moved(row):
        res = jnp.dot(one_hot(row), parts, preferred_element_type=F32)
        return res[:, :W] + (res[:, W : 2 * W] + res[:, 2 * W :])

    bound = finals(0)
    hot_ref[0] = one_hot(pick(bound[0], bound[2]))
    hot_ref[1] = one_hot(pick(bound[1], bound[3]))
    outer = moved(bound[0])
    inner = moved(finals(1)[0])
    lane = lax.broadcasted_iota(jnp.int32, (n, W), 1)
    low = pick(0, SPLIT)
    high = pick(SPLIT, LEV)
    extra = pick(W, L_TOP)
    is_inner = jnp.logical_or(lane >= L_INNER, lane == extra)
    is_outer = jnp.logical_and(lane >= low, lane < high)
    base_ref[...] = jnp.where(is_outer, outer, jnp.where(is_inner, inner, 0.0))


def owner_kernel(tile_ref, got_ref, hot_ref, base_ref, mix_ref, out_ref, scr_ref):
    late = jnp.bitwise_and(jnp.right_shift(tile_ref[0], 5), 1)
    scr_ref[...] = got_ref[...].astype(F32)
    low = lax.broadcasted_iota(jnp.int32, (NT, W), 1) < CUT

    def row(r):
        if r < EPACK:
            return scr_ref[pl.ds(r, NT, stride=EPACK), :]
        first = pltpu.roll(row(2 * (r - EPACK)), W - LEV, 1)
        second = pltpu.roll(row(2 * (r - EPACK) + 1), W - LEV + CUT, 1)
        return jnp.where(low, first, second)

    moved = []
    for s in range(2):
        edge = jnp.concatenate([row(s * 4 + j) for j in range(4)], axis=0).astype(BF16)
        moved.append(jnp.dot(hot_ref[s], edge, preferred_element_type=F32).astype(BF16))
    total = jnp.dot(
        jnp.concatenate(moved, axis=1), mix_ref[late], preferred_element_type=F32
    )
    out_ref[...] = base_ref[...] + (
        total[:, :W] + (total[:, W : 2 * W] + total[:, 2 * W :])
    )


def nest_kernel(got_ref, out_ref, sum_ref, early_ref, late_ref):
    for b in range(2):
        early = got_ref[b * 2 * W : b * 2 * W + W, :]
        late = got_ref[b * 2 * W + W : (b + 1) * 2 * W, :]
        sum_ref[...] = (early + late).T
        early_ref[...] = early.T
        late_ref[...] = late.T
        out_ref[pl.ds(b, LEV, stride=4), :] = sum_ref[:LEV, :]
        inner = 2 + b
        out_ref[pl.ds(inner, SPLIT, stride=4), :] = early_ref[L_INNER:, :]
        out_ref[pl.ds(inner + 4 * SPLIT, SPLIT, stride=4), :] = late_ref[L_INNER:, :]
        top = inner + 8 * SPLIT
        out_ref[top : top + 1, :] = late_ref[L_TOP : L_TOP + 1, :]


def stats_kernel(own_ref, other_ref, mean_ref, var_ref):
    for half in range(2):
        a0, a1, b0, b1 = (
            ref[pl.ds(half * 2 + b, LEV, stride=4), :]
            for ref in (own_ref, other_ref)
            for b in range(2)
        )
        lanes = slice(half * W, (half + 1) * W)
        mean = ((a0 + a1) + (b0 + b1)) / 4.0
        mean_ref[:, lanes] = mean
        own = (a0 - mean) * (a0 - mean) + (a1 - mean) * (a1 - mean)
        other = (b0 - mean) * (b0 - mean) + (b1 - mean) * (b1 - mean)
        var_ref[:, lanes] = (own + other) / 4.0


def in_hbm(x):
    return pltpu.with_memory_space_constraint(x, pltpu.HBM)


def exchange(x):
    return lax.all_to_all(x, "tile", split_axis=0, concat_axis=0, tiled=True)


def on_device(parent_state, nest_state, terrain, shift_x, boundary_index, reloc_dest):
    q_mix, e_mix = constants()
    q_mix, e_mix = jnp.asarray(q_mix), jnp.asarray(e_mix)
    sds = jax.ShapeDtypeStruct
    tile = lax.axis_index("tile").astype(jnp.int32).reshape(1)
    parent = parent_state.reshape(FLAT, W)

    nest = nest_state.reshape(2, LEV, 2, W).transpose(1, 2, 0, 3)
    kept, down, up, nest, bidx, dest, q_mix = call(
        halo_kernel,
        (
            pltpu.VMEM((FLAT, W), F32),
            sds((HALO_ROWS, W), BF16),
            sds((HALO_ROWS, W), BF16),
            pltpu.VMEM((LEV, 2, 2, W), F32),
            pltpu.VMEM((STEPS, NT), jnp.int32),
            pltpu.VMEM((STEPS, 2 * W), jnp.int32),
            pltpu.VMEM((2 * W, 2 * W), F32),
        ),
        in_specs=[SM, HB, HB, HB, HB, HB, HB],
        scratch=[
            pltpu.VMEM((ROWS, W), jnp.int32),
            pltpu.VMEM((HALO_ROWS, W), F32),
            pltpu.VMEM((HALO_ROWS, W), F32),
            pltpu.VMEM((ROWS, W), F32),
            pltpu.SemaphoreType.DMA((6,)),
        ],
        name="halo",
        nbytes=1 << 20,
    )(
        tile,
        in_hbm(parent),
        in_hbm(terrain),
        in_hbm(nest),
        in_hbm(boundary_index),
        in_hbm(reloc_dest),
        in_hbm(q_mix),
    )
    message = call(
        send_kernel,
        sds((4 * NT, W), F32),
        in_specs=[HB, VM, VM, VM, VM],
        scratch=[
            pltpu.SMEM((STEPS,), jnp.int32),
            pltpu.VMEM((2, 2 * W, W), F32),
            pltpu.SemaphoreType.DMA((1,)),
        ],
        name="send",
        nbytes=64 << 20,
    )(in_hbm(shift_x), nest, bidx, dest, q_mix)
    pairs = [(i, i + 1) for i in range(0, NT, 2)] + [(i + 1, i) for i in range(0, NT, 2)]
    gaps = [(i, i + 1) for i in range(1, NT - 1, 2)]
    gaps = gaps + [(i + 1, i) for i in range(1, NT - 1, 2)]
    from_gap = lax.ppermute(up, "tile", gaps)
    from_pair = lax.ppermute(down, "tile", pairs)
    first = exchange(message.reshape(NT, 4, W)).reshape(4 * NT, W)
    cells, ring = call(
        parent_kernel,
        (
            pltpu.VMEM((STEPS, 2 * W, ROWS * W), BF16),
            pltpu.HBM((2 * BSTR, W), F32),
        ),
        in_specs=[SM, VM, VM, VM, HB],
        out_specs=(VM, HB),
        scratch=[
            pltpu.VMEM((HALO_ROWS, W), F32),
            pltpu.VMEM((HALO_ROWS, W), F32),
            pltpu.VMEM((FLAT, W), F32),
            pltpu.VMEM((ROWS, W), F32),
            pltpu.VMEM((2 * BSTR, W), F32),
            pltpu.VMEM((2 * BSTR, W), F32),
            pltpu.VMEM((2 * BSTR, W), F32),
            pltpu.VMEM((ROWS, W), jnp.int32),
            pltpu.SemaphoreType.DMA((2,)),
        ],
        name="parent",
        flops=1 << 33,
        nbytes=1 << 27,
    )(tile, kept, from_gap, from_pair, in_hbm(terrain))

    values = call(
        gather_kernel,
        sds((PACK * NT, W), BF16),
        scratch=[pltpu.VMEM((PACK * NT, W), F32)],
        name="gather",
        flops=1 << 29,
        nbytes=3 << 20,
    )(first, cells)
    second = exchange(values.reshape(PACK // 4 * NT, 4, W)).reshape(PACK * NT, W)

    hot, base = call(
        plan_kernel,
        (sds((2, 4 * NT, 4 * NT), BF16), sds((4 * NT, W), F32)),
        in_specs=[SM, VM],
        name="plan",
        flops=1 << 28,
        nbytes=3 << 20,
    )(tile, first)

    second, hot, base = lax.optimization_barrier((second, hot, base))
    bperm = boundary_index.reshape(STEPS, 32, 4).transpose(0, 2, 1).reshape(STEPS, NT)
    edges = call(
        regroup_kernel,
        sds((EPACK * NT, W), BF16),
        scratch=[pltpu.VMEM((PACK * NT, W), F32), pltpu.VMEM((EPACK * NT, W), F32)],
        name="regroup",
        flops=1 << 26,
        nbytes=1 << 20,
    )(bperm, second)
    third = exchange(edges.reshape(EPACK // 2 * NT, 2, W)).reshape(EPACK * NT, W)

    parent_out = call(
        last_parent_kernel,
        sds((2 * LEV, ROWS, W), F32),
        in_specs=[HB, HB],
        scratch=[
            pltpu.VMEM((2 * BSTR, W), F32),
            pltpu.VMEM((ROWS, W), jnp.int32),
            pltpu.SemaphoreType.DMA((2,)),
        ],
        name="last_parent",
        flops=1 << 22,
        nbytes=2 << 20,
    )(in_hbm(ring), in_hbm(terrain))
    third, parent_out = lax.optimization_barrier((third, parent_out))
    columns = call(
        owner_kernel,
        sds((4 * NT, W), F32),
        in_specs=[SM, VM, VM, VM, VM],
        scratch=[pltpu.VMEM((EPACK * NT, W), F32)],
        name="owner",
        flops=1 << 29,
        nbytes=3 << 20,
    )(tile, third, hot, base, e_mix)
    fourth = exchange(columns.reshape(NT, 4, W)).reshape(4 * NT, W)

    nest_out = call(
        nest_kernel,
        sds((4 * LEV, W), F32),
        scratch=[pltpu.VMEM((W, W), F32)] * 3,
        name="nest",
        nbytes=1 << 19,
    )(fourth)
    other = lax.ppermute(nest_out, "member", [(0, 1), (1, 0)])
    mean, variance = call(
        stats_kernel,
        (sds((LEV, 2 * W), F32), sds((LEV, 2 * W), F32)),
        name="stats",
        nbytes=1 << 19,
    )(nest_out, other)
    nest_out = nest_out.reshape(LEV, 2, 2, W).transpose(2, 0, 1, 3)
    nest_out = nest_out.reshape(nest_state.shape)
    return (parent_out.reshape(parent_state.shape), nest_out, mean, variance)


def solution(mesh):
    in_specs = (
        P("member", None, "tile", None),
        P("member", None, "tile"),
        P("tile", None),
        P(),
        P(None, "tile"),
        P(None, "tile"),
    )
    out_specs = (
        P("member", None, "tile", None),
        P("member", None, "tile"),
        P(None, "tile"),
        P(None, "tile"),
    )
    return jax.shard_map(
        on_device, mesh=mesh, in_specs=in_specs, out_specs=out_specs, check_vma=False
    )
```

```python
import functools

import jax
import jax.numpy as jnp
import numpy as np
from jax import lax
from jax.experimental import pallas as pl
from jax.experimental.pallas import tpu as pltpu
from jax.sharding import PartitionSpec as P

F32 = jnp.float32
BF16 = jnp.bfloat16
LEV = 81
STEPS = 4
NT = 128
ROWS = 8
W = 128
LPAD = 96
RING = 16
BSTR = LPAD * RING
SENT = 6
FLAT = 2 * LEV * ROWS
HALO_ROWS = 992
DIST = ((0, 1), (2, 3), (4, None), (5, None))
SPLIT = 40
PACK = 12
EPACK = 6
CUT = W - LEV
L_TOP = 81
L_REQ = 86
L_INNER = 88
L_DEST = (48, 8)
HORIZ = 0.15
VERT = 0.1
DRAG = 0.1
RELAX = 0.5
IMPL = 0.8
VMEM_LIMIT = 20 * 1024 * 1024


def solve_matrix():
    n = np.full(LEV, 2.0)
    n[0] = n[-1] = 1.0
    a = np.diag(1.0 + IMPL * n)
    a -= IMPL * (np.eye(LEV, k=1) + np.eye(LEV, k=-1))
    return np.linalg.inv(a)


def padded_transpose(m):
    out = np.zeros((W, W))
    out[:LEV, :LEV] = m.T
    return out


def split3(m):
    m = np.asarray(m, np.float64)
    parts = []
    for _ in range(3):
        part = m.astype(jnp.bfloat16)
        parts.append(part)
        m = m - part.astype(np.float64)
    return parts


def constants():
    s = solve_matrix()
    power = [np.linalg.matrix_power(s, k) for k in range(STEPS + 1)]
    keep = 1.0 - RELAX
    inner = power[STEPS].T
    bound = power[STEPS].T * keep**STEPS
    send = np.zeros((2, W, 2, W))
    send[0, :LEV, 0, :SPLIT] = bound[:, :SPLIT]
    send[0, :LEV, 1, SPLIT:LEV] = bound[:, SPLIT:]
    send[1, :LEV, 0, L_INNER:] = inner[:, :SPLIT]
    send[1, :LEV, 1, L_INNER:] = inner[:, SPLIT : 2 * SPLIT]
    send[1, :LEV, 1, L_TOP] = inner[:, 2 * SPLIT]
    for part in range(2):
        for owner in range(2):
            for k in range(STEPS):
                send[part, LEV + k, owner, L_DEST[owner] + part * STEPS + k] = 1.0
    coarse, fine, _ = split3(send.reshape(2 * W, 2 * W))
    send = np.concatenate([coarse, coarse, fine])
    mix = [
        padded_transpose(power[STEPS - k] * RELAX * keep ** (STEPS - 1 - k))
        for k in range(STEPS)
    ]
    edge = np.stack(
        [
            np.concatenate(split3(np.concatenate(mix[:2])), axis=1),
            np.concatenate(split3(np.concatenate(mix[2:])), axis=1),
        ]
    )
    return send, edge


def call(
    body, out_shape, in_specs=None, out_specs=None, scratch=(), name=None, flops=0, nbytes=0
):
    kwargs = {} if in_specs is None else {"in_specs": in_specs}
    if out_specs is not None:
        kwargs["out_specs"] = out_specs
    return pl.pallas_call(
        body,
        out_shape=out_shape,
        scratch_shapes=list(scratch),
        compiler_params=pltpu.CompilerParams(vmem_limit_bytes=VMEM_LIMIT),
        cost_estimate=pl.CostEstimate(
            flops=flops, bytes_accessed=nbytes, transcendentals=0
        ),
        name=name,
        **kwargs,
    )


VM = pl.BlockSpec(memory_space=pltpu.VMEM)
HB = pl.BlockSpec(memory_space=pltpu.HBM)
SM = pl.BlockSpec(memory_space=pltpu.SMEM)


def start_all(pairs, sems):
    copies = [pltpu.make_async_copy(x, y, sems.at[i]) for i, (x, y) in enumerate(pairs)]
    for copy in copies:
        copy.start()
    return copies


def halo_kernel(
    tile_ref, parent_hbm, terrain_hbm, nest_hbm, bidx_hbm, dest_hbm, mix_hbm,
    parent_ref, first_ref, second_ref, nest_ref, bidx_ref, dest_ref, mix_ref,
    terrain_ref, down_ref, up_ref, damp_ref, sems,
):
    copies = start_all(
        [
            (parent_hbm, parent_ref),
            (terrain_hbm, terrain_ref),
            (bidx_hbm, bidx_ref),
            (dest_hbm, dest_ref),
            (mix_hbm, mix_ref),
        ]
        + [
            (nest_hbm.at[:, part, b, :], nest_ref.at[b * 2 + part])
            for b in range(2)
            for part in range(2)
        ],
        sems,
    )
    for copy in copies[:2]:
        copy.wait()
    damp_ref[...] = DRAG * terrain_ref[...].astype(F32) / 3000.0
    for ref, rows in ((down_ref, (7, 6, 5, 4)), (up_ref, (0, 1, 2, 3))):
        ref[HALO_ROWS - 24 :, :] = jnp.zeros((24, W), F32)
        for row, (coarse, fine) in zip(rows, DIST):
            for count, base, value in (
                (2 * LEV, 0, parent_ref[pl.ds(row, 2 * LEV, stride=ROWS), :]),
                (1, 2 * LEV * SENT, damp_ref[row : row + 1, :]),
            ):
                ref[pl.ds(base + coarse, count, stride=SENT), :] = value
                if fine is not None:
                    rest = value - value.astype(BF16).astype(F32)
                    ref[pl.ds(base + fine, count, stride=SENT), :] = rest
    even = jnp.bitwise_and(tile_ref[0], 1) == 0
    down, up = down_ref[...], up_ref[...]
    first_ref[...] = jnp.where(even, down, up).astype(BF16)
    second_ref[...] = jnp.where(even, up, down).astype(BF16)
    for copy in copies[2:]:
        copy.wait()


def send_kernel(
    shift_hbm, nest_ref, bidx_ref, dest_ref, mix_ref,
    msg_ref,
    shift_ref, pad_ref, sems,
):
    copies = start_all([(shift_hbm, shift_ref)], sems)
    zeros = jnp.zeros((W - LEV + 1, W), F32)
    for b in range(2):
        for part in range(2):
            top = part * W
            pad_ref[b, top + LEV - 1 : top + W, :] = zeros
            pad_ref[b, top : top + LEV, :] = nest_ref[b * 2 + part]
            pad_ref[b, top + LEV : top + LEV + STEPS, :] = dest_ref[
                :, part * W : (part + 1) * W
            ].astype(F32)
        value = pad_ref[b]
        coarse = value.astype(BF16)
        fine = (value - coarse.astype(F32)).astype(BF16)
        res = lax.dot_general(
            jnp.concatenate([coarse, fine, coarse], axis=0),
            mix_ref[...],
            (((0,), (0,)), ((), ())),
            preferred_element_type=F32,
        )
        for owner in range(2):
            start = b * 2 * W + owner * W
            msg_ref[start : start + W, :] = res[:, owner * W : (owner + 1) * W]
    copies[0].wait()
    lane = lax.broadcasted_iota(jnp.int32, (NT, W), 1)
    tile = lax.broadcasted_iota(jnp.int32, (NT, W), 0)
    asked = jnp.logical_or(lane == L_REQ, lane == L_REQ + 1)
    wanted = tile == L_REQ + jnp.bitwise_and(lane, 1)
    for s in range(STEPS):
        idx = bidx_ref[s : s + 1, :]
        owner = jnp.right_shift(idx, 10)
        row = jnp.bitwise_and(jnp.right_shift(idx, 7), ROWS - 1)
        col = jnp.bitwise_and(jnp.bitwise_and(idx, W - 1) + shift_ref[s], W - 1)
        mine = jnp.where(tile == owner, 1.0, 0.0).astype(BF16)
        found = []
        for value in (row + 1, col):
            value = jnp.broadcast_to(value.astype(F32), (NT, W))
            value = jnp.where(wanted, value, 0.0).astype(BF16)
            found.append(
                lax.dot_general(
                    mine, value, (((1,), (1,)), ((), ())), preferred_element_type=F32
                )
            )
        cell = (found[0] - 1.0) * W + found[1]
        rows = msg_ref[pl.ds(s, NT, stride=4), :]
        msg_ref[pl.ds(s, NT, stride=4), :] = jnp.where(asked, cell, rows)


def ring_step(read, write, level_stride, coef, own_only=False):
    row = lax.broadcasted_iota(jnp.int32, (ROWS, W), 0)
    last = row == ROWS - 1
    head = row == 0
    c0, c1, h1, v1 = coef
    chunk = 9

    def body(step, carry):
        start = step * chunk
        ends = jnp.maximum(start - 1, 0), jnp.minimum(start + chunk, LEV - 1)
        for member in range(2):
            base = member * level_stride
            column = [read(base + start + k) for k in range(chunk)]
            column = [read(base + ends[0])] + column + [read(base + ends[1])]
            for k in range(chunk):
                (d0, d1), (x0, x1), (u0, u1) = column[k : k + 3]
                f0 = pltpu.roll(x0, ROWS - 1, 0)
                f1 = pltpu.roll(x1, ROWS - 1, 0)
                g0 = pltpu.roll(x0, 1, 0)
                g1 = pltpu.roll(x1, 1, 0)
                near0 = jnp.where(last, f1, f0) + jnp.where(head, g1, g0)
                near0 = near0 + (pltpu.roll(x0, 1, 1) + pltpu.roll(x0, W - 1, 1))
                y0 = c0 * x0 + HORIZ * near0 + VERT * (d0 + u0)
                if own_only:
                    write(member, start + k, y0, None)
                    continue
                near1 = jnp.where(last, f0, f1) + jnp.where(head, g0, g1)
                near1 = near1 + (pltpu.roll(x1, 1, 1) + pltpu.roll(x1, W - 1, 1))
                y1 = c1 * x1 + h1 * near1 + v1 * (d1 + u1)
                write(member, start + k, y0, y1)
        return carry

    lax.fori_loop(0, LEV // chunk, body, 0)


def parent_kernel(
    tile_ref, parent_ref, second_ref, first_ref, terrain_hbm,
    cells_ref, ring_hbm,
    next_ref, prev_ref, halo_ref, damp_ref, a_ref, b_ref, ring_ref, terrain_ref, sems,
):
    copies = start_all([(terrain_hbm, terrain_ref)], sems)
    store = pltpu.make_async_copy(ring_ref, ring_hbm, sems.at[1])
    tile = tile_ref[0]
    even = jnp.bitwise_and(tile, 1) == 0
    first, second = first_ref[...].astype(F32), second_ref[...].astype(F32)
    next_ref[...] = jnp.where(even, first, second)
    prev_ref[...] = jnp.where(even, second, first)
    for ref, rows in ((next_ref, (0, 1, 2, 3)), (prev_ref, (7, 6, 5, 4))):
        for row, (coarse, fine) in zip(rows, DIST):
            for count, base, out in ((2 * LEV, 0, halo_ref), (1, 2 * LEV * SENT, damp_ref)):
                value = ref[pl.ds(base + coarse, count, stride=SENT), :]
                if fine is not None:
                    value = value + ref[pl.ds(base + fine, count, stride=SENT), :]
                out[pl.ds(row, count, stride=ROWS), :] = value
    copies[0].wait()
    damping = DRAG * terrain_ref[...].astype(F32) / 3000.0
    pads = jnp.zeros(((LPAD - LEV) * RING, W), F32)
    for ref in (a_ref, b_ref, ring_ref):
        for member in range(2):
            top = member * BSTR + LEV * RING
            ref[top : top + (LPAD - LEV) * RING, :] = pads
    for s in range(STEPS):
        for member in range(2):
            start = LPAD if s else LEV - 1
            cells_ref[s, member * W + start : (member + 1) * W, :] = jnp.zeros(
                (W - start, ROWS * W), BF16
            )
    row = lax.broadcasted_iota(jnp.int32, (ROWS, W), 0)
    south = jnp.where(tile < NT - 1, 1.0, 0.0).astype(F32)
    north = jnp.where(tile > 0, 1.0, 0.0).astype(F32)
    valid = jnp.where(row < 4, south, north)
    stay = 1.0 - 4.0 * HORIZ - 2.0 * VERT
    coef = (stay - damping, (stay - damp_ref[...]) * valid, HORIZ * valid, VERT * valid)

    def emit(s, ref, count, stride):
        for member in range(2):
            for y in range(ROWS):
                start = member * count * stride + y
                rows = ref[pl.ds(start, count, stride=stride), :]
                cells_ref[s, member * W : member * W + count, y * W : (y + 1) * W] = (
                    rows.astype(BF16)
                )

    def read_first(index):
        base = pl.multiple_of(index * ROWS, ROWS)
        return parent_ref[pl.ds(base, ROWS), :], halo_ref[pl.ds(base, ROWS), :]

    emit(0, parent_ref, LEV, ROWS)
    read, stride = read_first, LEV
    for s, dst in zip(range(1, STEPS), (a_ref, b_ref, ring_ref)):

        def write(member, level, y0, y1, dst=dst):
            base = pl.multiple_of((member * LPAD + level) * RING, RING)
            dst[pl.ds(base, ROWS), :] = y0
            dst[pl.ds(base + ROWS, ROWS), :] = y1

        ring_step(read, write, stride, coef)
        if s == STEPS - 1:
            store.start()
        emit(s, dst, LPAD, RING)

        def read(index, src=dst):
            base = pl.multiple_of(index * RING, RING)
            return src[pl.ds(base, ROWS), :], src[pl.ds(base + ROWS, ROWS), :]

        stride = LPAD
    store.wait()


def last_parent_kernel(ring_hbm, terrain_hbm, out_ref, ring_ref, terrain_ref, sems):
    for copy in start_all([(ring_hbm, ring_ref), (terrain_hbm, terrain_ref)], sems):
        copy.wait()
    damping = DRAG * terrain_ref[...].astype(F32) / 3000.0
    stay = 1.0 - 4.0 * HORIZ - 2.0 * VERT

    def read(index):
        base = pl.multiple_of(index * RING, RING)
        return ring_ref[pl.ds(base, ROWS), :], ring_ref[pl.ds(base + ROWS, ROWS), :]

    def write(member, level, y0, y1):
        out_ref[member * LEV + level] = y0

    ring_step(read, write, LPAD, (stay - damping, None, None, None), own_only=True)


def gather_kernel(got_ref, cells_ref, out_ref, scr_ref):
    cell = lax.broadcasted_iota(jnp.int32, (NT, ROWS * W), 1).astype(F32)
    lane = lax.broadcasted_iota(jnp.int32, (NT, W), 1)
    rows = {}
    for s in range(STEPS):
        asked = got_ref[pl.ds(s, NT, stride=4), :]
        hot = [
            jnp.where(cell == asked[:, L_REQ + c : L_REQ + c + 1], 1.0, 0.0).astype(BF16)
            for c in range(2)
        ]
        hot = jnp.concatenate(hot, axis=0)
        res = lax.dot_general(
            hot, cells_ref[s], (((1,), (1,)), ((), ())), preferred_element_type=F32
        )
        for b in range(2):
            for c in range(2):
                rows[b * 8 + s * 2 + c] = res[c * W : (c + 1) * W, b * W : (b + 1) * W]
    for r in range(PACK):
        row = rows[r]
        if r < 8:
            extra = rows[PACK + r // 2]
            if r % 2 == 0:
                row = row + pltpu.roll(jnp.where(lane < CUT, extra, 0.0), LEV, 1)
            else:
                row = row + pltpu.roll(jnp.where(lane < CUT, 0.0, extra), LEV - CUT, 1)
        scr_ref[pl.ds(r, NT, stride=PACK), :] = row
    out_ref[...] = scr_ref[...].astype(BF16)


def regroup_kernel(bperm_ref, got_ref, out_ref, scr_ref, scr2_ref):
    scr_ref[...] = got_ref[...].astype(F32)
    low = lax.broadcasted_iota(jnp.int32, (NT, W), 1) < CUT

    def row(r):
        if r < PACK:
            return scr_ref[pl.ds(r, NT, stride=PACK), :]
        first = pltpu.roll(row(2 * (r - PACK)), W - LEV, 1)
        second = pltpu.roll(row(2 * (r - PACK) + 1), W - LEV + CUT, 1)
        return jnp.where(low, first, second)

    sub = lax.broadcasted_iota(jnp.int32, (2 * NT, W), 0)
    lane = lax.broadcasted_iota(jnp.int32, (2 * NT, W), 1)
    parity = jnp.bitwise_and(jnp.right_shift(lane, 5), 1)
    target = sub - parity * NT
    found = {}
    for s in range(STEPS):
        owner = jnp.right_shift(bperm_ref[s : s + 1, :], 10)
        hot = jnp.where(target == owner, 1.0, 0.0).astype(BF16)
        values = jnp.concatenate(
            [
                jnp.concatenate(
                    [row(b * 8 + s * 2 + c) for b in range(2)],
                    axis=1,
                )
                for c in range(2)
            ],
            axis=0,
        ).astype(BF16)
        res = lax.dot_general(
            hot, values, (((0,), (0,)), ((), ())), preferred_element_type=F32
        )
        for b in range(2):
            for j in range(4):
                found[b, s // 2, (s % 2) * 4 + j] = res[
                    j * 32 : (j + 1) * 32, b * W : (b + 1) * W
                ]
    lane = lax.broadcasted_iota(jnp.int32, (32, W), 1)
    for b in range(2):
        for half in range(2):
            for r in range(EPACK):
                value = found[b, half, r]
                if r < 4:
                    extra = found[b, half, EPACK + r // 2]
                    turn = LEV if r % 2 == 0 else LEV - CUT
                    value = jnp.where(lane < LEV, value, pltpu.roll(extra, turn, 1))
                start = (b * 64 + half * 32) * EPACK + r
                scr2_ref[pl.ds(start, 32, stride=EPACK), :] = value
    out_ref[...] = scr2_ref[...].astype(BF16)


def plan_kernel(tile_ref, got_ref, hot_ref, base_ref):
    late = jnp.bitwise_and(jnp.right_shift(tile_ref[0], 5), 1) == 1
    n = 4 * NT
    turned = [got_ref[pl.ds(j, NT, stride=4), :].T for j in range(4)]
    sub = lax.broadcasted_iota(jnp.int32, (n, n), 0)

    def pick(early_value, late_value):
        return jnp.where(late, late_value, early_value)

    def one_hot(row):
        return jnp.where(sub == row, 1.0, 0.0).astype(BF16)

    def dest(part, s):
        k = part * STEPS + s
        row = jnp.concatenate(
            [
                pick(
                    t[L_DEST[0] + k : L_DEST[0] + k + 1, :],
                    t[L_DEST[1] + k : L_DEST[1] + k + 1, :],
                )
                for t in turned
            ],
            axis=1,
        )
        row = (row + 0.5).astype(jnp.int32)
        return jnp.right_shift(row, 8), jnp.bitwise_and(row, 3)

    def finals(part):
        tile_to, slot_to = dest(part, STEPS - 1)
        rows = {STEPS - 1: tile_to * 4 + slot_to}
        for s in range(STEPS - 2, -1, -1):
            mid_tile, mid_slot = dest(part, s)
            move = one_hot(mid_slot * NT + mid_tile)
            later = jnp.concatenate(
                [
                    jnp.broadcast_to(tile_to, (8, n)),
                    jnp.broadcast_to(slot_to, (8, n)),
                ],
                axis=0,
            )
            both = jnp.dot(
                later.astype(F32).astype(BF16), move, preferred_element_type=F32
            )
            tile_to = both[0:1, :].astype(jnp.int32)
            slot_to = both[8:9, :].astype(jnp.int32)
            rows[s] = tile_to * 4 + slot_to
        return rows

    columns = jnp.concatenate(
        [got_ref[pl.ds(j, NT, stride=4), :] for j in range(4)], axis=0
    )
    parts = []
    for _ in range(3):
        part = columns.astype(BF16)
        parts.append(part)
        columns = columns - part.astype(F32)
    parts = jnp.concatenate(parts, axis=1)

    def moved(row):
        res = jnp.dot(one_hot(row), parts, preferred_element_type=F32)
        return res[:, :W] + (res[:, W : 2 * W] + res[:, 2 * W :])

    bound = finals(0)
    hot_ref[0] = one_hot(pick(bound[0], bound[2]))
    hot_ref[1] = one_hot(pick(bound[1], bound[3]))
    outer = moved(bound[0])
    inner = moved(finals(1)[0])
    lane = lax.broadcasted_iota(jnp.int32, (n, W), 1)
    low = pick(0, SPLIT)
    high = pick(SPLIT, LEV)
    extra = pick(W, L_TOP)
    is_inner = jnp.logical_or(lane >= L_INNER, lane == extra)
    is_outer = jnp.logical_and(lane >= low, lane < high)
    base_ref[...] = jnp.where(is_outer, outer, jnp.where(is_inner, inner, 0.0))


def owner_kernel(tile_ref, got_ref, hot_ref, base_ref, mix_ref, out_ref, scr_ref):
    late = jnp.bitwise_and(jnp.right_shift(tile_ref[0], 5), 1)
    scr_ref[...] = got_ref[...].astype(F32)
    low = lax.broadcasted_iota(jnp.int32, (NT, W), 1) < CUT

    def row(r):
        if r < EPACK:
            return scr_ref[pl.ds(r, NT, stride=EPACK), :]
        first = pltpu.roll(row(2 * (r - EPACK)), W - LEV, 1)
        second = pltpu.roll(row(2 * (r - EPACK) + 1), W - LEV + CUT, 1)
        return jnp.where(low, first, second)

    moved = []
    for s in range(2):
        edge = jnp.concatenate([row(s * 4 + j) for j in range(4)], axis=0).astype(BF16)
        moved.append(jnp.dot(hot_ref[s], edge, preferred_element_type=F32).astype(BF16))
    total = jnp.dot(
        jnp.concatenate(moved, axis=1), mix_ref[late], preferred_element_type=F32
    )
    out_ref[...] = base_ref[...] + (
        total[:, :W] + (total[:, W : 2 * W] + total[:, 2 * W :])
    )


def nest_kernel(got_ref, out_ref, sum_ref, early_ref, late_ref):
    for b in range(2):
        early = got_ref[b * 2 * W : b * 2 * W + W, :]
        late = got_ref[b * 2 * W + W : (b + 1) * 2 * W, :]
        sum_ref[...] = (early + late).T
        early_ref[...] = early.T
        late_ref[...] = late.T
        out_ref[2 * b] = sum_ref[:LEV, :]
        inner = 2 * b + 1
        out_ref[inner, :SPLIT, :] = early_ref[L_INNER:, :]
        out_ref[inner, SPLIT : 2 * SPLIT, :] = late_ref[L_INNER:, :]
        out_ref[inner, 2 * SPLIT :, :] = late_ref[L_TOP : L_TOP + 1, :]


def stats_kernel(own_ref, other_ref, mean_ref, var_ref, nest_hbm, sems):
    copies = start_all(
        [
            (own_ref.at[2 * b + part], nest_hbm.at[:, part, b, :])
            for b in range(2)
            for part in range(2)
        ],
        sems,
    )
    for part in range(2):
        a0, a1, b0, b1 = (
            ref[2 * b + part] for ref in (own_ref, other_ref) for b in range(2)
        )
        lanes = slice(part * W, (part + 1) * W)
        mean = ((a0 + a1) + (b0 + b1)) / 4.0
        mean_ref[:, lanes] = mean
        own = (a0 - mean) * (a0 - mean) + (a1 - mean) * (a1 - mean)
        other = (b0 - mean) * (b0 - mean) + (b1 - mean) * (b1 - mean)
        var_ref[:, lanes] = (own + other) / 4.0
    for copy in copies:
        copy.wait()


def in_hbm(x):
    return pltpu.with_memory_space_constraint(x, pltpu.HBM)


def exchange(x):
    return lax.all_to_all(x, "tile", split_axis=0, concat_axis=0, tiled=True)


def on_device(parent_state, nest_state, terrain, shift_x, boundary_index, reloc_dest):
    q_mix, e_mix = constants()
    q_mix, e_mix = jnp.asarray(q_mix), jnp.asarray(e_mix)
    sds = jax.ShapeDtypeStruct
    tile = lax.axis_index("tile").astype(jnp.int32).reshape(1)
    parent = parent_state.reshape(FLAT, W)

    nest = nest_state.reshape(2, LEV, 2, W).transpose(1, 2, 0, 3)
    kept, down, up, nest, bidx, dest, q_mix = call(
        halo_kernel,
        (
            pltpu.VMEM((FLAT, W), F32),
            sds((HALO_ROWS, W), BF16),
            sds((HALO_ROWS, W), BF16),
            pltpu.VMEM((4, LEV, W), F32),
            pltpu.VMEM((STEPS, NT), jnp.int32),
            pltpu.VMEM((STEPS, 2 * W), jnp.int32),
            pltpu.VMEM((6 * W, 2 * W), BF16),
        ),
        in_specs=[SM, HB, HB, HB, HB, HB, HB],
        scratch=[
            pltpu.VMEM((ROWS, W), jnp.int32),
            pltpu.VMEM((HALO_ROWS, W), F32),
            pltpu.VMEM((HALO_ROWS, W), F32),
            pltpu.VMEM((ROWS, W), F32),
            pltpu.SemaphoreType.DMA((9,)),
        ],
        name="halo",
        nbytes=1 << 20,
    )(
        tile,
        in_hbm(parent),
        in_hbm(terrain),
        in_hbm(nest),
        in_hbm(boundary_index),
        in_hbm(reloc_dest),
        in_hbm(q_mix),
    )
    message = call(
        send_kernel,
        sds((4 * NT, W), F32),
        in_specs=[HB, VM, VM, VM, VM],
        scratch=[
            pltpu.SMEM((STEPS,), jnp.int32),
            pltpu.VMEM((2, 2 * W, W), F32),
            pltpu.SemaphoreType.DMA((1,)),
        ],
        name="send",
        nbytes=64 << 20,
    )(in_hbm(shift_x), nest, bidx, dest, q_mix)
    pairs = [(i, i + 1) for i in range(0, NT, 2)] + [(i + 1, i) for i in range(0, NT, 2)]
    gaps = [(i, i + 1) for i in range(1, NT - 1, 2)]
    gaps = gaps + [(i + 1, i) for i in range(1, NT - 1, 2)]
    from_gap = lax.ppermute(up, "tile", gaps)
    from_pair = lax.ppermute(down, "tile", pairs)
    first = exchange(message.reshape(NT, 4, W)).reshape(4 * NT, W)
    cells, ring = call(
        parent_kernel,
        (
            pltpu.VMEM((STEPS, 2 * W, ROWS * W), BF16),
            pltpu.HBM((2 * BSTR, W), F32),
        ),
        in_specs=[SM, VM, VM, VM, HB],
        out_specs=(VM, HB),
        scratch=[
            pltpu.VMEM((HALO_ROWS, W), F32),
            pltpu.VMEM((HALO_ROWS, W), F32),
            pltpu.VMEM((FLAT, W), F32),
            pltpu.VMEM((ROWS, W), F32),
            pltpu.VMEM((2 * BSTR, W), F32),
            pltpu.VMEM((2 * BSTR, W), F32),
            pltpu.VMEM((2 * BSTR, W), F32),
            pltpu.VMEM((ROWS, W), jnp.int32),
            pltpu.SemaphoreType.DMA((2,)),
        ],
        name="parent",
        flops=1 << 33,
        nbytes=1 << 27,
    )(tile, kept, from_gap, from_pair, in_hbm(terrain))

    values = call(
        gather_kernel,
        sds((PACK * NT, W), BF16),
        scratch=[pltpu.VMEM((PACK * NT, W), F32)],
        name="gather",
        flops=1 << 29,
        nbytes=3 << 20,
    )(first, cells)
    second = exchange(values.reshape(PACK // 4 * NT, 4, W)).reshape(PACK * NT, W)

    hot, base = call(
        plan_kernel,
        (sds((2, 4 * NT, 4 * NT), BF16), sds((4 * NT, W), F32)),
        in_specs=[SM, VM],
        name="plan",
        flops=1 << 28,
        nbytes=3 << 20,
    )(tile, first)

    second, hot, base = lax.optimization_barrier((second, hot, base))
    bperm = boundary_index.reshape(STEPS, 32, 4).transpose(0, 2, 1).reshape(STEPS, NT)
    edges = call(
        regroup_kernel,
        sds((EPACK * NT, W), BF16),
        scratch=[pltpu.VMEM((PACK * NT, W), F32), pltpu.VMEM((EPACK * NT, W), F32)],
        name="regroup",
        flops=1 << 26,
        nbytes=1 << 20,
    )(bperm, second)
    third = exchange(edges.reshape(EPACK // 2 * NT, 2, W)).reshape(EPACK * NT, W)

    parent_out = call(
        last_parent_kernel,
        sds((2 * LEV, ROWS, W), F32),
        in_specs=[HB, HB],
        scratch=[
            pltpu.VMEM((2 * BSTR, W), F32),
            pltpu.VMEM((ROWS, W), jnp.int32),
            pltpu.SemaphoreType.DMA((2,)),
        ],
        name="last_parent",
        flops=1 << 22,
        nbytes=2 << 20,
    )(in_hbm(ring), in_hbm(terrain))
    third, parent_out = lax.optimization_barrier((third, parent_out))
    columns = call(
        owner_kernel,
        sds((4 * NT, W), F32),
        in_specs=[SM, VM, VM, VM, VM],
        scratch=[pltpu.VMEM((EPACK * NT, W), F32)],
        name="owner",
        flops=1 << 29,
        nbytes=3 << 20,
    )(tile, third, hot, base, e_mix)
    fourth = exchange(columns.reshape(NT, 4, W)).reshape(4 * NT, W)

    own = call(
        nest_kernel,
        pltpu.VMEM((4, LEV, W), F32),
        scratch=[pltpu.VMEM((W, W), F32)] * 3,
        name="nest",
        nbytes=1 << 19,
    )(fourth)
    other = lax.ppermute(own, "member", [(0, 1), (1, 0)])
    mean, variance, nest_out = call(
        stats_kernel,
        (
            sds((LEV, 2 * W), F32),
            sds((LEV, 2 * W), F32),
            pltpu.HBM((LEV, 2, 2, W), F32),
        ),
        in_specs=[VM, VM],
        out_specs=(VM, VM, HB),
        scratch=[pltpu.SemaphoreType.DMA((4,))],
        name="stats",
        nbytes=1 << 19,
    )(own, other)
    nest_out = nest_out.transpose(2, 0, 1, 3)
    nest_out = nest_out.reshape(nest_state.shape)
    return (parent_out.reshape(parent_state.shape), nest_out, mean, variance)


def solution(mesh):
    in_specs = (
        P("member", None, "tile", None),
        P("member", None, "tile"),
        P("tile", None),
        P(),
        P(None, "tile"),
        P(None, "tile"),
    )
    out_specs = (
        P("member", None, "tile", None),
        P("member", None, "tile"),
        P(None, "tile"),
        P(None, "tile"),
    )
    return jax.shard_map(
        on_device, mesh=mesh, in_specs=in_specs, out_specs=out_specs, check_vma=False
    )
```

```python
import functools

import jax
import jax.numpy as jnp
import numpy as np
from jax import lax
from jax.experimental import pallas as pl
from jax.experimental.pallas import tpu as pltpu
from jax.sharding import PartitionSpec as P

F32 = jnp.float32
BF16 = jnp.bfloat16
LEV = 81
STEPS = 4
NT = 128
ROWS = 8
W = 128
LPAD = 96
RING = 16
BSTR = LPAD * RING
SENT = 6
FLAT = 2 * LEV * ROWS
HALO_ROWS = 992
DIST = ((0, 1), (2, 3), (4, None), (5, None))
SPLIT = 40
PACK = 12
EPACK = 6
CUT = W - LEV
L_TOP = 81
L_REQ = 86
L_INNER = 88
L_DEST = (48, 8)
HORIZ = 0.15
VERT = 0.1
DRAG = 0.1
RELAX = 0.5
IMPL = 0.8
VMEM_LIMIT = 20 * 1024 * 1024


def solve_matrix():
    n = np.full(LEV, 2.0)
    n[0] = n[-1] = 1.0
    a = np.diag(1.0 + IMPL * n)
    a -= IMPL * (np.eye(LEV, k=1) + np.eye(LEV, k=-1))
    return np.linalg.inv(a)


def padded_transpose(m):
    out = np.zeros((W, W))
    out[:LEV, :LEV] = m.T
    return out


def split3(m):
    m = np.asarray(m, np.float64)
    parts = []
    for _ in range(3):
        part = m.astype(jnp.bfloat16)
        parts.append(part)
        m = m - part.astype(np.float64)
    return parts


def constants():
    s = solve_matrix()
    power = [np.linalg.matrix_power(s, k) for k in range(STEPS + 1)]
    keep = 1.0 - RELAX
    inner = power[STEPS].T
    bound = power[STEPS].T * keep**STEPS
    send = np.zeros((2, W, 2, W))
    send[0, :LEV, 0, :SPLIT] = bound[:, :SPLIT]
    send[0, :LEV, 1, SPLIT:LEV] = bound[:, SPLIT:]
    send[1, :LEV, 0, L_INNER:] = inner[:, :SPLIT]
    send[1, :LEV, 1, L_INNER:] = inner[:, SPLIT : 2 * SPLIT]
    send[1, :LEV, 1, L_TOP] = inner[:, 2 * SPLIT]
    for part in range(2):
        for owner in range(2):
            for k in range(STEPS):
                send[part, LEV + k, owner, L_DEST[owner] + part * STEPS + k] = 1.0
    coarse, fine, _ = split3(send.reshape(2 * W, 2 * W))
    send = np.concatenate([coarse, coarse, fine])
    mix = [
        padded_transpose(power[STEPS - k] * RELAX * keep ** (STEPS - 1 - k))
        for k in range(STEPS)
    ]
    edge = np.stack(
        [
            np.concatenate(split3(np.concatenate(mix[:2])), axis=1),
            np.concatenate(split3(np.concatenate(mix[2:])), axis=1),
        ]
    )
    return send, edge


def call(
    body, out_shape, in_specs=None, out_specs=None, scratch=(), name=None, flops=0, nbytes=0
):
    kwargs = {} if in_specs is None else {"in_specs": in_specs}
    if out_specs is not None:
        kwargs["out_specs"] = out_specs
    return pl.pallas_call(
        body,
        out_shape=out_shape,
        scratch_shapes=list(scratch),
        compiler_params=pltpu.CompilerParams(vmem_limit_bytes=VMEM_LIMIT),
        cost_estimate=pl.CostEstimate(
            flops=flops, bytes_accessed=nbytes, transcendentals=0
        ),
        name=name,
        **kwargs,
    )


VM = pl.BlockSpec(memory_space=pltpu.VMEM)
HB = pl.BlockSpec(memory_space=pltpu.HBM)
SM = pl.BlockSpec(memory_space=pltpu.SMEM)


def start_all(pairs, sems):
    copies = [pltpu.make_async_copy(x, y, sems.at[i]) for i, (x, y) in enumerate(pairs)]
    for copy in copies:
        copy.start()
    return copies


def halo_kernel(
    tile_ref, parent_hbm, terrain_hbm, nest_hbm, bidx_hbm, dest_hbm, mix_hbm, shift_hbm,
    parent_ref, first_ref, second_ref, nest_ref, moved_ref, dest_ref, mix_ref,
    terrain_ref, down_ref, up_ref, damp_ref, bidx_ref, shift_ref, sems,
):
    copies = start_all(
        [
            (parent_hbm, parent_ref),
            (terrain_hbm, terrain_ref),
            (bidx_hbm, bidx_ref),
            (dest_hbm, dest_ref),
            (mix_hbm, mix_ref),
            (shift_hbm, shift_ref),
        ]
        + [
            (nest_hbm.at[:, part, b, :], nest_ref.at[b * 2 + part])
            for b in range(2)
            for part in range(2)
        ],
        sems,
    )
    for copy in copies[:2]:
        copy.wait()
    damp_ref[...] = DRAG * terrain_ref[...].astype(F32) / 3000.0
    for ref, rows in ((down_ref, (7, 6, 5, 4)), (up_ref, (0, 1, 2, 3))):
        ref[HALO_ROWS - 24 :, :] = jnp.zeros((24, W), F32)
        for row, (coarse, fine) in zip(rows, DIST):
            for count, base, value in (
                (2 * LEV, 0, parent_ref[pl.ds(row, 2 * LEV, stride=ROWS), :]),
                (1, 2 * LEV * SENT, damp_ref[row : row + 1, :]),
            ):
                ref[pl.ds(base + coarse, count, stride=SENT), :] = value
                if fine is not None:
                    rest = value - value.astype(BF16).astype(F32)
                    ref[pl.ds(base + fine, count, stride=SENT), :] = rest
    even = jnp.bitwise_and(tile_ref[0], 1) == 0
    down, up = down_ref[...], up_ref[...]
    first_ref[...] = jnp.where(even, down, up).astype(BF16)
    second_ref[...] = jnp.where(even, up, down).astype(BF16)
    for copy in copies[2:]:
        copy.wait()
    for s in range(STEPS):
        idx = bidx_ref[s : s + 1, :]
        col = jnp.bitwise_and(idx, W - 1)
        moved = jnp.bitwise_and(col + shift_ref[s], W - 1)
        moved_ref[s : s + 1, :] = idx - col + moved


def send_kernel(nest_ref, moved_ref, dest_ref, mix_ref, msg_ref, pad_ref):
    zeros = jnp.zeros((W - LEV + 1, W), F32)
    for b in range(2):
        for part in range(2):
            top = part * W
            pad_ref[b, top + LEV - 1 : top + W, :] = zeros
            pad_ref[b, top : top + LEV, :] = nest_ref[b * 2 + part]
            pad_ref[b, top + LEV : top + LEV + STEPS, :] = dest_ref[
                :, part * W : (part + 1) * W
            ].astype(F32)
        value = pad_ref[b]
        coarse = value.astype(BF16)
        fine = (value - coarse.astype(F32)).astype(BF16)
        res = lax.dot_general(
            jnp.concatenate([coarse, fine, coarse], axis=0),
            mix_ref[...],
            (((0,), (0,)), ((), ())),
            preferred_element_type=F32,
        )
        for owner in range(2):
            start = b * 2 * W + owner * W
            msg_ref[start : start + W, :] = res[:, owner * W : (owner + 1) * W]
    lane = lax.broadcasted_iota(jnp.int32, (NT, W), 1)
    tile = lax.broadcasted_iota(jnp.int32, (NT, W), 0)
    asked = jnp.logical_or(lane == L_REQ, lane == L_REQ + 1)
    wanted = tile == L_REQ + jnp.bitwise_and(lane, 1)
    for s in range(STEPS):
        idx = moved_ref[s : s + 1, :]
        owner = jnp.right_shift(idx, 10)
        row = jnp.bitwise_and(jnp.right_shift(idx, 7), ROWS - 1)
        col = jnp.bitwise_and(idx, W - 1)
        mine = jnp.where(tile == owner, 1.0, 0.0).astype(BF16)
        found = []
        for value in (row + 1, col):
            value = jnp.broadcast_to(value.astype(F32), (NT, W))
            value = jnp.where(wanted, value, 0.0).astype(BF16)
            found.append(
                lax.dot_general(
                    mine, value, (((1,), (1,)), ((), ())), preferred_element_type=F32
                )
            )
        cell = (found[0] - 1.0) * W + found[1]
        rows = msg_ref[pl.ds(s, NT, stride=4), :]
        msg_ref[pl.ds(s, NT, stride=4), :] = jnp.where(asked, cell, rows)


def ring_step(read, write, level_stride, coef, own_only=False):
    row = lax.broadcasted_iota(jnp.int32, (ROWS, W), 0)
    last = row == ROWS - 1
    head = row == 0
    c0, c1, h1, v1 = coef
    chunk = 9

    def body(step, carry):
        start = step * chunk
        ends = jnp.maximum(start - 1, 0), jnp.minimum(start + chunk, LEV - 1)
        for member in range(2):
            base = member * level_stride
            column = [read(base + start + k) for k in range(chunk)]
            column = [read(base + ends[0])] + column + [read(base + ends[1])]
            for k in range(chunk):
                (d0, d1), (x0, x1), (u0, u1) = column[k : k + 3]
                f0 = pltpu.roll(x0, ROWS - 1, 0)
                f1 = pltpu.roll(x1, ROWS - 1, 0)
                g0 = pltpu.roll(x0, 1, 0)
                g1 = pltpu.roll(x1, 1, 0)
                near0 = jnp.where(last, f1, f0) + jnp.where(head, g1, g0)
                near0 = near0 + (pltpu.roll(x0, 1, 1) + pltpu.roll(x0, W - 1, 1))
                y0 = c0 * x0 + HORIZ * near0 + VERT * (d0 + u0)
                if own_only:
                    write(member, start + k, y0, None)
                    continue
                near1 = jnp.where(last, f0, f1) + jnp.where(head, g0, g1)
                near1 = near1 + (pltpu.roll(x1, 1, 1) + pltpu.roll(x1, W - 1, 1))
                y1 = c1 * x1 + h1 * near1 + v1 * (d1 + u1)
                write(member, start + k, y0, y1)
        return carry

    lax.fori_loop(0, LEV // chunk, body, 0)


def parent_kernel(
    tile_ref, parent_ref, second_ref, first_ref, terrain_hbm,
    cells_ref, ring_hbm,
    next_ref, prev_ref, halo_ref, damp_ref, a_ref, b_ref, ring_ref, terrain_ref, sems,
):
    copies = start_all([(terrain_hbm, terrain_ref)], sems)
    store = pltpu.make_async_copy(ring_ref, ring_hbm, sems.at[1])
    tile = tile_ref[0]
    even = jnp.bitwise_and(tile, 1) == 0
    first, second = first_ref[...].astype(F32), second_ref[...].astype(F32)
    next_ref[...] = jnp.where(even, first, second)
    prev_ref[...] = jnp.where(even, second, first)
    for ref, rows in ((next_ref, (0, 1, 2, 3)), (prev_ref, (7, 6, 5, 4))):
        for row, (coarse, fine) in zip(rows, DIST):
            for count, base, out in ((2 * LEV, 0, halo_ref), (1, 2 * LEV * SENT, damp_ref)):
                value = ref[pl.ds(base + coarse, count, stride=SENT), :]
                if fine is not None:
                    value = value + ref[pl.ds(base + fine, count, stride=SENT), :]
                out[pl.ds(row, count, stride=ROWS), :] = value
    copies[0].wait()
    damping = DRAG * terrain_ref[...].astype(F32) / 3000.0
    pads = jnp.zeros(((LPAD - LEV) * RING, W), F32)
    for ref in (a_ref, b_ref, ring_ref):
        for member in range(2):
            top = member * BSTR + LEV * RING
            ref[top : top + (LPAD - LEV) * RING, :] = pads
    for s in range(STEPS):
        for member in range(2):
            start = LPAD if s else LEV - 1
            cells_ref[s, member * W + start : (member + 1) * W, :] = jnp.zeros(
                (W - start, ROWS * W), BF16
            )
    row = lax.broadcasted_iota(jnp.int32, (ROWS, W), 0)
    south = jnp.where(tile < NT - 1, 1.0, 0.0).astype(F32)
    north = jnp.where(tile > 0, 1.0, 0.0).astype(F32)
    valid = jnp.where(row < 4, south, north)
    stay = 1.0 - 4.0 * HORIZ - 2.0 * VERT
    coef = (stay - damping, (stay - damp_ref[...]) * valid, HORIZ * valid, VERT * valid)

    def emit(s, ref, count, stride):
        for member in range(2):
            for y in range(ROWS):
                start = member * count * stride + y
                rows = ref[pl.ds(start, count, stride=stride), :]
                cells_ref[s, member * W : member * W + count, y * W : (y + 1) * W] = (
                    rows.astype(BF16)
                )

    def read_first(index):
        base = pl.multiple_of(index * ROWS, ROWS)
        return parent_ref[pl.ds(base, ROWS), :], halo_ref[pl.ds(base, ROWS), :]

    emit(0, parent_ref, LEV, ROWS)
    read, stride = read_first, LEV
    for s, dst in zip(range(1, STEPS), (a_ref, b_ref, ring_ref)):

        def write(member, level, y0, y1, dst=dst):
            base = pl.multiple_of((member * LPAD + level) * RING, RING)
            dst[pl.ds(base, ROWS), :] = y0
            dst[pl.ds(base + ROWS, ROWS), :] = y1

        ring_step(read, write, stride, coef)
        if s == STEPS - 1:
            store.start()
        emit(s, dst, LPAD, RING)

        def read(index, src=dst):
            base = pl.multiple_of(index * RING, RING)
            return src[pl.ds(base, ROWS), :], src[pl.ds(base + ROWS, ROWS), :]

        stride = LPAD
    store.wait()


def last_parent_kernel(ring_hbm, terrain_hbm, out_ref, ring_ref, terrain_ref, sems):
    for copy in start_all([(ring_hbm, ring_ref), (terrain_hbm, terrain_ref)], sems):
        copy.wait()
    damping = DRAG * terrain_ref[...].astype(F32) / 3000.0
    stay = 1.0 - 4.0 * HORIZ - 2.0 * VERT

    def read(index):
        base = pl.multiple_of(index * RING, RING)
        return ring_ref[pl.ds(base, ROWS), :], ring_ref[pl.ds(base + ROWS, ROWS), :]

    def write(member, level, y0, y1):
        out_ref[member * LEV + level] = y0

    ring_step(read, write, LPAD, (stay - damping, None, None, None), own_only=True)


def gather_kernel(got_ref, cells_ref, out_ref, scr_ref):
    cell = lax.broadcasted_iota(jnp.int32, (NT, ROWS * W), 1).astype(F32)
    lane = lax.broadcasted_iota(jnp.int32, (NT, W), 1)
    rows = {}
    for s in range(STEPS):
        asked = got_ref[pl.ds(s, NT, stride=4), :]
        hot = [
            jnp.where(cell == asked[:, L_REQ + c : L_REQ + c + 1], 1.0, 0.0).astype(BF16)
            for c in range(2)
        ]
        hot = jnp.concatenate(hot, axis=0)
        res = lax.dot_general(
            hot, cells_ref[s], (((1,), (1,)), ((), ())), preferred_element_type=F32
        )
        for b in range(2):
            for c in range(2):
                rows[b * 8 + s * 2 + c] = res[c * W : (c + 1) * W, b * W : (b + 1) * W]
    for r in range(PACK):
        row = rows[r]
        if r < 8:
            extra = rows[PACK + r // 2]
            if r % 2 == 0:
                row = row + pltpu.roll(jnp.where(lane < CUT, extra, 0.0), LEV, 1)
            else:
                row = row + pltpu.roll(jnp.where(lane < CUT, 0.0, extra), LEV - CUT, 1)
        scr_ref[pl.ds(r, NT, stride=PACK), :] = row
    out_ref[...] = scr_ref[...].astype(BF16)


def regroup_kernel(bperm_ref, got_ref, out_ref, scr_ref, scr2_ref):
    scr_ref[...] = got_ref[...].astype(F32)
    low = lax.broadcasted_iota(jnp.int32, (NT, W), 1) < CUT

    def row(r):
        if r < PACK:
            return scr_ref[pl.ds(r, NT, stride=PACK), :]
        first = pltpu.roll(row(2 * (r - PACK)), W - LEV, 1)
        second = pltpu.roll(row(2 * (r - PACK) + 1), W - LEV + CUT, 1)
        return jnp.where(low, first, second)

    sub = lax.broadcasted_iota(jnp.int32, (2 * NT, W), 0)
    lane = lax.broadcasted_iota(jnp.int32, (2 * NT, W), 1)
    parity = jnp.bitwise_and(jnp.right_shift(lane, 5), 1)
    target = sub - parity * NT
    found = {}
    for s in range(STEPS):
        owner = jnp.right_shift(bperm_ref[s : s + 1, :], 10)
        hot = jnp.where(target == owner, 1.0, 0.0).astype(BF16)
        values = jnp.concatenate(
            [
                jnp.concatenate(
                    [row(b * 8 + s * 2 + c) for b in range(2)],
                    axis=1,
                )
                for c in range(2)
            ],
            axis=0,
        ).astype(BF16)
        res = lax.dot_general(
            hot, values, (((0,), (0,)), ((), ())), preferred_element_type=F32
        )
        for b in range(2):
            for j in range(4):
                found[b, s // 2, (s % 2) * 4 + j] = res[
                    j * 32 : (j + 1) * 32, b * W : (b + 1) * W
                ]
    lane = lax.broadcasted_iota(jnp.int32, (32, W), 1)
    for b in range(2):
        for half in range(2):
            for r in range(EPACK):
                value = found[b, half, r]
                if r < 4:
                    extra = found[b, half, EPACK + r // 2]
                    turn = LEV if r % 2 == 0 else LEV - CUT
                    value = jnp.where(lane < LEV, value, pltpu.roll(extra, turn, 1))
                start = (b * 64 + half * 32) * EPACK + r
                scr2_ref[pl.ds(start, 32, stride=EPACK), :] = value
    out_ref[...] = scr2_ref[...].astype(BF16)


def plan_kernel(tile_ref, got_ref, hot_ref, base_ref):
    late = jnp.bitwise_and(jnp.right_shift(tile_ref[0], 5), 1) == 1
    n = 4 * NT
    turned = [got_ref[pl.ds(j, NT, stride=4), :].T for j in range(4)]
    sub = lax.broadcasted_iota(jnp.int32, (n, n), 0)

    def pick(early_value, late_value):
        return jnp.where(late, late_value, early_value)

    def one_hot(row):
        return jnp.where(sub == row, 1.0, 0.0).astype(BF16)

    def dest(part, s):
        k = part * STEPS + s
        row = jnp.concatenate(
            [
                pick(
                    t[L_DEST[0] + k : L_DEST[0] + k + 1, :],
                    t[L_DEST[1] + k : L_DEST[1] + k + 1, :],
                )
                for t in turned
            ],
            axis=1,
        )
        row = (row + 0.5).astype(jnp.int32)
        return jnp.right_shift(row, 8), jnp.bitwise_and(row, 3)

    def finals(part):
        tile_to, slot_to = dest(part, STEPS - 1)
        rows = {STEPS - 1: tile_to * 4 + slot_to}
        for s in range(STEPS - 2, -1, -1):
            mid_tile, mid_slot = dest(part, s)
            move = one_hot(mid_slot * NT + mid_tile)
            later = jnp.concatenate(
                [
                    jnp.broadcast_to(tile_to, (8, n)),
                    jnp.broadcast_to(slot_to, (8, n)),
                ],
                axis=0,
            )
            both = jnp.dot(
                later.astype(F32).astype(BF16), move, preferred_element_type=F32
            )
            tile_to = both[0:1, :].astype(jnp.int32)
            slot_to = both[8:9, :].astype(jnp.int32)
            rows[s] = tile_to * 4 + slot_to
        return rows

    columns = jnp.concatenate(
        [got_ref[pl.ds(j, NT, stride=4), :] for j in range(4)], axis=0
    )
    parts = []
    for _ in range(3):
        part = columns.astype(BF16)
        parts.append(part)
        columns = columns - part.astype(F32)
    parts = jnp.concatenate(parts, axis=1)

    def moved(row):
        res = jnp.dot(one_hot(row), parts, preferred_element_type=F32)
        return res[:, :W] + (res[:, W : 2 * W] + res[:, 2 * W :])

    bound = finals(0)
    hot_ref[0] = one_hot(pick(bound[0], bound[2]))
    hot_ref[1] = one_hot(pick(bound[1], bound[3]))
    outer = moved(bound[0])
    inner = moved(finals(1)[0])
    lane = lax.broadcasted_iota(jnp.int32, (n, W), 1)
    low = pick(0, SPLIT)
    high = pick(SPLIT, LEV)
    extra = pick(W, L_TOP)
    is_inner = jnp.logical_or(lane >= L_INNER, lane == extra)
    is_outer = jnp.logical_and(lane >= low, lane < high)
    base_ref[...] = jnp.where(is_outer, outer, jnp.where(is_inner, inner, 0.0))


def owner_kernel(tile_ref, got_ref, hot_ref, base_ref, mix_ref, out_ref, scr_ref):
    late = jnp.bitwise_and(jnp.right_shift(tile_ref[0], 5), 1)
    scr_ref[...] = got_ref[...].astype(F32)
    low = lax.broadcasted_iota(jnp.int32, (NT, W), 1) < CUT

    def row(r):
        if r < EPACK:
            return scr_ref[pl.ds(r, NT, stride=EPACK), :]
        first = pltpu.roll(row(2 * (r - EPACK)), W - LEV, 1)
        second = pltpu.roll(row(2 * (r - EPACK) + 1), W - LEV + CUT, 1)
        return jnp.where(low, first, second)

    moved = []
    for s in range(2):
        edge = jnp.concatenate([row(s * 4 + j) for j in range(4)], axis=0).astype(BF16)
        moved.append(jnp.dot(hot_ref[s], edge, preferred_element_type=F32).astype(BF16))
    total = jnp.dot(
        jnp.concatenate(moved, axis=1), mix_ref[late], preferred_element_type=F32
    )
    out_ref[...] = base_ref[...] + (
        total[:, :W] + (total[:, W : 2 * W] + total[:, 2 * W :])
    )


def nest_kernel(got_ref, out_ref, sum_ref, early_ref, late_ref):
    for b in range(2):
        early = got_ref[b * 2 * W : b * 2 * W + W, :]
        late = got_ref[b * 2 * W + W : (b + 1) * 2 * W, :]
        sum_ref[...] = (early + late).T
        early_ref[...] = early.T
        late_ref[...] = late.T
        out_ref[pl.ds(b, LEV, stride=4), :] = sum_ref[:LEV, :]
        inner = 2 + b
        out_ref[pl.ds(inner, SPLIT, stride=4), :] = early_ref[L_INNER:, :]
        out_ref[pl.ds(inner + 4 * SPLIT, SPLIT, stride=4), :] = late_ref[L_INNER:, :]
        top = inner + 8 * SPLIT
        out_ref[top : top + 1, :] = late_ref[L_TOP : L_TOP + 1, :]


def stats_kernel(own_ref, other_ref, mean_ref, var_ref):
    for half in range(2):
        a0, a1, b0, b1 = (
            ref[pl.ds(half * 2 + b, LEV, stride=4), :]
            for ref in (own_ref, other_ref)
            for b in range(2)
        )
        lanes = slice(half * W, (half + 1) * W)
        mean = ((a0 + a1) + (b0 + b1)) / 4.0
        mean_ref[:, lanes] = mean
        own = (a0 - mean) * (a0 - mean) + (a1 - mean) * (a1 - mean)
        other = (b0 - mean) * (b0 - mean) + (b1 - mean) * (b1 - mean)
        var_ref[:, lanes] = (own + other) / 4.0


def in_hbm(x):
    return pltpu.with_memory_space_constraint(x, pltpu.HBM)


def exchange(x):
    return lax.all_to_all(x, "tile", split_axis=0, concat_axis=0, tiled=True)


def on_device(parent_state, nest_state, terrain, shift_x, boundary_index, reloc_dest):
    q_mix, e_mix = constants()
    q_mix, e_mix = jnp.asarray(q_mix), jnp.asarray(e_mix)
    sds = jax.ShapeDtypeStruct
    tile = lax.axis_index("tile").astype(jnp.int32).reshape(1)
    parent = parent_state.reshape(FLAT, W)

    nest = nest_state.reshape(2, LEV, 2, W).transpose(1, 2, 0, 3)
    kept, down, up, nest, moved, dest, q_mix = call(
        halo_kernel,
        (
            pltpu.VMEM((FLAT, W), F32),
            sds((HALO_ROWS, W), BF16),
            sds((HALO_ROWS, W), BF16),
            pltpu.VMEM((4, LEV, W), F32),
            pltpu.VMEM((STEPS, NT), jnp.int32),
            pltpu.VMEM((STEPS, 2 * W), jnp.int32),
            pltpu.VMEM((6 * W, 2 * W), BF16),
        ),
        in_specs=[SM, HB, HB, HB, HB, HB, HB, HB],
        scratch=[
            pltpu.VMEM((ROWS, W), jnp.int32),
            pltpu.VMEM((HALO_ROWS, W), F32),
            pltpu.VMEM((HALO_ROWS, W), F32),
            pltpu.VMEM((ROWS, W), F32),
            pltpu.VMEM((STEPS, NT), jnp.int32),
            pltpu.SMEM((STEPS,), jnp.int32),
            pltpu.SemaphoreType.DMA((10,)),
        ],
        name="halo",
        nbytes=1 << 20,
    )(
        tile,
        in_hbm(parent),
        in_hbm(terrain),
        in_hbm(nest),
        in_hbm(boundary_index),
        in_hbm(reloc_dest),
        in_hbm(q_mix),
        in_hbm(shift_x),
    )
    message = call(
        send_kernel,
        sds((4 * NT, W), F32),
        scratch=[pltpu.VMEM((2, 2 * W, W), F32)],
        name="send",
        nbytes=64 << 20,
    )(nest, moved, dest, q_mix)
    pairs = [(i, i + 1) for i in range(0, NT, 2)] + [(i + 1, i) for i in range(0, NT, 2)]
    gaps = [(i, i + 1) for i in range(1, NT - 1, 2)]
    gaps = gaps + [(i + 1, i) for i in range(1, NT - 1, 2)]
    from_gap = lax.ppermute(up, "tile", gaps)
    from_pair = lax.ppermute(down, "tile", pairs)
    first = exchange(message.reshape(NT, 4, W)).reshape(4 * NT, W)
    cells, ring = call(
        parent_kernel,
        (
            pltpu.VMEM((STEPS, 2 * W, ROWS * W), BF16),
            pltpu.HBM((2 * BSTR, W), F32),
        ),
        in_specs=[SM, VM, VM, VM, HB],
        out_specs=(VM, HB),
        scratch=[
            pltpu.VMEM((HALO_ROWS, W), F32),
            pltpu.VMEM((HALO_ROWS, W), F32),
            pltpu.VMEM((FLAT, W), F32),
            pltpu.VMEM((ROWS, W), F32),
            pltpu.VMEM((2 * BSTR, W), F32),
            pltpu.VMEM((2 * BSTR, W), F32),
            pltpu.VMEM((2 * BSTR, W), F32),
            pltpu.VMEM((ROWS, W), jnp.int32),
            pltpu.SemaphoreType.DMA((2,)),
        ],
        name="parent",
        flops=1 << 33,
        nbytes=1 << 27,
    )(tile, kept, from_gap, from_pair, in_hbm(terrain))

    values = call(
        gather_kernel,
        sds((PACK * NT, W), BF16),
        scratch=[pltpu.VMEM((PACK * NT, W), F32)],
        name="gather",
        flops=1 << 29,
        nbytes=3 << 20,
    )(first, cells)
    second = exchange(values.reshape(PACK // 4 * NT, 4, W)).reshape(PACK * NT, W)

    hot, base = call(
        plan_kernel,
        (sds((2, 4 * NT, 4 * NT), BF16), sds((4 * NT, W), F32)),
        in_specs=[SM, VM],
        name="plan",
        flops=1 << 28,
        nbytes=3 << 20,
    )(tile, first)

    second, hot, base = lax.optimization_barrier((second, hot, base))
    bperm = boundary_index.reshape(STEPS, 32, 4).transpose(0, 2, 1).reshape(STEPS, NT)
    edges = call(
        regroup_kernel,
        sds((EPACK * NT, W), BF16),
        scratch=[pltpu.VMEM((PACK * NT, W), F32), pltpu.VMEM((EPACK * NT, W), F32)],
        name="regroup",
        flops=1 << 26,
        nbytes=1 << 20,
    )(bperm, second)
    third = exchange(edges.reshape(EPACK // 2 * NT, 2, W)).reshape(EPACK * NT, W)

    parent_out = call(
        last_parent_kernel,
        sds((2 * LEV, ROWS, W), F32),
        in_specs=[HB, HB],
        scratch=[
            pltpu.VMEM((2 * BSTR, W), F32),
            pltpu.VMEM((ROWS, W), jnp.int32),
            pltpu.SemaphoreType.DMA((2,)),
        ],
        name="last_parent",
        flops=1 << 22,
        nbytes=2 << 20,
    )(in_hbm(ring), in_hbm(terrain))
    third, parent_out = lax.optimization_barrier((third, parent_out))
    columns = call(
        owner_kernel,
        sds((4 * NT, W), F32),
        in_specs=[SM, VM, VM, VM, VM],
        scratch=[pltpu.VMEM((EPACK * NT, W), F32)],
        name="owner",
        flops=1 << 29,
        nbytes=3 << 20,
    )(tile, third, hot, base, e_mix)
    fourth = exchange(columns.reshape(NT, 4, W)).reshape(4 * NT, W)

    nest_out = call(
        nest_kernel,
        sds((4 * LEV, W), F32),
        scratch=[pltpu.VMEM((W, W), F32)] * 3,
        name="nest",
        nbytes=1 << 19,
    )(fourth)
    other = lax.ppermute(nest_out, "member", [(0, 1), (1, 0)])
    mean, variance = call(
        stats_kernel,
        (sds((LEV, 2 * W), F32), sds((LEV, 2 * W), F32)),
        name="stats",
        nbytes=1 << 19,
    )(nest_out, other)
    nest_out = nest_out.reshape(LEV, 2, 2, W).transpose(2, 0, 1, 3)
    nest_out = nest_out.reshape(nest_state.shape)
    return (parent_out.reshape(parent_state.shape), nest_out, mean, variance)


def solution(mesh):
    in_specs = (
        P("member", None, "tile", None),
        P("member", None, "tile"),
        P("tile", None),
        P(),
        P(None, "tile"),
        P(None, "tile"),
    )
    out_specs = (
        P("member", None, "tile", None),
        P("member", None, "tile"),
        P(None, "tile"),
        P(None, "tile"),
    )
    return jax.shard_map(
        on_device, mesh=mesh, in_specs=in_specs, out_specs=out_specs, check_vma=False
    )
```

```python
import functools

import jax
import jax.numpy as jnp
import numpy as np
from jax import lax
from jax.experimental import pallas as pl
from jax.experimental.pallas import tpu as pltpu
from jax.sharding import PartitionSpec as P

F32 = jnp.float32
BF16 = jnp.bfloat16
LEV = 81
STEPS = 4
NT = 128
ROWS = 8
W = 128
LPAD = 96
RING = 16
BSTR = LPAD * RING
SENT = 6
FLAT = 2 * LEV * ROWS
HALO_ROWS = 992
DIST = ((0, 1), (2, 3), (4, None), (5, None))
SPLIT = 40
PACK = 12
EPACK = 6
CUT = W - LEV
L_TOP = 81
L_REQ = 86
L_INNER = 88
L_DEST = (48, 8)
HORIZ = 0.15
VERT = 0.1
DRAG = 0.1
RELAX = 0.5
IMPL = 0.8
VMEM_LIMIT = 20 * 1024 * 1024


def solve_matrix():
    n = np.full(LEV, 2.0)
    n[0] = n[-1] = 1.0
    a = np.diag(1.0 + IMPL * n)
    a -= IMPL * (np.eye(LEV, k=1) + np.eye(LEV, k=-1))
    return np.linalg.inv(a)


def padded_transpose(m):
    out = np.zeros((W, W))
    out[:LEV, :LEV] = m.T
    return out


def split3(m):
    m = np.asarray(m, np.float64)
    parts = []
    for _ in range(3):
        part = m.astype(jnp.bfloat16)
        parts.append(part)
        m = m - part.astype(np.float64)
    return parts


def constants():
    s = solve_matrix()
    power = [np.linalg.matrix_power(s, k) for k in range(STEPS + 1)]
    keep = 1.0 - RELAX
    inner = power[STEPS].T
    bound = power[STEPS].T * keep**STEPS
    send = np.zeros((2, W, 2, W))
    send[0, :LEV, 0, :SPLIT] = bound[:, :SPLIT]
    send[0, :LEV, 1, SPLIT:LEV] = bound[:, SPLIT:]
    send[1, :LEV, 0, L_INNER:] = inner[:, :SPLIT]
    send[1, :LEV, 1, L_INNER:] = inner[:, SPLIT : 2 * SPLIT]
    send[1, :LEV, 1, L_TOP] = inner[:, 2 * SPLIT]
    for part in range(2):
        for owner in range(2):
            for k in range(STEPS):
                send[part, LEV + k, owner, L_DEST[owner] + part * STEPS + k] = 1.0
    coarse, fine, _ = split3(send.reshape(2 * W, 2 * W))
    send = np.concatenate([coarse, coarse, fine])
    mix = [
        padded_transpose(power[STEPS - k] * RELAX * keep ** (STEPS - 1 - k))
        for k in range(STEPS)
    ]
    edge = np.stack(
        [
            np.concatenate(split3(np.concatenate(mix[:2])), axis=1),
            np.concatenate(split3(np.concatenate(mix[2:])), axis=1),
        ]
    )
    return send, edge


def call(
    body, out_shape, in_specs=None, out_specs=None, scratch=(), name=None, flops=0, nbytes=0
):
    kwargs = {} if in_specs is None else {"in_specs": in_specs}
    if out_specs is not None:
        kwargs["out_specs"] = out_specs
    return pl.pallas_call(
        body,
        out_shape=out_shape,
        scratch_shapes=list(scratch),
        compiler_params=pltpu.CompilerParams(vmem_limit_bytes=VMEM_LIMIT),
        cost_estimate=pl.CostEstimate(
            flops=flops, bytes_accessed=nbytes, transcendentals=0
        ),
        name=name,
        **kwargs,
    )


VM = pl.BlockSpec(memory_space=pltpu.VMEM)
HB = pl.BlockSpec(memory_space=pltpu.HBM)
SM = pl.BlockSpec(memory_space=pltpu.SMEM)


def start_all(pairs, sems):
    copies = [pltpu.make_async_copy(x, y, sems.at[i]) for i, (x, y) in enumerate(pairs)]
    for copy in copies:
        copy.start()
    return copies


def halo_kernel(
    tile_ref, parent_hbm, terrain_hbm, nest_hbm, bidx_hbm, dest_hbm, mix_hbm, shift_hbm,
    parent_ref, first_ref, second_ref, nest_ref, moved_ref, dest_ref, mix_ref,
    terrain_ref, down_ref, up_ref, damp_ref, bidx_ref, shift_ref, sems,
):
    half = FLAT // 2
    copies = start_all(
        [
            (terrain_hbm, terrain_ref),
            (parent_hbm.at[pl.ds(0, half)], parent_ref.at[pl.ds(0, half)]),
            (parent_hbm.at[pl.ds(half, half)], parent_ref.at[pl.ds(half, half)]),
            (bidx_hbm, bidx_ref),
            (dest_hbm, dest_ref),
            (mix_hbm, mix_ref),
            (shift_hbm, shift_ref),
        ]
        + [
            (nest_hbm.at[:, part, b, :], nest_ref.at[b * 2 + part])
            for b in range(2)
            for part in range(2)
        ],
        sems,
    )

    def put(ref, distance, base, count, value):
        coarse, fine = DIST[distance]
        ref[pl.ds(base + coarse, count, stride=SENT), :] = value
        if fine is not None:
            rest = value - value.astype(BF16).astype(F32)
            ref[pl.ds(base + fine, count, stride=SENT), :] = rest

    sides = ((down_ref, (7, 6, 5, 4)), (up_ref, (0, 1, 2, 3)))
    copies[0].wait()
    damp_ref[...] = DRAG * terrain_ref[...].astype(F32) / 3000.0
    for ref, rows in sides:
        ref[HALO_ROWS - 24 :, :] = jnp.zeros((24, W), F32)
        for distance, row in enumerate(rows):
            put(ref, distance, 2 * LEV * SENT, 1, damp_ref[row : row + 1, :])
    for member in range(2):
        copies[1 + member].wait()
        for ref, rows in sides:
            for distance, row in enumerate(rows):
                value = parent_ref[pl.ds(member * half + row, LEV, stride=ROWS), :]
                put(ref, distance, member * LEV * SENT, LEV, value)
    even = jnp.bitwise_and(tile_ref[0], 1) == 0
    down, up = down_ref[...], up_ref[...]
    first_ref[...] = jnp.where(even, down, up).astype(BF16)
    second_ref[...] = jnp.where(even, up, down).astype(BF16)
    for copy in copies[3:]:
        copy.wait()
    for s in range(STEPS):
        idx = bidx_ref[s : s + 1, :]
        col = jnp.bitwise_and(idx, W - 1)
        moved = jnp.bitwise_and(col + shift_ref[s], W - 1)
        moved_ref[s : s + 1, :] = idx - col + moved


def send_kernel(nest_ref, moved_ref, dest_ref, mix_ref, msg_ref, pad_ref):
    zeros = jnp.zeros((W - LEV + 1, W), F32)
    for b in range(2):
        for part in range(2):
            top = part * W
            pad_ref[b, top + LEV - 1 : top + W, :] = zeros
            pad_ref[b, top : top + LEV, :] = nest_ref[b * 2 + part]
            pad_ref[b, top + LEV : top + LEV + STEPS, :] = dest_ref[
                :, part * W : (part + 1) * W
            ].astype(F32)
        value = pad_ref[b]
        coarse = value.astype(BF16)
        fine = (value - coarse.astype(F32)).astype(BF16)
        res = lax.dot_general(
            jnp.concatenate([coarse, fine, coarse], axis=0),
            mix_ref[...],
            (((0,), (0,)), ((), ())),
            preferred_element_type=F32,
        )
        for owner in range(2):
            start = b * 2 * W + owner * W
            msg_ref[start : start + W, :] = res[:, owner * W : (owner + 1) * W]
    lane = lax.broadcasted_iota(jnp.int32, (NT, W), 1)
    tile = lax.broadcasted_iota(jnp.int32, (NT, W), 0)
    asked = jnp.logical_or(lane == L_REQ, lane == L_REQ + 1)
    wanted = tile == L_REQ + jnp.bitwise_and(lane, 1)
    for s in range(STEPS):
        idx = moved_ref[s : s + 1, :]
        owner = jnp.right_shift(idx, 10)
        row = jnp.bitwise_and(jnp.right_shift(idx, 7), ROWS - 1)
        col = jnp.bitwise_and(idx, W - 1)
        mine = jnp.where(tile == owner, 1.0, 0.0).astype(BF16)
        found = []
        for value in (row + 1, col):
            value = jnp.broadcast_to(value.astype(F32), (NT, W))
            value = jnp.where(wanted, value, 0.0).astype(BF16)
            found.append(
                lax.dot_general(
                    mine, value, (((1,), (1,)), ((), ())), preferred_element_type=F32
                )
            )
        cell = (found[0] - 1.0) * W + found[1]
        rows = msg_ref[pl.ds(s, NT, stride=4), :]
        msg_ref[pl.ds(s, NT, stride=4), :] = jnp.where(asked, cell, rows)


def ring_step(read, write, level_stride, coef, own_only=False):
    row = lax.broadcasted_iota(jnp.int32, (ROWS, W), 0)
    last = row == ROWS - 1
    head = row == 0
    c0, c1, h1, v1 = coef
    chunk = 9

    def body(step, carry):
        start = step * chunk
        ends = jnp.maximum(start - 1, 0), jnp.minimum(start + chunk, LEV - 1)
        for member in range(2):
            base = member * level_stride
            column = [read(base + start + k) for k in range(chunk)]
            column = [read(base + ends[0])] + column + [read(base + ends[1])]
            for k in range(chunk):
                (d0, d1), (x0, x1), (u0, u1) = column[k : k + 3]
                f0 = pltpu.roll(x0, ROWS - 1, 0)
                f1 = pltpu.roll(x1, ROWS - 1, 0)
                g0 = pltpu.roll(x0, 1, 0)
                g1 = pltpu.roll(x1, 1, 0)
                near0 = jnp.where(last, f1, f0) + jnp.where(head, g1, g0)
                near0 = near0 + (pltpu.roll(x0, 1, 1) + pltpu.roll(x0, W - 1, 1))
                y0 = c0 * x0 + HORIZ * near0 + VERT * (d0 + u0)
                if own_only:
                    write(member, start + k, y0, None)
                    continue
                near1 = jnp.where(last, f0, f1) + jnp.where(head, g0, g1)
                near1 = near1 + (pltpu.roll(x1, 1, 1) + pltpu.roll(x1, W - 1, 1))
                y1 = c1 * x1 + h1 * near1 + v1 * (d1 + u1)
                write(member, start + k, y0, y1)
        return carry

    lax.fori_loop(0, LEV // chunk, body, 0)


def parent_kernel(
    tile_ref, parent_ref, first_ref, second_ref, terrain_hbm,
    cells_ref, ring_hbm,
    next_ref, prev_ref, halo_ref, damp_ref, a_ref, b_ref, ring_ref, terrain_ref, sems,
):
    copies = start_all([(terrain_hbm, terrain_ref)], sems)
    store = pltpu.make_async_copy(ring_ref, ring_hbm, sems.at[1])
    tile = tile_ref[0]
    even = jnp.bitwise_and(tile, 1) == 0
    first, second = first_ref[...].astype(F32), second_ref[...].astype(F32)
    next_ref[...] = jnp.where(even, first, second)
    prev_ref[...] = jnp.where(even, second, first)
    for ref, rows in ((next_ref, (0, 1, 2, 3)), (prev_ref, (7, 6, 5, 4))):
        for row, (coarse, fine) in zip(rows, DIST):
            for count, base, out in ((2 * LEV, 0, halo_ref), (1, 2 * LEV * SENT, damp_ref)):
                value = ref[pl.ds(base + coarse, count, stride=SENT), :]
                if fine is not None:
                    value = value + ref[pl.ds(base + fine, count, stride=SENT), :]
                out[pl.ds(row, count, stride=ROWS), :] = value
    copies[0].wait()
    damping = DRAG * terrain_ref[...].astype(F32) / 3000.0
    pads = jnp.zeros(((LPAD - LEV) * RING, W), F32)
    for ref in (a_ref, b_ref, ring_ref):
        for member in range(2):
            top = member * BSTR + LEV * RING
            ref[top : top + (LPAD - LEV) * RING, :] = pads
    for s in range(STEPS):
        for member in range(2):
            start = LPAD if s else LEV - 1
            cells_ref[s, member * W + start : (member + 1) * W, :] = jnp.zeros(
                (W - start, ROWS * W), BF16
            )
    row = lax.broadcasted_iota(jnp.int32, (ROWS, W), 0)
    south = jnp.where(tile < NT - 1, 1.0, 0.0).astype(F32)
    north = jnp.where(tile > 0, 1.0, 0.0).astype(F32)
    valid = jnp.where(row < 4, south, north)
    stay = 1.0 - 4.0 * HORIZ - 2.0 * VERT
    coef = (stay - damping, (stay - damp_ref[...]) * valid, HORIZ * valid, VERT * valid)

    def emit(s, ref, count, stride):
        for member in range(2):
            for y in range(ROWS):
                start = member * count * stride + y
                rows = ref[pl.ds(start, count, stride=stride), :]
                cells_ref[s, member * W : member * W + count, y * W : (y + 1) * W] = (
                    rows.astype(BF16)
                )

    def read_first(index):
        base = pl.multiple_of(index * ROWS, ROWS)
        return parent_ref[pl.ds(base, ROWS), :], halo_ref[pl.ds(base, ROWS), :]

    emit(0, parent_ref, LEV, ROWS)
    read, stride = read_first, LEV
    for s, dst in zip(range(1, STEPS), (a_ref, b_ref, ring_ref)):

        def write(member, level, y0, y1, dst=dst):
            base = pl.multiple_of((member * LPAD + level) * RING, RING)
            dst[pl.ds(base, ROWS), :] = y0
            dst[pl.ds(base + ROWS, ROWS), :] = y1

        ring_step(read, write, stride, coef)
        if s == STEPS - 1:
            store.start()
        emit(s, dst, LPAD, RING)

        def read(index, src=dst):
            base = pl.multiple_of(index * RING, RING)
            return src[pl.ds(base, ROWS), :], src[pl.ds(base + ROWS, ROWS), :]

        stride = LPAD
    store.wait()


def last_parent_kernel(ring_hbm, terrain_hbm, out_ref, ring_ref, terrain_ref, sems):
    for copy in start_all([(ring_hbm, ring_ref), (terrain_hbm, terrain_ref)], sems):
        copy.wait()
    damping = DRAG * terrain_ref[...].astype(F32) / 3000.0
    stay = 1.0 - 4.0 * HORIZ - 2.0 * VERT

    def read(index):
        base = pl.multiple_of(index * RING, RING)
        return ring_ref[pl.ds(base, ROWS), :], ring_ref[pl.ds(base + ROWS, ROWS), :]

    def write(member, level, y0, y1):
        out_ref[member * LEV + level] = y0

    ring_step(read, write, LPAD, (stay - damping, None, None, None), own_only=True)


def gather_kernel(got_ref, cells_ref, out_ref, scr_ref):
    cell = lax.broadcasted_iota(jnp.int32, (NT, ROWS * W), 1).astype(F32)
    lane = lax.broadcasted_iota(jnp.int32, (NT, W), 1)
    rows = {}
    for s in range(STEPS):
        asked = got_ref[pl.ds(s, NT, stride=4), :]
        hot = [
            jnp.where(cell == asked[:, L_REQ + c : L_REQ + c + 1], 1.0, 0.0).astype(BF16)
            for c in range(2)
        ]
        hot = jnp.concatenate(hot, axis=0)
        res = lax.dot_general(
            hot, cells_ref[s], (((1,), (1,)), ((), ())), preferred_element_type=F32
        )
        for b in range(2):
            for c in range(2):
                rows[b * 8 + s * 2 + c] = res[c * W : (c + 1) * W, b * W : (b + 1) * W]
    for r in range(PACK):
        row = rows[r]
        if r < 8:
            extra = rows[PACK + r // 2]
            if r % 2 == 0:
                row = row + pltpu.roll(jnp.where(lane < CUT, extra, 0.0), LEV, 1)
            else:
                row = row + pltpu.roll(jnp.where(lane < CUT, 0.0, extra), LEV - CUT, 1)
        scr_ref[pl.ds(r, NT, stride=PACK), :] = row
    out_ref[...] = scr_ref[...].astype(BF16)


def regroup_kernel(bperm_ref, got_ref, out_ref, scr_ref, scr2_ref):
    scr_ref[...] = got_ref[...].astype(F32)
    low = lax.broadcasted_iota(jnp.int32, (NT, W), 1) < CUT

    def row(r):
        if r < PACK:
            return scr_ref[pl.ds(r, NT, stride=PACK), :]
        first = pltpu.roll(row(2 * (r - PACK)), W - LEV, 1)
        second = pltpu.roll(row(2 * (r - PACK) + 1), W - LEV + CUT, 1)
        return jnp.where(low, first, second)

    sub = lax.broadcasted_iota(jnp.int32, (2 * NT, W), 0)
    lane = lax.broadcasted_iota(jnp.int32, (2 * NT, W), 1)
    parity = jnp.bitwise_and(jnp.right_shift(lane, 5), 1)
    target = sub - parity * NT
    found = {}
    for s in range(STEPS):
        owner = jnp.right_shift(bperm_ref[s : s + 1, :], 10)
        hot = jnp.where(target == owner, 1.0, 0.0).astype(BF16)
        values = jnp.concatenate(
            [
                jnp.concatenate(
                    [row(b * 8 + s * 2 + c) for b in range(2)],
                    axis=1,
                )
                for c in range(2)
            ],
            axis=0,
        ).astype(BF16)
        res = lax.dot_general(
            hot, values, (((0,), (0,)), ((), ())), preferred_element_type=F32
        )
        for b in range(2):
            for j in range(4):
                found[b, s // 2, (s % 2) * 4 + j] = res[
                    j * 32 : (j + 1) * 32, b * W : (b + 1) * W
                ]
    lane = lax.broadcasted_iota(jnp.int32, (32, W), 1)
    for b in range(2):
        for half in range(2):
            for r in range(EPACK):
                value = found[b, half, r]
                if r < 4:
                    extra = found[b, half, EPACK + r // 2]
                    turn = LEV if r % 2 == 0 else LEV - CUT
                    value = jnp.where(lane < LEV, value, pltpu.roll(extra, turn, 1))
                start = (b * 64 + half * 32) * EPACK + r
                scr2_ref[pl.ds(start, 32, stride=EPACK), :] = value
    out_ref[...] = scr2_ref[...].astype(BF16)


def plan_kernel(tile_ref, got_ref, hot_ref, base_ref):
    late = jnp.bitwise_and(jnp.right_shift(tile_ref[0], 5), 1) == 1
    n = 4 * NT
    turned = [got_ref[pl.ds(j, NT, stride=4), :].T for j in range(4)]
    sub = lax.broadcasted_iota(jnp.int32, (n, n), 0)

    def pick(early_value, late_value):
        return jnp.where(late, late_value, early_value)

    def one_hot(row):
        return jnp.where(sub == row, 1.0, 0.0).astype(BF16)

    def dest(part, s):
        k = part * STEPS + s
        row = jnp.concatenate(
            [
                pick(
                    t[L_DEST[0] + k : L_DEST[0] + k + 1, :],
                    t[L_DEST[1] + k : L_DEST[1] + k + 1, :],
                )
                for t in turned
            ],
            axis=1,
        )
        row = (row + 0.5).astype(jnp.int32)
        return jnp.right_shift(row, 8), jnp.bitwise_and(row, 3)

    def finals(part):
        tile_to, slot_to = dest(part, STEPS - 1)
        rows = {STEPS - 1: tile_to * 4 + slot_to}
        for s in range(STEPS - 2, -1, -1):
            mid_tile, mid_slot = dest(part, s)
            move = one_hot(mid_slot * NT + mid_tile)
            later = jnp.concatenate(
                [
                    jnp.broadcast_to(tile_to, (8, n)),
                    jnp.broadcast_to(slot_to, (8, n)),
                ],
                axis=0,
            )
            both = jnp.dot(
                later.astype(F32).astype(BF16), move, preferred_element_type=F32
            )
            tile_to = both[0:1, :].astype(jnp.int32)
            slot_to = both[8:9, :].astype(jnp.int32)
            rows[s] = tile_to * 4 + slot_to
        return rows

    columns = jnp.concatenate(
        [got_ref[pl.ds(j, NT, stride=4), :] for j in range(4)], axis=0
    )
    parts = []
    for _ in range(3):
        part = columns.astype(BF16)
        parts.append(part)
        columns = columns - part.astype(F32)
    parts = jnp.concatenate(parts, axis=1)

    def moved(row):
        res = jnp.dot(one_hot(row), parts, preferred_element_type=F32)
        return res[:, :W] + (res[:, W : 2 * W] + res[:, 2 * W :])

    bound = finals(0)
    hot_ref[0] = one_hot(pick(bound[0], bound[2]))
    hot_ref[1] = one_hot(pick(bound[1], bound[3]))
    outer = moved(bound[0])
    inner = moved(finals(1)[0])
    lane = lax.broadcasted_iota(jnp.int32, (n, W), 1)
    low = pick(0, SPLIT)
    high = pick(SPLIT, LEV)
    extra = pick(W, L_TOP)
    is_inner = jnp.logical_or(lane >= L_INNER, lane == extra)
    is_outer = jnp.logical_and(lane >= low, lane < high)
    base_ref[...] = jnp.where(is_outer, outer, jnp.where(is_inner, inner, 0.0))


def owner_kernel(tile_ref, got_ref, hot_ref, base_ref, mix_ref, out_ref, scr_ref):
    late = jnp.bitwise_and(jnp.right_shift(tile_ref[0], 5), 1)
    scr_ref[...] = got_ref[...].astype(F32)
    low = lax.broadcasted_iota(jnp.int32, (NT, W), 1) < CUT

    def row(r):
        if r < EPACK:
            return scr_ref[pl.ds(r, NT, stride=EPACK), :]
        first = pltpu.roll(row(2 * (r - EPACK)), W - LEV, 1)
        second = pltpu.roll(row(2 * (r - EPACK) + 1), W - LEV + CUT, 1)
        return jnp.where(low, first, second)

    moved = []
    for s in range(2):
        edge = jnp.concatenate([row(s * 4 + j) for j in range(4)], axis=0).astype(BF16)
        moved.append(jnp.dot(hot_ref[s], edge, preferred_element_type=F32).astype(BF16))
    total = jnp.dot(
        jnp.concatenate(moved, axis=1), mix_ref[late], preferred_element_type=F32
    )
    out_ref[...] = base_ref[...] + (
        total[:, :W] + (total[:, W : 2 * W] + total[:, 2 * W :])
    )


def nest_kernel(got_ref, out_ref, sum_ref, early_ref, late_ref):
    for b in range(2):
        early = got_ref[b * 2 * W : b * 2 * W + W, :]
        late = got_ref[b * 2 * W + W : (b + 1) * 2 * W, :]
        sum_ref[...] = (early + late).T
        early_ref[...] = early.T
        late_ref[...] = late.T
        out_ref[pl.ds(b, LEV, stride=4), :] = sum_ref[:LEV, :]
        inner = 2 + b
        out_ref[pl.ds(inner, SPLIT, stride=4), :] = early_ref[L_INNER:, :]
        out_ref[pl.ds(inner + 4 * SPLIT, SPLIT, stride=4), :] = late_ref[L_INNER:, :]
        top = inner + 8 * SPLIT
        out_ref[top : top + 1, :] = late_ref[L_TOP : L_TOP + 1, :]


def stats_kernel(own_ref, other_ref, mean_ref, var_ref):
    for half in range(2):
        a0, a1, b0, b1 = (
            ref[pl.ds(half * 2 + b, LEV, stride=4), :]
            for ref in (own_ref, other_ref)
            for b in range(2)
        )
        lanes = slice(half * W, (half + 1) * W)
        mean = ((a0 + a1) + (b0 + b1)) / 4.0
        mean_ref[:, lanes] = mean
        own = (a0 - mean) * (a0 - mean) + (a1 - mean) * (a1 - mean)
        other = (b0 - mean) * (b0 - mean) + (b1 - mean) * (b1 - mean)
        var_ref[:, lanes] = (own + other) / 4.0


def in_hbm(x):
    return pltpu.with_memory_space_constraint(x, pltpu.HBM)


def exchange(x):
    return lax.all_to_all(x, "tile", split_axis=0, concat_axis=0, tiled=True)


def on_device(parent_state, nest_state, terrain, shift_x, boundary_index, reloc_dest):
    q_mix, e_mix = constants()
    q_mix, e_mix = jnp.asarray(q_mix), jnp.asarray(e_mix)
    sds = jax.ShapeDtypeStruct
    tile = lax.axis_index("tile").astype(jnp.int32).reshape(1)
    parent = parent_state.reshape(FLAT, W)

    nest = nest_state.reshape(2, LEV, 2, W).transpose(1, 2, 0, 3)
    kept, down, up, nest, moved, dest, q_mix = call(
        halo_kernel,
        (
            pltpu.VMEM((FLAT, W), F32),
            sds((HALO_ROWS, W), BF16),
            sds((HALO_ROWS, W), BF16),
            pltpu.VMEM((4, LEV, W), F32),
            pltpu.VMEM((STEPS, NT), jnp.int32),
            pltpu.VMEM((STEPS, 2 * W), jnp.int32),
            pltpu.VMEM((6 * W, 2 * W), BF16),
        ),
        in_specs=[SM, HB, HB, HB, HB, HB, HB, HB],
        scratch=[
            pltpu.VMEM((ROWS, W), jnp.int32),
            pltpu.VMEM((HALO_ROWS, W), F32),
            pltpu.VMEM((HALO_ROWS, W), F32),
            pltpu.VMEM((ROWS, W), F32),
            pltpu.VMEM((STEPS, NT), jnp.int32),
            pltpu.SMEM((STEPS,), jnp.int32),
            pltpu.SemaphoreType.DMA((11,)),
        ],
        name="halo",
        nbytes=1 << 20,
    )(
        tile,
        in_hbm(parent),
        in_hbm(terrain),
        in_hbm(nest),
        in_hbm(boundary_index),
        in_hbm(reloc_dest),
        in_hbm(q_mix),
        in_hbm(shift_x),
    )
    message = call(
        send_kernel,
        sds((4 * NT, W), F32),
        scratch=[pltpu.VMEM((2, 2 * W, W), F32)],
        name="send",
        nbytes=64 << 20,
    )(nest, moved, dest, q_mix)
    pairs = [(i, i + 1) for i in range(0, NT, 2)] + [(i + 1, i) for i in range(0, NT, 2)]
    gaps = [(i, i + 1) for i in range(1, NT - 1, 2)]
    gaps = gaps + [(i + 1, i) for i in range(1, NT - 1, 2)]
    from_pair = lax.ppermute(down, "tile", pairs)
    from_gap = lax.ppermute(up, "tile", gaps)
    first = exchange(message.reshape(NT, 4, W)).reshape(4 * NT, W)
    cells, ring = call(
        parent_kernel,
        (
            pltpu.VMEM((STEPS, 2 * W, ROWS * W), BF16),
            pltpu.HBM((2 * BSTR, W), F32),
        ),
        in_specs=[SM, VM, VM, VM, HB],
        out_specs=(VM, HB),
        scratch=[
            pltpu.VMEM((HALO_ROWS, W), F32),
            pltpu.VMEM((HALO_ROWS, W), F32),
            pltpu.VMEM((FLAT, W), F32),
            pltpu.VMEM((ROWS, W), F32),
            pltpu.VMEM((2 * BSTR, W), F32),
            pltpu.VMEM((2 * BSTR, W), F32),
            pltpu.VMEM((2 * BSTR, W), F32),
            pltpu.VMEM((ROWS, W), jnp.int32),
            pltpu.SemaphoreType.DMA((2,)),
        ],
        name="parent",
        flops=1 << 33,
        nbytes=1 << 27,
    )(tile, kept, from_pair, from_gap, in_hbm(terrain))

    values = call(
        gather_kernel,
        sds((PACK * NT, W), BF16),
        scratch=[pltpu.VMEM((PACK * NT, W), F32)],
        name="gather",
        flops=1 << 29,
        nbytes=3 << 20,
    )(first, cells)
    second = exchange(values.reshape(PACK // 4 * NT, 4, W)).reshape(PACK * NT, W)

    hot, base = call(
        plan_kernel,
        (sds((2, 4 * NT, 4 * NT), BF16), sds((4 * NT, W), F32)),
        in_specs=[SM, VM],
        name="plan",
        flops=1 << 28,
        nbytes=3 << 20,
    )(tile, first)

    second, hot, base = lax.optimization_barrier((second, hot, base))
    bperm = boundary_index.reshape(STEPS, 32, 4).transpose(0, 2, 1).reshape(STEPS, NT)
    edges = call(
        regroup_kernel,
        sds((EPACK * NT, W), BF16),
        scratch=[pltpu.VMEM((PACK * NT, W), F32), pltpu.VMEM((EPACK * NT, W), F32)],
        name="regroup",
        flops=1 << 26,
        nbytes=1 << 20,
    )(bperm, second)
    third = exchange(edges.reshape(EPACK // 2 * NT, 2, W)).reshape(EPACK * NT, W)

    parent_out = call(
        last_parent_kernel,
        sds((2 * LEV, ROWS, W), F32),
        in_specs=[HB, HB],
        scratch=[
            pltpu.VMEM((2 * BSTR, W), F32),
            pltpu.VMEM((ROWS, W), jnp.int32),
            pltpu.SemaphoreType.DMA((2,)),
        ],
        name="last_parent",
        flops=1 << 22,
        nbytes=2 << 20,
    )(in_hbm(ring), in_hbm(terrain))
    third, parent_out = lax.optimization_barrier((third, parent_out))
    columns = call(
        owner_kernel,
        sds((4 * NT, W), F32),
        in_specs=[SM, VM, VM, VM, VM],
        scratch=[pltpu.VMEM((EPACK * NT, W), F32)],
        name="owner",
        flops=1 << 29,
        nbytes=3 << 20,
    )(tile, third, hot, base, e_mix)
    fourth = exchange(columns.reshape(NT, 4, W)).reshape(4 * NT, W)

    nest_out = call(
        nest_kernel,
        sds((4 * LEV, W), F32),
        scratch=[pltpu.VMEM((W, W), F32)] * 3,
        name="nest",
        nbytes=1 << 19,
    )(fourth)
    other = lax.ppermute(nest_out, "member", [(0, 1), (1, 0)])
    mean, variance = call(
        stats_kernel,
        (sds((LEV, 2 * W), F32), sds((LEV, 2 * W), F32)),
        name="stats",
        nbytes=1 << 19,
    )(nest_out, other)
    nest_out = nest_out.reshape(LEV, 2, 2, W).transpose(2, 0, 1, 3)
    nest_out = nest_out.reshape(nest_state.shape)
    return (parent_out.reshape(parent_state.shape), nest_out, mean, variance)


def solution(mesh):
    in_specs = (
        P("member", None, "tile", None),
        P("member", None, "tile"),
        P("tile", None),
        P(),
        P(None, "tile"),
        P(None, "tile"),
    )
    out_specs = (
        P("member", None, "tile", None),
        P("member", None, "tile"),
        P(None, "tile"),
        P(None, "tile"),
    )
    return jax.shard_map(
        on_device, mesh=mesh, in_specs=in_specs, out_specs=out_specs, check_vma=False
    )
```

```python
import functools

import jax
import jax.numpy as jnp
import numpy as np
from jax import lax
from jax.experimental import pallas as pl
from jax.experimental.pallas import tpu as pltpu
from jax.sharding import PartitionSpec as P

F32 = jnp.float32
BF16 = jnp.bfloat16
LEV = 81
STEPS = 4
NT = 128
ROWS = 8
W = 128
LPAD = 96
RING = 16
BSTR = LPAD * RING
SENT = 6
FLAT = 2 * LEV * ROWS
HALO_ROWS = 992
DIST = ((0, 1), (2, 3), (4, None), (5, None))
SPLIT = 40
PACK = 12
EPACK = 6
CUT = W - LEV
L_TOP = 81
L_REQ = 86
L_INNER = 88
L_DEST = (48, 8)
HORIZ = 0.15
VERT = 0.1
DRAG = 0.1
RELAX = 0.5
IMPL = 0.8
VMEM_LIMIT = 20 * 1024 * 1024


def solve_matrix():
    n = np.full(LEV, 2.0)
    n[0] = n[-1] = 1.0
    a = np.diag(1.0 + IMPL * n)
    a -= IMPL * (np.eye(LEV, k=1) + np.eye(LEV, k=-1))
    return np.linalg.inv(a)


def padded_transpose(m):
    out = np.zeros((W, W))
    out[:LEV, :LEV] = m.T
    return out


def split3(m):
    m = np.asarray(m, np.float64)
    parts = []
    for _ in range(3):
        part = m.astype(jnp.bfloat16)
        parts.append(part)
        m = m - part.astype(np.float64)
    return parts


def constants():
    s = solve_matrix()
    power = [np.linalg.matrix_power(s, k) for k in range(STEPS + 1)]
    keep = 1.0 - RELAX
    inner = power[STEPS].T
    bound = power[STEPS].T * keep**STEPS
    send = np.zeros((2, W, 2, W))
    send[0, :LEV, 0, :SPLIT] = bound[:, :SPLIT]
    send[0, :LEV, 1, SPLIT:LEV] = bound[:, SPLIT:]
    send[1, :LEV, 0, L_INNER:] = inner[:, :SPLIT]
    send[1, :LEV, 1, L_INNER:] = inner[:, SPLIT : 2 * SPLIT]
    send[1, :LEV, 1, L_TOP] = inner[:, 2 * SPLIT]
    for part in range(2):
        for owner in range(2):
            for k in range(STEPS):
                send[part, LEV + k, owner, L_DEST[owner] + part * STEPS + k] = 1.0
    coarse, fine, _ = split3(send.reshape(2 * W, 2 * W))
    send = np.concatenate([coarse, coarse, fine])
    mix = [
        padded_transpose(power[STEPS - k] * RELAX * keep ** (STEPS - 1 - k))
        for k in range(STEPS)
    ]
    edge = np.stack(
        [
            np.concatenate(split3(np.concatenate(mix[:2])), axis=1),
            np.concatenate(split3(np.concatenate(mix[2:])), axis=1),
        ]
    )
    return send, edge


def call(
    body, out_shape, in_specs=None, out_specs=None, scratch=(), name=None, flops=0, nbytes=0
):
    kwargs = {} if in_specs is None else {"in_specs": in_specs}
    if out_specs is not None:
        kwargs["out_specs"] = out_specs
    return pl.pallas_call(
        body,
        out_shape=out_shape,
        scratch_shapes=list(scratch),
        compiler_params=pltpu.CompilerParams(vmem_limit_bytes=VMEM_LIMIT),
        cost_estimate=pl.CostEstimate(
            flops=flops, bytes_accessed=nbytes, transcendentals=0
        ),
        name=name,
        **kwargs,
    )


VM = pl.BlockSpec(memory_space=pltpu.VMEM)
HB = pl.BlockSpec(memory_space=pltpu.HBM)
SM = pl.BlockSpec(memory_space=pltpu.SMEM)


def start_all(pairs, sems):
    copies = [pltpu.make_async_copy(x, y, sems.at[i]) for i, (x, y) in enumerate(pairs)]
    for copy in copies:
        copy.start()
    return copies


def halo_kernel(
    tile_ref, parent_hbm, terrain_hbm, nest_hbm, bidx_hbm, dest_hbm, mix_hbm, shift_hbm,
    parent_ref, first_ref, second_ref, nest_ref, moved_ref, dest_ref, mix_ref,
    terrain_ref, down_ref, up_ref, damp_ref, bidx_ref, shift_ref, sems,
):
    copies = start_all(
        [
            (parent_hbm, parent_ref),
            (terrain_hbm, terrain_ref),
            (bidx_hbm, bidx_ref),
            (dest_hbm, dest_ref),
            (mix_hbm, mix_ref),
            (shift_hbm, shift_ref),
        ]
        + [
            (nest_hbm.at[:, part, b, :], nest_ref.at[b * 2 + part])
            for b in range(2)
            for part in range(2)
        ],
        sems,
    )
    for copy in copies[:2]:
        copy.wait()
    damp_ref[...] = DRAG * terrain_ref[...].astype(F32) / 3000.0
    for ref, rows in ((down_ref, (7, 6, 5, 4)), (up_ref, (0, 1, 2, 3))):
        ref[HALO_ROWS - 24 :, :] = jnp.zeros((24, W), F32)
        for row, (coarse, fine) in zip(rows, DIST):
            for count, base, value in (
                (2 * LEV, 0, parent_ref[pl.ds(row, 2 * LEV, stride=ROWS), :]),
                (1, 2 * LEV * SENT, damp_ref[row : row + 1, :]),
            ):
                ref[pl.ds(base + coarse, count, stride=SENT), :] = value
                if fine is not None:
                    rest = value - value.astype(BF16).astype(F32)
                    ref[pl.ds(base + fine, count, stride=SENT), :] = rest
    even = jnp.bitwise_and(tile_ref[0], 1) == 0
    down, up = down_ref[...], up_ref[...]
    first_ref[...] = jnp.where(even, down, up).astype(BF16)
    second_ref[...] = jnp.where(even, up, down).astype(BF16)
    for copy in copies[2:]:
        copy.wait()
    for s in range(STEPS):
        idx = bidx_ref[s : s + 1, :]
        col = jnp.bitwise_and(idx, W - 1)
        moved = jnp.bitwise_and(col + shift_ref[s], W - 1)
        moved_ref[s : s + 1, :] = idx - col + moved


def send_kernel(nest_ref, moved_ref, dest_ref, mix_ref, msg_ref, pad_ref):
    zeros = jnp.zeros((W - LEV + 1, W), F32)
    for b in range(2):
        for part in range(2):
            top = part * W
            pad_ref[b, top + LEV - 1 : top + W, :] = zeros
            pad_ref[b, top : top + LEV, :] = nest_ref[b * 2 + part]
            pad_ref[b, top + LEV : top + LEV + STEPS, :] = dest_ref[
                :, part * W : (part + 1) * W
            ].astype(F32)
        value = pad_ref[b]
        coarse = value.astype(BF16)
        fine = (value - coarse.astype(F32)).astype(BF16)
        res = lax.dot_general(
            jnp.concatenate([coarse, fine, coarse], axis=0),
            mix_ref[...],
            (((0,), (0,)), ((), ())),
            preferred_element_type=F32,
        )
        for owner in range(2):
            start = b * 2 * W + owner * W
            msg_ref[start : start + W, :] = res[:, owner * W : (owner + 1) * W]
    lane = lax.broadcasted_iota(jnp.int32, (NT, W), 1)
    tile = lax.broadcasted_iota(jnp.int32, (NT, W), 0)
    asked = jnp.logical_or(lane == L_REQ, lane == L_REQ + 1)
    wanted = tile == L_REQ + jnp.bitwise_and(lane, 1)
    for s in range(STEPS):
        idx = moved_ref[s : s + 1, :]
        owner = jnp.right_shift(idx, 10)
        row = jnp.bitwise_and(jnp.right_shift(idx, 7), ROWS - 1)
        col = jnp.bitwise_and(idx, W - 1)
        mine = jnp.where(tile == owner, 1.0, 0.0).astype(BF16)
        found = []
        for value in (row + 1, col):
            value = jnp.broadcast_to(value.astype(F32), (NT, W))
            value = jnp.where(wanted, value, 0.0).astype(BF16)
            found.append(
                lax.dot_general(
                    mine, value, (((1,), (1,)), ((), ())), preferred_element_type=F32
                )
            )
        cell = (found[0] - 1.0) * W + found[1]
        rows = msg_ref[pl.ds(s, NT, stride=4), :]
        msg_ref[pl.ds(s, NT, stride=4), :] = jnp.where(asked, cell, rows)


def ring_step(read, write, level_stride, coef, own_only=False):
    row = lax.broadcasted_iota(jnp.int32, (ROWS, W), 0)
    last = row == ROWS - 1
    head = row == 0
    c0, c1, h1, v1 = coef
    chunk = 9

    def body(step, carry):
        start = step * chunk
        ends = jnp.maximum(start - 1, 0), jnp.minimum(start + chunk, LEV - 1)
        for member in range(2):
            base = member * level_stride
            column = [read(base + start + k) for k in range(chunk)]
            column = [read(base + ends[0])] + column + [read(base + ends[1])]
            for k in range(chunk):
                (d0, d1), (x0, x1), (u0, u1) = column[k : k + 3]
                f0 = pltpu.roll(x0, ROWS - 1, 0)
                f1 = pltpu.roll(x1, ROWS - 1, 0)
                g0 = pltpu.roll(x0, 1, 0)
                g1 = pltpu.roll(x1, 1, 0)
                near0 = jnp.where(last, f1, f0) + jnp.where(head, g1, g0)
                near0 = near0 + (pltpu.roll(x0, 1, 1) + pltpu.roll(x0, W - 1, 1))
                y0 = c0 * x0 + HORIZ * near0 + VERT * (d0 + u0)
                if own_only:
                    write(member, start + k, y0, None)
                    continue
                near1 = jnp.where(last, f0, f1) + jnp.where(head, g0, g1)
                near1 = near1 + (pltpu.roll(x1, 1, 1) + pltpu.roll(x1, W - 1, 1))
                y1 = c1 * x1 + h1 * near1 + v1 * (d1 + u1)
                write(member, start + k, y0, y1)
        return carry

    lax.fori_loop(0, LEV // chunk, body, 0)


def parent_kernel(
    tile_ref, parent_ref, second_ref, first_ref, terrain_hbm,
    cells_ref, ring_hbm,
    next_ref, prev_ref, halo_ref, damp_ref, a_ref, b_ref, ring_ref, terrain_ref, sems,
):
    copies = start_all([(terrain_hbm, terrain_ref)], sems)
    store = pltpu.make_async_copy(ring_ref, ring_hbm, sems.at[1])
    tile = tile_ref[0]
    even = jnp.bitwise_and(tile, 1) == 0
    first, second = first_ref[...].astype(F32), second_ref[...].astype(F32)
    next_ref[...] = jnp.where(even, first, second)
    prev_ref[...] = jnp.where(even, second, first)
    for ref, rows in ((next_ref, (0, 1, 2, 3)), (prev_ref, (7, 6, 5, 4))):
        for row, (coarse, fine) in zip(rows, DIST):
            for count, base, out in ((2 * LEV, 0, halo_ref), (1, 2 * LEV * SENT, damp_ref)):
                value = ref[pl.ds(base + coarse, count, stride=SENT), :]
                if fine is not None:
                    value = value + ref[pl.ds(base + fine, count, stride=SENT), :]
                out[pl.ds(row, count, stride=ROWS), :] = value
    copies[0].wait()
    damping = DRAG * terrain_ref[...].astype(F32) / 3000.0
    pads = jnp.zeros(((LPAD - LEV) * RING, W), F32)
    for ref in (a_ref, b_ref, ring_ref):
        for member in range(2):
            top = member * BSTR + LEV * RING
            ref[top : top + (LPAD - LEV) * RING, :] = pads
    for s in range(STEPS):
        for member in range(2):
            start = LPAD if s else LEV - 1
            cells_ref[s, member * W + start : (member + 1) * W, :] = jnp.zeros(
                (W - start, ROWS * W), BF16
            )
    row = lax.broadcasted_iota(jnp.int32, (ROWS, W), 0)
    south = jnp.where(tile < NT - 1, 1.0, 0.0).astype(F32)
    north = jnp.where(tile > 0, 1.0, 0.0).astype(F32)
    valid = jnp.where(row < 4, south, north)
    stay = 1.0 - 4.0 * HORIZ - 2.0 * VERT
    coef = (stay - damping, (stay - damp_ref[...]) * valid, HORIZ * valid, VERT * valid)

    def emit(s, ref, count, stride):
        for member in range(2):
            for y in range(ROWS):
                start = member * count * stride + y
                rows = ref[pl.ds(start, count, stride=stride), :]
                cells_ref[s, member * W : member * W + count, y * W : (y + 1) * W] = (
                    rows.astype(BF16)
                )

    def read_first(index):
        base = pl.multiple_of(index * ROWS, ROWS)
        return parent_ref[pl.ds(base, ROWS), :], halo_ref[pl.ds(base, ROWS), :]

    emit(0, parent_ref, LEV, ROWS)
    read, stride = read_first, LEV
    for s, dst in zip(range(1, STEPS), (a_ref, b_ref, ring_ref)):

        def write(member, level, y0, y1, dst=dst):
            base = pl.multiple_of((member * LPAD + level) * RING, RING)
            dst[pl.ds(base, ROWS), :] = y0
            dst[pl.ds(base + ROWS, ROWS), :] = y1

        ring_step(read, write, stride, coef)
        if s == STEPS - 1:
            store.start()
        emit(s, dst, LPAD, RING)

        def read(index, src=dst):
            base = pl.multiple_of(index * RING, RING)
            return src[pl.ds(base, ROWS), :], src[pl.ds(base + ROWS, ROWS), :]

        stride = LPAD
    store.wait()


def last_parent_kernel(ring_hbm, terrain_hbm, out_ref, ring_ref, terrain_ref, sems):
    for copy in start_all([(ring_hbm, ring_ref), (terrain_hbm, terrain_ref)], sems):
        copy.wait()
    damping = DRAG * terrain_ref[...].astype(F32) / 3000.0
    stay = 1.0 - 4.0 * HORIZ - 2.0 * VERT

    def read(index):
        base = pl.multiple_of(index * RING, RING)
        return ring_ref[pl.ds(base, ROWS), :], ring_ref[pl.ds(base + ROWS, ROWS), :]

    def write(member, level, y0, y1):
        out_ref[member * LEV + level] = y0

    ring_step(read, write, LPAD, (stay - damping, None, None, None), own_only=True)


def gather_kernel(got_ref, cells_ref, out_ref, scr_ref):
    cell = lax.broadcasted_iota(jnp.int32, (NT, ROWS * W), 1).astype(F32)
    lane = lax.broadcasted_iota(jnp.int32, (NT, W), 1)
    rows = {}
    for s in range(STEPS):
        asked = got_ref[pl.ds(s, NT, stride=4), :]
        hot = [
            jnp.where(cell == asked[:, L_REQ + c : L_REQ + c + 1], 1.0, 0.0).astype(BF16)
            for c in range(2)
        ]
        hot = jnp.concatenate(hot, axis=0)
        res = lax.dot_general(
            hot, cells_ref[s], (((1,), (1,)), ((), ())), preferred_element_type=F32
        )
        for b in range(2):
            for c in range(2):
                rows[b * 8 + s * 2 + c] = res[c * W : (c + 1) * W, b * W : (b + 1) * W]
    for r in range(PACK):
        row = rows[r]
        if r < 8:
            extra = rows[PACK + r // 2]
            if r % 2 == 0:
                row = row + pltpu.roll(jnp.where(lane < CUT, extra, 0.0), LEV, 1)
            else:
                row = row + pltpu.roll(jnp.where(lane < CUT, 0.0, extra), LEV - CUT, 1)
        scr_ref[pl.ds(r, NT, stride=PACK), :] = row
    out_ref[...] = scr_ref[...].astype(BF16)


def regroup_kernel(select_ref, got_ref, out_ref, scr_ref, scr2_ref):
    scr_ref[...] = got_ref[...].astype(F32)
    low = lax.broadcasted_iota(jnp.int32, (NT, W), 1) < CUT

    def row(r):
        if r < PACK:
            return scr_ref[pl.ds(r, NT, stride=PACK), :]
        first = pltpu.roll(row(2 * (r - PACK)), W - LEV, 1)
        second = pltpu.roll(row(2 * (r - PACK) + 1), W - LEV + CUT, 1)
        return jnp.where(low, first, second)

    found = {}
    for s in range(STEPS):
        values = jnp.concatenate(
            [
                jnp.concatenate(
                    [row(b * 8 + s * 2 + c) for b in range(2)],
                    axis=1,
                )
                for c in range(2)
            ],
            axis=0,
        ).astype(BF16)
        res = jnp.dot(select_ref[s], values, preferred_element_type=F32)
        for b in range(2):
            for j in range(4):
                found[b, s // 2, (s % 2) * 4 + j] = res[
                    j * 32 : (j + 1) * 32, b * W : (b + 1) * W
                ]
    lane = lax.broadcasted_iota(jnp.int32, (32, W), 1)
    for b in range(2):
        for half in range(2):
            for r in range(EPACK):
                value = found[b, half, r]
                if r < 4:
                    extra = found[b, half, EPACK + r // 2]
                    turn = LEV if r % 2 == 0 else LEV - CUT
                    value = jnp.where(lane < LEV, value, pltpu.roll(extra, turn, 1))
                start = (b * 64 + half * 32) * EPACK + r
                scr2_ref[pl.ds(start, 32, stride=EPACK), :] = value
    out_ref[...] = scr2_ref[...].astype(BF16)


def plan_kernel(tile_ref, got_ref, bperm_ref, hot_ref, base_ref, select_ref):
    sub = lax.broadcasted_iota(jnp.int32, (2 * NT, W), 0)
    lane = lax.broadcasted_iota(jnp.int32, (2 * NT, W), 1)
    parity = jnp.bitwise_and(jnp.right_shift(lane, 5), 1)
    target = sub - parity * NT
    for s in range(STEPS):
        owner = jnp.right_shift(bperm_ref[s : s + 1, :], 10)
        select_ref[s] = jnp.where(target == owner, 1.0, 0.0).T.astype(BF16)
    late = jnp.bitwise_and(jnp.right_shift(tile_ref[0], 5), 1) == 1
    n = 4 * NT
    turned = [got_ref[pl.ds(j, NT, stride=4), :].T for j in range(4)]
    sub = lax.broadcasted_iota(jnp.int32, (n, n), 0)

    def pick(early_value, late_value):
        return jnp.where(late, late_value, early_value)

    def one_hot(row):
        return jnp.where(sub == row, 1.0, 0.0).astype(BF16)

    def dest(part, s):
        k = part * STEPS + s
        row = jnp.concatenate(
            [
                pick(
                    t[L_DEST[0] + k : L_DEST[0] + k + 1, :],
                    t[L_DEST[1] + k : L_DEST[1] + k + 1, :],
                )
                for t in turned
            ],
            axis=1,
        )
        row = (row + 0.5).astype(jnp.int32)
        return jnp.right_shift(row, 8), jnp.bitwise_and(row, 3)

    def finals(part):
        tile_to, slot_to = dest(part, STEPS - 1)
        rows = {STEPS - 1: tile_to * 4 + slot_to}
        for s in range(STEPS - 2, -1, -1):
            mid_tile, mid_slot = dest(part, s)
            move = one_hot(mid_slot * NT + mid_tile)
            later = jnp.concatenate(
                [
                    jnp.broadcast_to(tile_to, (8, n)),
                    jnp.broadcast_to(slot_to, (8, n)),
                ],
                axis=0,
            )
            both = jnp.dot(
                later.astype(F32).astype(BF16), move, preferred_element_type=F32
            )
            tile_to = both[0:1, :].astype(jnp.int32)
            slot_to = both[8:9, :].astype(jnp.int32)
            rows[s] = tile_to * 4 + slot_to
        return rows

    columns = jnp.concatenate(
        [got_ref[pl.ds(j, NT, stride=4), :] for j in range(4)], axis=0
    )
    parts = []
    for _ in range(3):
        part = columns.astype(BF16)
        parts.append(part)
        columns = columns - part.astype(F32)
    parts = jnp.concatenate(parts, axis=1)

    def moved(row):
        res = jnp.dot(one_hot(row), parts, preferred_element_type=F32)
        return res[:, :W] + (res[:, W : 2 * W] + res[:, 2 * W :])

    bound = finals(0)
    hot_ref[0] = one_hot(pick(bound[0], bound[2]))
    hot_ref[1] = one_hot(pick(bound[1], bound[3]))
    outer = moved(bound[0])
    inner = moved(finals(1)[0])
    lane = lax.broadcasted_iota(jnp.int32, (n, W), 1)
    low = pick(0, SPLIT)
    high = pick(SPLIT, LEV)
    extra = pick(W, L_TOP)
    is_inner = jnp.logical_or(lane >= L_INNER, lane == extra)
    is_outer = jnp.logical_and(lane >= low, lane < high)
    base_ref[...] = jnp.where(is_outer, outer, jnp.where(is_inner, inner, 0.0))


def owner_kernel(tile_ref, got_ref, hot_ref, base_ref, mix_ref, out_ref, scr_ref):
    late = jnp.bitwise_and(jnp.right_shift(tile_ref[0], 5), 1)
    scr_ref[...] = got_ref[...].astype(F32)
    low = lax.broadcasted_iota(jnp.int32, (NT, W), 1) < CUT

    def row(r):
        if r < EPACK:
            return scr_ref[pl.ds(r, NT, stride=EPACK), :]
        first = pltpu.roll(row(2 * (r - EPACK)), W - LEV, 1)
        second = pltpu.roll(row(2 * (r - EPACK) + 1), W - LEV + CUT, 1)
        return jnp.where(low, first, second)

    moved = []
    for s in range(2):
        edge = jnp.concatenate([row(s * 4 + j) for j in range(4)], axis=0).astype(BF16)
        moved.append(jnp.dot(hot_ref[s], edge, preferred_element_type=F32).astype(BF16))
    total = jnp.dot(
        jnp.concatenate(moved, axis=1), mix_ref[late], preferred_element_type=F32
    )
    out_ref[...] = base_ref[...] + (
        total[:, :W] + (total[:, W : 2 * W] + total[:, 2 * W :])
    )


def nest_kernel(got_ref, out_ref, sum_ref, early_ref, late_ref):
    for b in range(2):
        early = got_ref[b * 2 * W : b * 2 * W + W, :]
        late = got_ref[b * 2 * W + W : (b + 1) * 2 * W, :]
        sum_ref[...] = (early + late).T
        early_ref[...] = early.T
        late_ref[...] = late.T
        out_ref[pl.ds(b, LEV, stride=4), :] = sum_ref[:LEV, :]
        inner = 2 + b
        out_ref[pl.ds(inner, SPLIT, stride=4), :] = early_ref[L_INNER:, :]
        out_ref[pl.ds(inner + 4 * SPLIT, SPLIT, stride=4), :] = late_ref[L_INNER:, :]
        top = inner + 8 * SPLIT
        out_ref[top : top + 1, :] = late_ref[L_TOP : L_TOP + 1, :]


def stats_kernel(own_ref, other_ref, mean_ref, var_ref):
    for half in range(2):
        a0, a1, b0, b1 = (
            ref[pl.ds(half * 2 + b, LEV, stride=4), :]
            for ref in (own_ref, other_ref)
            for b in range(2)
        )
        lanes = slice(half * W, (half + 1) * W)
        mean = ((a0 + a1) + (b0 + b1)) / 4.0
        mean_ref[:, lanes] = mean
        own = (a0 - mean) * (a0 - mean) + (a1 - mean) * (a1 - mean)
        other = (b0 - mean) * (b0 - mean) + (b1 - mean) * (b1 - mean)
        var_ref[:, lanes] = (own + other) / 4.0


def in_hbm(x):
    return pltpu.with_memory_space_constraint(x, pltpu.HBM)


def exchange(x):
    return lax.all_to_all(x, "tile", split_axis=0, concat_axis=0, tiled=True)


def on_device(parent_state, nest_state, terrain, shift_x, boundary_index, reloc_dest):
    q_mix, e_mix = constants()
    q_mix, e_mix = jnp.asarray(q_mix), jnp.asarray(e_mix)
    sds = jax.ShapeDtypeStruct
    tile = lax.axis_index("tile").astype(jnp.int32).reshape(1)
    parent = parent_state.reshape(FLAT, W)

    nest = nest_state.reshape(2, LEV, 2, W).transpose(1, 2, 0, 3)
    kept, down, up, nest, moved, dest, q_mix = call(
        halo_kernel,
        (
            pltpu.VMEM((FLAT, W), F32),
            sds((HALO_ROWS, W), BF16),
            sds((HALO_ROWS, W), BF16),
            pltpu.VMEM((4, LEV, W), F32),
            pltpu.VMEM((STEPS, NT), jnp.int32),
            pltpu.VMEM((STEPS, 2 * W), jnp.int32),
            pltpu.VMEM((6 * W, 2 * W), BF16),
        ),
        in_specs=[SM, HB, HB, HB, HB, HB, HB, HB],
        scratch=[
            pltpu.VMEM((ROWS, W), jnp.int32),
            pltpu.VMEM((HALO_ROWS, W), F32),
            pltpu.VMEM((HALO_ROWS, W), F32),
            pltpu.VMEM((ROWS, W), F32),
            pltpu.VMEM((STEPS, NT), jnp.int32),
            pltpu.SMEM((STEPS,), jnp.int32),
            pltpu.SemaphoreType.DMA((10,)),
        ],
        name="halo",
        nbytes=1 << 20,
    )(
        tile,
        in_hbm(parent),
        in_hbm(terrain),
        in_hbm(nest),
        in_hbm(boundary_index),
        in_hbm(reloc_dest),
        in_hbm(q_mix),
        in_hbm(shift_x),
    )
    message = call(
        send_kernel,
        sds((4 * NT, W), F32),
        scratch=[pltpu.VMEM((2, 2 * W, W), F32)],
        name="send",
        nbytes=64 << 20,
    )(nest, moved, dest, q_mix)
    pairs = [(i, i + 1) for i in range(0, NT, 2)] + [(i + 1, i) for i in range(0, NT, 2)]
    gaps = [(i, i + 1) for i in range(1, NT - 1, 2)]
    gaps = gaps + [(i + 1, i) for i in range(1, NT - 1, 2)]
    from_gap = lax.ppermute(up, "tile", gaps)
    from_pair = lax.ppermute(down, "tile", pairs)
    first = exchange(message.reshape(NT, 4, W)).reshape(4 * NT, W)
    cells, ring = call(
        parent_kernel,
        (
            pltpu.VMEM((STEPS, 2 * W, ROWS * W), BF16),
            pltpu.HBM((2 * BSTR, W), F32),
        ),
        in_specs=[SM, VM, VM, VM, HB],
        out_specs=(VM, HB),
        scratch=[
            pltpu.VMEM((HALO_ROWS, W), F32),
            pltpu.VMEM((HALO_ROWS, W), F32),
            pltpu.VMEM((FLAT, W), F32),
            pltpu.VMEM((ROWS, W), F32),
            pltpu.VMEM((2 * BSTR, W), F32),
            pltpu.VMEM((2 * BSTR, W), F32),
            pltpu.VMEM((2 * BSTR, W), F32),
            pltpu.VMEM((ROWS, W), jnp.int32),
            pltpu.SemaphoreType.DMA((2,)),
        ],
        name="parent",
        flops=1 << 33,
        nbytes=1 << 27,
    )(tile, kept, from_gap, from_pair, in_hbm(terrain))

    values = call(
        gather_kernel,
        sds((PACK * NT, W), BF16),
        scratch=[pltpu.VMEM((PACK * NT, W), F32)],
        name="gather",
        flops=1 << 29,
        nbytes=3 << 20,
    )(first, cells)
    second = exchange(values.reshape(PACK // 4 * NT, 4, W)).reshape(PACK * NT, W)

    bperm = boundary_index.reshape(STEPS, 32, 4).transpose(0, 2, 1).reshape(STEPS, NT)
    hot, base, select = call(
        plan_kernel,
        (
            sds((2, 4 * NT, 4 * NT), BF16),
            sds((4 * NT, W), F32),
            pltpu.VMEM((STEPS, W, 2 * NT), BF16),
        ),
        in_specs=[SM, VM, VM],
        name="plan",
        flops=1 << 28,
        nbytes=3 << 20,
    )(tile, first, bperm)

    second, hot, base, select = lax.optimization_barrier((second, hot, base, select))
    edges = call(
        regroup_kernel,
        sds((EPACK * NT, W), BF16),
        scratch=[pltpu.VMEM((PACK * NT, W), F32), pltpu.VMEM((EPACK * NT, W), F32)],
        name="regroup",
        flops=1 << 26,
        nbytes=1 << 20,
    )(select, second)
    third = exchange(edges.reshape(EPACK // 2 * NT, 2, W)).reshape(EPACK * NT, W)

    parent_out = call(
        last_parent_kernel,
        sds((2 * LEV, ROWS, W), F32),
        in_specs=[HB, HB],
        scratch=[
            pltpu.VMEM((2 * BSTR, W), F32),
            pltpu.VMEM((ROWS, W), jnp.int32),
            pltpu.SemaphoreType.DMA((2,)),
        ],
        name="last_parent",
        flops=1 << 22,
        nbytes=2 << 20,
    )(in_hbm(ring), in_hbm(terrain))
    third, parent_out = lax.optimization_barrier((third, parent_out))
    columns = call(
        owner_kernel,
        sds((4 * NT, W), F32),
        in_specs=[SM, VM, VM, VM, VM],
        scratch=[pltpu.VMEM((EPACK * NT, W), F32)],
        name="owner",
        flops=1 << 29,
        nbytes=3 << 20,
    )(tile, third, hot, base, e_mix)
    fourth = exchange(columns.reshape(NT, 4, W)).reshape(4 * NT, W)

    nest_out = call(
        nest_kernel,
        sds((4 * LEV, W), F32),
        scratch=[pltpu.VMEM((W, W), F32)] * 3,
        name="nest",
        nbytes=1 << 19,
    )(fourth)
    other = lax.ppermute(nest_out, "member", [(0, 1), (1, 0)])
    mean, variance = call(
        stats_kernel,
        (sds((LEV, 2 * W), F32), sds((LEV, 2 * W), F32)),
        name="stats",
        nbytes=1 << 19,
    )(nest_out, other)
    nest_out = nest_out.reshape(LEV, 2, 2, W).transpose(2, 0, 1, 3)
    nest_out = nest_out.reshape(nest_state.shape)
    return (parent_out.reshape(parent_state.shape), nest_out, mean, variance)


def solution(mesh):
    in_specs = (
        P("member", None, "tile", None),
        P("member", None, "tile"),
        P("tile", None),
        P(),
        P(None, "tile"),
        P(None, "tile"),
    )
    out_specs = (
        P("member", None, "tile", None),
        P("member", None, "tile"),
        P(None, "tile"),
        P(None, "tile"),
    )
    return jax.shard_map(
        on_device, mesh=mesh, in_specs=in_specs, out_specs=out_specs, check_vma=False
    )
```
